32 devices in a mesh: dp: 8 (over y, x, core), mp: 4 (over z).
Axes of the slice: x: 2, y: 2, z: 4, core: 2. Of those that a mesh axis runs over, the one named last changes fastest.
Arguments:
- inputs: bfloat16 [768, 16384], P('mp', 'dp'), may hold values from -6 to 6
- token_order: int32 [8, 2048], P('dp'), may hold values from 0 to 2047, each once within a row
- lengths: int32 [8, 4], P('dp'), may hold values from 1 to 1024, 2048 in all within a row
- token_mask: int32 [16384], P('dp'), may hold values 0 or 1
- cotangent: bfloat16 [16384, 128], P('dp'), may hold values from -6 to 6
- query_weight: bfloat16 [768, 768], P('dp', 'mp'), may hold values from -0.21875 to 0.21875
- key_weight: bfloat16 [768, 768], P('dp', 'mp'), may hold values from -0.21875 to 0.21875
- value_weight: bfloat16 [768, 768], P('dp', 'mp'), may hold values from -0.21875 to 0.21875
- output_weight: bfloat16 [768, 768], P('mp', 'dp'), may hold values from -1.5 to 1.5
- inner_weight: bfloat16 [768, 3072], P('dp', 'mp'), may hold values from -0.21875 to 0.21875
- outer_weight: bfloat16 [3072, 768], P('mp', 'dp'), may hold values from -0.109375 to 0.109375
- final_weight: bfloat16 [768, 128], P('mp', 'dp'), may hold values from -0.21875 to 0.21875
- query_bias: float32 [768], P('mp'), may hold values from -2.5 to 2.5
- value_bias: float32 [768], P('mp'), may hold values from -2.5 to 2.5
- output_bias: float32 [768], P('mp'), may hold values from -2.5 to 2.5
- inner_bias: float32 [3072], P('mp'), may hold values from -2.5 to 2.5
- outer_bias: float32 [768], P('mp'), may hold values from -2.5 to 2.5
- first_gain: float32 [768], P('mp'), may hold values from 0.5 to 1.5
- first_shift: float32 [768], P('mp'), may hold values from -2.5 to 2.5
- second_gain: float32 [768], P('mp'), may hold values from 0.5 to 1.5
- second_shift: float32 [768], P('mp'), may hold values from -2.5 to 2.5
Outputs:
- passage_vectors: float32 [16384, 128], P('dp')
- inputs_grad: float32 [768, 16384], P('mp', 'dp')
- query_weight_grad: float32 [768, 768], P('dp', 'mp')
- key_weight_grad: float32 [768, 768], P('dp', 'mp')
- value_weight_grad: float32 [768, 768], P('dp', 'mp')
- output_weight_grad: float32 [768, 768], P('mp', 'dp')
- inner_weight_grad: float32 [768, 3072], P('dp', 'mp')
- outer_weight_grad: float32 [3072, 768], P('mp', 'dp')
- final_weight_grad: float32 [768, 128], P('mp', 'dp')
- query_bias_grad: float32 [768], P('mp')
- value_bias_grad: float32 [768], P('mp')
- output_bias_grad: float32 [768], P('mp')
- inner_bias_grad: float32 [3072], P('mp')
- outer_bias_grad: float32 [768], P('mp')
- first_gain_grad: float32 [768], P('mp')
- first_shift_grad: float32 [768], P('mp')
- second_gain_grad: float32 [768], P('mp')
- second_shift_grad: float32 [768], P('mp')
The draws below stay inside these ranges and needn't reach their ends.
Inputs may be any that keep to these rules, and one draw needn't show every extreme that they name: Each row of token_order lists every number 0 to 2047 once. Each row of lengths sums to 2048, and one passage in each row is 1024 long.
All inputs are finite; a program needn't handle non-finite values. No bound on the sum of `token_mask` on one device may be relied on, other than what follows from the above.
Results may differ from the reference program's by a relative error of at most 0.015.
Values may be sent and summed in bfloat16 or wider, within the bound.
No kernel may reach another device: no remote copies, remote signals or barrier semaphores. Data moves between devices by JAX's collectives and lax.ppermute only.
A program may use at most 128 MiB of HBM per device.

```python
import math
import jax
import jax.numpy as jnp
import numpy as np
from jax import lax

D = 768
HEADS = 12
HD = 64
FF = 3072
OUT = 128
TOK_DEV = 2048
SLOTS = 4
QBLOCK = 512
MAXLEN = 1024
GROUPS = 8
TOKENS = 16384


def plant(entries, rng, smallest, top_value):
    extent = entries.shape
    index_at = [jax.random.randint(jax.random.fold_in(rng, axis), (), 0, extent[axis]) for axis in range(len(extent))]
    entries = entries.at[tuple(index_at)].set(smallest)
    longest = extent.index(max(extent))
    index_at[longest] = (index_at[longest] + 1) % extent[longest]
    return entries.at[tuple(index_at)].set(top_value)


def shard_levels(rng, extent, pieces, least, largest):
    level, own = 1.0, jax.random.fold_in(rng, 6)
    for dim, shards_of in pieces:
        heights = jnp.exp(jax.random.uniform(jax.random.fold_in(own, dim), (shards_of,), jnp.float32, least / len(pieces), largest / len(pieces)))
        level = level * jnp.repeat(heights, extent[dim] // shards_of).reshape([-1 if axis == dim else 1 for axis in range(len(extent))])
    return level


def length_profile(number_of, total, limit, slope):
    portions = [(1 << 20) // math.isqrt(grade ** slope) + 1 for grade in range(2, number_of + 1)]
    surplus, counts = total - limit - (number_of - 1), [1] * (number_of - 1)
    while surplus > 0:
        free = [i for i in range(number_of - 1) if counts[i] < limit]
        mass, left = sum([portions[i] for i in free]), surplus
        for i in free:
            more = min(limit - counts[i], max(1, left * portions[i] // mass), surplus)
            counts[i] = counts[i] + more
            surplus = surplus - more
    return np.array([limit] + counts)


def ragged(rng, number_of, total, most, slope):
    if number_of == 2:
        one = jax.random.randint(rng, (), max(1, total - most), min(most, total - 1) + 1)
        return jnp.stack([one, total - one])
    sizes = jnp.asarray(length_profile(number_of, total, most, slope), jnp.int32)
    pairs = (number_of - 1) // 2
    donor, receiver = sizes[1:1 + 2 * pairs:2], sizes[2:2 + 2 * pairs:2]
    margin = jnp.minimum(donor - 1, most - receiver)
    shifted = jax.random.randint(jax.random.fold_in(rng, 1), (pairs,), 0, 1 << 20) % (margin + 1)
    sizes = sizes.at[1:1 + 2 * pairs:2].set(donor - shifted).at[2:2 + 2 * pairs:2].set(receiver + shifted)
    return sizes[jax.random.permutation(jax.random.fold_in(rng, 2), number_of)]


def gaussian(own_key, shape, spread, most, cuts=(), kind=jnp.bfloat16):
    loudness = shard_levels(own_key, shape, cuts, -0.22, 0.18) if cuts else 1.0
    values = jax.random.normal(own_key, shape, jnp.float32) * spread * loudness
    return jnp.minimum(jnp.maximum(values, -most), most).astype(kind)


def setup_inputs(seed: int = 0) -> dict:
    key_list = jax.random.split(jax.random.key(seed), 22)
    return {
        "inputs": gaussian(key_list[0], (D, TOKENS), 1.0, 6.0, ((0, 4), (1, 8))),
        "token_order": jax.vmap(lambda own: jax.random.permutation(own, TOK_DEV))(jax.random.split(key_list[1], GROUPS)).reshape((GROUPS, TOK_DEV)).astype(jnp.int32),
        "lengths": jax.vmap(lambda own: ragged(own, SLOTS, TOK_DEV, MAXLEN, 2))(jax.random.split(key_list[2], GROUPS)).reshape((GROUPS, SLOTS)).astype(jnp.int32),
        "token_mask": plant((jax.random.randint(key_list[3], (TOKENS,), 0, 8) < 7).astype(jnp.int32), jax.random.fold_in(key_list[3], 1), 0, 1),
        "cotangent": gaussian(key_list[4], (TOKENS, OUT), 1.0, 6.0, ((0, 8),)),
        "query_weight": gaussian(key_list[5], (D, D), D ** -0.5, 0.21875, ((0, 8), (1, 4))),
        "key_weight": gaussian(key_list[6], (D, D), D ** -0.5, 0.21875, ((0, 8), (1, 4))),
        "value_weight": gaussian(key_list[7], (D, D), D ** -0.5, 0.21875, ((0, 8), (1, 4))),
        "output_weight": gaussian(key_list[8], (D, D), (max(D // 48, 4)) ** -0.5, 1.5, ((0, 4), (1, 8))),
        "inner_weight": gaussian(key_list[9], (D, FF), D ** -0.5, 0.21875, ((0, 8), (1, 4))),
        "outer_weight": gaussian(key_list[10], (FF, D), FF ** -0.5, 0.109375, ((0, 4), (1, 8))),
        "final_weight": gaussian(key_list[11], (D, OUT), D ** -0.5, 0.21875, ((0, 4), (1, 8))),
        "query_bias": gaussian(key_list[12], (D,), 0.3, 2.5, ((0, 4),), jnp.float32),
        "value_bias": gaussian(key_list[13], (D,), 0.3, 2.5, ((0, 4),), jnp.float32),
        "output_bias": gaussian(key_list[14], (D,), 0.3, 2.5, ((0, 4),), jnp.float32),
        "inner_bias": gaussian(key_list[15], (FF,), 0.3, 2.5, ((0, 4),), jnp.float32),
        "outer_bias": gaussian(key_list[16], (D,), 0.3, 2.5, ((0, 4),), jnp.float32),
        "first_gain": jnp.clip(1.0 + 0.1 * jax.random.normal(key_list[17], (D,), jnp.float32), 0.5, 1.5),
        "first_shift": gaussian(key_list[18], (D,), 0.3, 2.5, ((0, 4),), jnp.float32),
        "second_gain": jnp.clip(1.0 + 0.1 * jax.random.normal(key_list[19], (D,), jnp.float32), 0.5, 1.5),
        "second_shift": gaussian(key_list[20], (D,), 0.3, 2.5, ((0, 4),), jnp.float32),
    }


norm_epsilon = 1e-06
length_epsilon = 1e-06
highest = lax.Precision.HIGHEST

@jax.custom_vjp
def low(v):
    return lax.optimization_barrier(v.astype(jnp.bfloat16)).astype(jnp.float32)

@jax.custom_vjp
def low_back(v):
    return v

def low_keep(v):
    return (low(v), None)

def low_pass(kept, grad):
    return (grad,)

def back_keep(v):
    return (v, None)

def back_low(kept, grad):
    return (low(grad),)
low.defvjp(low_keep, low_pass)
low_back.defvjp(back_keep, back_low)

def matmul(left_side, right_side):
    return jnp.dot(left_side, right_side, precision=highest, preferred_element_type=jnp.float32)

def layer_norm(residual, norm_gain, norm_shift):
    mean_row = lax.optimization_barrier(jnp.mean(residual, axis=1, keepdims=True))
    spread_row = lax.optimization_barrier(jnp.mean(residual * residual, axis=1, keepdims=True)) - mean_row * mean_row
    return (residual - mean_row) * lax.rsqrt(spread_row + norm_epsilon) * norm_gain + norm_shift

def passage_number(lengths_row, row_count):
    passage_ends = jnp.cumsum(lengths_row)
    position = jnp.arange(row_count, dtype=jnp.int32)
    return lax.optimization_barrier(jnp.sum((position[:, None] >= passage_ends[None, :]).astype(jnp.int32), axis=1))

def allowed_block(segments, kept_mask, first_row, block_rows):
    row_count = segments.shape[0]
    query_segments = lax.dynamic_slice_in_dim(segments, first_row, block_rows, 0)
    query_position = first_row + jnp.arange(block_rows, dtype=jnp.int32)
    key_position = jnp.arange(row_count, dtype=jnp.int32)
    same_passage = query_segments[:, None] == segments[None, :]
    return same_passage & ((kept_mask[None, :] > 0) | (query_position[:, None] == key_position[None, :]))

def attention(queries, key_rows, values, segments, kept_mask):
    row_count = queries.shape[0]
    query_heads = queries.reshape(row_count, HEADS, HD)
    key_heads = key_rows.reshape(row_count, HEADS, HD)
    value_heads = values.reshape(row_count, HEADS, HD)
    score_scale = HD ** (-0.5)

    def one_block(block_index):
        first_row = block_index * QBLOCK
        query_rows = lax.dynamic_slice_in_dim(query_heads, first_row, QBLOCK, 0)
        allowed = allowed_block(segments, kept_mask, first_row, QBLOCK)
        scores = jnp.einsum('qhd,khd->hqk', query_rows, key_heads, precision=highest) * score_scale
        scores = jnp.where(allowed[None], low_back(scores), -1e+30)
        row_max = lax.optimization_barrier(jnp.max(scores, axis=2, keepdims=True))
        exponent = jnp.exp(scores - row_max)
        probabilities = exponent / lax.optimization_barrier(jnp.sum(exponent, axis=2, keepdims=True))
        context = jnp.einsum('hqk,khd->qhd', low(probabilities), value_heads, precision=highest)
        return context.reshape(QBLOCK, HEADS * HD)
    blocks = lax.map(jax.checkpoint(one_block), jnp.arange(row_count // QBLOCK, dtype=jnp.int32))
    return blocks.reshape(row_count, HEADS * HD)

def layer_group(params, inputs, token_order, token_mask, lengths):
    query_weight, key_weight, value_weight, output_weight, inner_weight, outer_weight, final_weight, query_bias, value_bias, output_bias, inner_bias, outer_bias, first_gain, first_shift, second_gain, second_shift = params
    packed = inputs[token_order]
    kept_mask = token_mask[token_order]
    segments = passage_number(lengths, packed.shape[0])
    packed_low = low(packed)
    queries = low(low_back(matmul(packed_low, query_weight)) + query_bias)
    key_rows = low(low_back(matmul(packed_low, key_weight)))
    values = low(low_back(matmul(packed_low, value_weight)) + value_bias)
    context = low(low_back(attention(queries, key_rows, values, segments, kept_mask)))
    attended = low_back(matmul(context, output_weight))
    first_normed = layer_norm(packed + attended + output_bias, first_gain, first_shift)
    hidden_pre = low_back(matmul(low(first_normed), inner_weight)) + inner_bias
    hidden_act = low(jax.nn.gelu(hidden_pre, approximate=False))
    hidden_out = low_back(matmul(hidden_act, outer_weight))
    second_normed = layer_norm(first_normed + hidden_out + outer_bias, second_gain, second_shift)
    projected = low_back(matmul(low(second_normed), final_weight))
    unit_rows = projected * lax.rsqrt(lax.optimization_barrier(jnp.sum(projected * projected, axis=1, keepdims=True)) + length_epsilon)
    vectors = unit_rows * kept_mask[:, None].astype(jnp.float32)
    return jnp.zeros_like(vectors).at[token_order].set(vectors)

def reference(inputs, token_order, lengths, token_mask, cotangent, query_weight, key_weight, value_weight, output_weight, inner_weight, outer_weight, final_weight, query_bias, value_bias, output_bias, inner_bias, outer_bias, first_gain, first_shift, second_gain, second_shift):
    params = tuple((weight_array.astype(jnp.float32) for weight_array in (query_weight, key_weight, value_weight, output_weight, inner_weight, outer_weight, final_weight, query_bias, value_bias, output_bias, inner_bias, outer_bias, first_gain, first_shift, second_gain, second_shift)))
    stacked = inputs.astype(jnp.float32).T.reshape(GROUPS, TOK_DEV, D)
    mask_groups = token_mask.reshape(GROUPS, TOK_DEV)

    def whole_layer(params, stacked):

        def group_step(carried, group_item):
            result = jax.checkpoint(layer_group)(params, group_item[0], group_item[1], group_item[2], group_item[3])
            return (carried, result)
        _, vectors = lax.scan(group_step, jnp.zeros((), jnp.float32), (stacked, token_order, mask_groups, lengths))
        return vectors
    vectors, pull_back = jax.vjp(whole_layer, params, stacked)
    param_grads, input_grads = pull_back(cotangent.astype(jnp.float32).reshape(GROUPS, TOK_DEV, OUT))
    return (vectors.reshape(TOKENS, OUT), input_grads.reshape(TOKENS, D).T, param_grads[0], param_grads[1], param_grads[2], param_grads[3], param_grads[4], param_grads[5], param_grads[6], param_grads[7], param_grads[8], param_grads[9], param_grads[10], param_grads[11], param_grads[12], param_grads[13], param_grads[14], param_grads[15])
```

```python
import functools
import math

import jax
import jax.numpy as jnp
from jax import lax
from jax.experimental import pallas as pl
from jax.experimental.pallas import tpu as pltpu
from jax.sharding import PartitionSpec as P

D = 768
HD = 64
HL = 192
FB = 96
PARTS = 8
OUT = 128
TOK = 2048
ROWS = 512
KEYS = 1024
LONG = 1024
EPS = 1e-06
F32 = jnp.float32
BF = jnp.bfloat16
VMEM_LIMIT = 56 * 1024 * 1024


def dot_nn(a, b):
    return lax.dot_general(a, b, (((1,), (0,)), ((), ())), preferred_element_type=F32)


def dot_nt(a, b):
    return lax.dot_general(a, b, (((1,), (1,)), ((), ())), preferred_element_type=F32)


def dot_tn(a, b):
    return lax.dot_general(a, b, (((0,), (0,)), ((), ())), preferred_element_type=F32)


def swap(array, axis, bit):
    size = lax.axis_size(axis)
    return lax.ppermute(array, axis, [(a, a ^ bit) for a in range(size)])


def full(shape):
    zeros = (0,) * len(shape)
    return pl.BlockSpec(shape, lambda *_: zeros)


SMEM = pl.BlockSpec(memory_space=pltpu.SMEM)


def call(body, grid, in_specs, out_specs, out_shape, scratch=()):
    return pl.pallas_call(
        body,
        grid=grid,
        in_specs=in_specs,
        out_specs=out_specs,
        out_shape=out_shape,
        scratch_shapes=list(scratch),
        compiler_params=pltpu.CompilerParams(
            dimension_semantics=("arbitrary",) * len(grid), vmem_limit_bytes=VMEM_LIMIT
        ),
    )


def shape(dims, dtype=BF):
    return jax.ShapeDtypeStruct(dims, dtype)


def gather_pieces(own):
    low = jnp.stack([own, swap(own, "mp", 2)])
    held = jnp.concatenate([low, swap(low, "mp", 1)], axis=0)
    if lax.axis_size("dp") != 8:
        return [lax.all_gather(held, "dp", axis=1, tiled=True)]
    x_part = swap(held, "dp", 2)
    y_part = swap(held, "dp", 4)
    far = jnp.concatenate([swap(y_part[:2], "dp", 2), swap(x_part[2:], "dp", 4)], axis=0)
    mine = [held, x_part, y_part, far]
    return mine + [swap(part, "dp", 1) for part in mine]


def scatter_plain(both):
    n_dp = lax.axis_size("dp")
    total = lax.psum_scatter(both[:, :, :FB].reshape(4, D, D), "dp", scatter_dimension=1, tiled=True)
    if both.shape[2] == FB:
        return total
    final = both[:, :, FB:, :256].reshape(4, OUT, 256)
    final = lax.psum_scatter(final, "dp", scatter_dimension=1, tiled=True)
    final = jnp.pad(final, ((0, 0), (0, 16 - OUT // n_dp), (0, 0)))
    sums = lax.psum(both[:, 0, FB:, 256:], "dp")
    return jnp.concatenate([total, jnp.concatenate([final, sums], axis=2)], axis=1)


def reduce_pieces(keep, send):
    if lax.axis_size("dp") != 8:
        both = scatter_plain(jnp.concatenate([keep, send], axis=1).astype(F32))
        upper, lower = both[:2], both[2:].astype(BF)
    else:
        total = keep.astype(F32) + swap(send, "dp", 1).astype(F32)
        total = total.reshape((4, 2, 2) + total.shape[2:])
        x_out = swap(total[:2, :, 1].astype(BF), "dp", 2)
        y_out = swap(total[2:, 1].astype(BF), "dp", 4)
        by_x = total[:2, :, 0] + x_out.astype(F32)
        by_y = total[2:, 0] + y_out.astype(F32)
        upper = by_x[:, 0] + swap(by_x[:, 1].astype(BF), "dp", 4).astype(F32)
        lower = (by_y[:, 0] + swap(by_y[:, 1].astype(BF), "dp", 2).astype(F32)).astype(BF)
    upper = upper + swap(lower, "mp", 1).astype(F32)
    return upper[0] + swap(upper[1].astype(BF), "mp", 2).astype(F32)


def pick(scal, frow, n):
    first = (scal[1] ^ ((n & 1) * 2 + (n >> 1))) * HL
    rows = lax.broadcasted_iota(jnp.int32, (HL, D), 0) + first
    return jnp.where(rows == frow, 1.0, 0.0).astype(BF)


def spread(order_row):
    rows = lax.broadcasted_iota(jnp.int32, (TOK, order_row.shape[1]), 0)
    return jnp.where(rows == order_row, 1.0, 0.0).astype(BF)


def pack_in_body(order_ref, x_ref, mask_ref, cot_ref, out_ref, kept_ref, cot_out_ref):
    block = pl.program_id(0)
    one_hot = spread(order_ref[...])
    out_ref[...] = dot_nn(x_ref[...], one_hot).astype(BF)
    mask = mask_ref[...].astype(F32)

    @pl.when(block < 2)
    def _():
        kept_ref[...] = dot_nn(jnp.broadcast_to(mask, (16, TOK)).astype(BF), one_hot)[:8]

    @pl.when(block == 0)
    def _():
        cot = (jnp.transpose(cot_ref[...].astype(F32)) * mask).astype(BF)
        cot_out_ref[...] = jnp.transpose(dot_nn(cot, one_hot))


def pack_in(order_row, inputs, mask_row, cotangent):
    return call(
        pack_in_body,
        (4,),
        [
            pl.BlockSpec((1, ROWS), lambda b: (0, b)),
            full((HL, TOK)),
            full((1, TOK)),
            full((TOK, OUT)),
        ],
        [
            pl.BlockSpec((HL, ROWS), lambda b: (0, b)),
            pl.BlockSpec((8, ROWS), lambda b: (0, jnp.minimum(b, 1))),
            full((ROWS, OUT)),
        ],
        [shape((HL, TOK)), shape((8, KEYS), F32), shape((ROWS, OUT), F32)],
    )(order_row, inputs, mask_row, cotangent)


def join(refs, rows, first=0, last=D):
    parts = [ref[0, :rows, first:last] for ref in refs]
    return parts[0] if len(parts) == 1 else jnp.concatenate(parts, axis=0)


def lanes_of_head(h, shift):
    lane = lax.broadcasted_iota(jnp.int32, (1, 256), 1)
    return (lane >= shift + h * HD) & (lane < shift + (h + 1) * HD)


def allowed_bias(scal, kept):
    pair = scal[1] & 1
    q_pos = lax.broadcasted_iota(jnp.int32, (ROWS, 1), 0) + pair * ROWS
    k_pos = lax.broadcasted_iota(jnp.int32, (1, KEYS), 1) + pair * ROWS
    k_pos = k_pos & (KEYS - 1)
    q_seg = (q_pos >= scal[2]).astype(jnp.int32) + (q_pos >= scal[3]).astype(jnp.int32)
    k_seg = (k_pos >= scal[2]).astype(jnp.int32) + (k_pos >= scal[3]).astype(jnp.int32)
    k_seg = jnp.where(kept > 0.5, k_seg, k_seg + 8)
    return jnp.where((q_seg == k_seg) | (q_pos == k_pos), 0.0, -1e30)


def attend_body(pieces, scal, frow_ref, kept_ref, x0, x2, x1, x3, extra_ref, *refs):
    weights = refs[:pieces]
    xr_ref, fvec_ref, kv_ref, q_ref, ctx_ref, ctx_f_ref, lse_ref, wo_ref, bias_ref = refs[pieces:]
    step = pl.program_id(0)
    rows = D // pieces

    @pl.when(step == 0)
    def _():
        frow = frow_ref[...]
        upper = jnp.zeros((ROWS, D), F32)
        lower = jnp.zeros((ROWS, D), F32)
        fvec = jnp.zeros((16, D), F32)
        for n, (ref, crossed) in enumerate(((x0, False), (x2, False), (x1, True), (x3, True))):
            chosen = pick(scal, frow, n)
            near, away = ref[:, :ROWS], ref[:, ROWS:]
            if crossed:
                near, away = away, near
            upper = upper + dot_tn(near, chosen)
            lower = lower + dot_tn(away, chosen)
            fvec = fvec + dot_nn(extra_ref[n, :, 512 : 512 + HL], chosen)
        xr_ref[:ROWS] = upper.astype(BF)
        xr_ref[ROWS:] = lower.astype(BF)
        fvec_ref[...] = fvec[:8] + fvec[8:]
        bias_ref[...] = allowed_bias(scal, kept_ref[:1])

    weight = join(weights, rows)
    wo_ref[0] = weight[:, 512:]
    window = extra_ref[pl.ds(step, 1), :, 256:512][0].astype(F32)
    q_bias = window[0:1] + window[1:2]
    v_bias = window[2:3] + window[3:4]
    lane = lax.broadcasted_iota(jnp.int32, (1, 256), 1)
    packed = xr_ref[...]
    kv = dot_nn(packed, weight[:, :384])
    kv_bias = jnp.concatenate([jnp.zeros((1, 128), F32), v_bias], axis=1)
    kv = (kv + kv_bias).astype(BF)
    queries = (dot_nn(packed[:ROWS], weight[:, 384:640]) + q_bias).astype(BF)
    queries = jnp.where(lane < HL, queries, jnp.zeros_like(queries)) * jnp.asarray(0.125, BF)
    kv_ref[0] = kv
    q_ref[0] = queries
    keys, values = kv[:, :256], kv[:, 128:]
    context = jnp.zeros((ROWS, 256), F32)
    for h in range(3):
        own = jnp.where(lanes_of_head(h, 0), queries, jnp.zeros_like(queries))
        scores = dot_nt(own, keys) + bias_ref[...]
        top = jnp.max(scores, axis=1, keepdims=True)
        weight_h = jnp.exp(scores - top)
        total = jnp.sum(weight_h, axis=1, keepdims=True)
        part = dot_nn(weight_h.astype(BF), values) / total
        context = jnp.where(lanes_of_head(h, HD), part, context)
        lse_ref[0, h] = jnp.broadcast_to(top + jnp.log(total), (ROWS, 128))
    ctx_ref[0] = context.astype(BF)
    ctx_f_ref[0] = context


def attend(scal, frow, kept, xs, extra, weights):
    pieces = len(weights)
    return call(
        functools.partial(attend_body, pieces),
        (4,),
        [SMEM, full((1, D)), full((8, KEYS))]
        + [full((HL, KEYS))] * 4
        + [full((4, 16, D))]
        + [pl.BlockSpec((1,) + w.shape[1:], lambda j: (j, 0, 0)) for w in weights],
        [
            full((KEYS, D)),
            full((8, D)),
            pl.BlockSpec((1, KEYS, 384), lambda j: (j, 0, 0)),
            pl.BlockSpec((1, ROWS, 256), lambda j: (j, 0, 0)),
            pl.BlockSpec((1, ROWS, 256), lambda j: (j, 0, 0)),
            pl.BlockSpec((1, ROWS, 256), lambda j: (j, 0, 0)),
            pl.BlockSpec((1, 3, ROWS, 128), lambda j: (j, 0, 0, 0)),
            pl.BlockSpec((1, D, 256), lambda j: (j, 0, 0)),
        ],
        [
            shape((KEYS, D)),
            shape((8, D), F32),
            shape((4, KEYS, 384)),
            shape((4, ROWS, 256)),
            shape((4, ROWS, 256)),
            shape((4, ROWS, 256), F32),
            shape((4, 3, ROWS, 128), F32),
            shape((4, D, 256)),
        ],
        [pltpu.VMEM((ROWS, KEYS), F32)],
    )(scal, frow, kept, *xs, extra, *weights)


def norm(residual, gain, shift):
    mean = jnp.mean(residual, axis=1, keepdims=True)
    spread_row = jnp.mean(residual * residual, axis=1, keepdims=True) - mean * mean
    scale = lax.rsqrt(spread_row + EPS)
    unit = (residual - mean) * scale
    return unit * gain + shift, unit, scale


def norm_back(grad, gain, unit, scale):
    scaled = grad * gain
    mean = jnp.mean(scaled, axis=1, keepdims=True)
    cross = jnp.mean(scaled * unit, axis=1, keepdims=True)
    return scale * (scaled - mean - unit * cross)


def inner_body(pieces, ctx_ref, wo_ref, xr_ref, fvec_ref, extra_ref, *refs):
    weights = refs[:pieces]
    normed_ref, unit_ref, scale_ref, low_ref, act_ref, slope_ref = refs[pieces:]
    step = pl.program_id(0)

    @pl.when(step == 0)
    def _():
        lane = lax.broadcasted_iota(jnp.int32, (1, 256), 1)
        total = xr_ref[...].astype(F32) + fvec_ref[0:1]
        for n in range(4):
            total = total + dot_nt(ctx_ref[n], wo_ref[n])
        normed, unit, scale = norm(total, fvec_ref[2:3], fvec_ref[3:4])
        normed_ref[...] = normed
        unit_ref[...] = unit
        scale_ref[...] = jnp.broadcast_to(scale, (ROWS, 128))
        low_ref[...] = normed.astype(BF)

    window = extra_ref[pl.ds(step, 1), :, 256:512][0].astype(F32)
    bias = jnp.concatenate([window[4 + n : 5 + n] + window[7 + n : 8 + n] for n in range(3)], axis=1)
    pre = dot_nn(low_ref[...], join(weights, D // pieces)) + bias
    half = 0.5 + 0.5 * lax.erf(pre * math.sqrt(0.5))
    act_ref[0] = (pre * half).astype(BF)
    slope_ref[0] = half + pre * (jnp.exp(pre * pre * -0.5) * (1.0 / math.sqrt(2.0 * math.pi)))


def inner(context, wo, packed, fvec, extra, weights):
    pieces = len(weights)
    return call(
        functools.partial(inner_body, pieces),
        (4,),
        [full((4, ROWS, 256)), full((4, D, 256)), full((ROWS, D)), full((8, D)), full((4, 16, D))]
        + [pl.BlockSpec((1,) + w.shape[1:], lambda j: (j, 0, 0)) for w in weights],
        [
            full((ROWS, D)),
            full((ROWS, D)),
            full((ROWS, 128)),
            full((ROWS, D)),
            pl.BlockSpec((1, ROWS, D), lambda j: (j, 0, 0)),
            pl.BlockSpec((1, ROWS, D), lambda j: (j, 0, 0)),
        ],
        [
            shape((ROWS, D), F32),
            shape((ROWS, D), F32),
            shape((ROWS, 128), F32),
            shape((ROWS, D)),
            shape((4, ROWS, D)),
            shape((4, ROWS, D), F32),
        ],
    )(context, wo, packed, fvec, extra, *weights)


def outer_body(pieces, scal, frow_ref, orow_ref, act_ref, normed_ref, fvec_ref, fin_ref, cot_ref, *refs):
    weights = refs[:pieces]
    grad_ref, low_ref, vec_ref, fin_grad_ref, sums_ref, total_ref = refs[pieces:]
    step = pl.program_id(0)
    part = dot_nt(act_ref[0], join(weights, D // pieces))

    @pl.when(step == 0)
    def _():
        total_ref[...] = normed_ref[...] + fvec_ref[1:2] + part

    @pl.when(step > 0)
    def _():
        total_ref[...] += part

    @pl.when(step == 3)
    def _():
        gain = fvec_ref[4:5]
        normed, unit, scale = norm(total_ref[...], gain, fvec_ref[5:6])
        low = normed.astype(BF)
        frow = frow_ref[...]
        final = jnp.zeros((OUT, D), F32)
        for n in range(4):
            final = final + dot_nn(fin_ref[n], pick(scal, frow, n))
        columns = lax.broadcasted_iota(jnp.int32, (OUT, OUT), 0)
        place = jnp.where(columns == orow_ref[...], 1.0, 0.0).astype(BF)
        final = dot_nn(place, final.astype(BF)).astype(BF)
        projected = dot_nt(low, final)
        length = lax.rsqrt(jnp.sum(projected * projected, axis=1, keepdims=True) + EPS)
        units = projected * length
        vec_ref[...] = jnp.transpose(units).astype(BF)
        grads = cot_ref[...]
        grads = length * (grads - units * jnp.sum(grads * units, axis=1, keepdims=True))
        grads = grads.astype(BF)
        fin_grad = dot_tn(place, dot_tn(grads, low).astype(BF)).astype(BF)
        for n in range(4):
            fin_grad_ref[n] = dot_nt(fin_grad, pick(scal, frow, n)).astype(BF)
        grad = dot_nn(grads, final)
        back = norm_back(grad, gain, unit, scale)
        grad_ref[...] = back
        low_ref[...] = back.astype(BF)
        sums_ref[0:1] = jnp.sum(grad * unit, axis=0, keepdims=True)
        sums_ref[1:2] = jnp.sum(grad, axis=0, keepdims=True)
        sums_ref[2:3] = jnp.sum(back, axis=0, keepdims=True)
        sums_ref[3:] = jnp.zeros((5, D), F32)


def outer(scal, frow, orow, act, normed, fvec, final, cot, weights):
    pieces = len(weights)
    return call(
        functools.partial(outer_body, pieces),
        (4,),
        [SMEM, full((1, D)), full((1, OUT))]
        + [pl.BlockSpec((1, ROWS, D), lambda j: (j, 0, 0)), full((ROWS, D)), full((8, D))]
        + [full((4, OUT, HL)), full((ROWS, OUT))]
        + [pl.BlockSpec((1,) + w.shape[1:], lambda j: (j, 0, 0)) for w in weights],
        [
            full((ROWS, D)),
            full((ROWS, D)),
            full((OUT, ROWS)),
            full((4, OUT, HL)),
            full((8, D)),
        ],
        [
            shape((ROWS, D), F32),
            shape((ROWS, D)),
            shape((OUT, ROWS)),
            shape((4, OUT, HL)),
            shape((8, D), F32),
        ],
        [pltpu.VMEM((ROWS, D), F32)],
    )(scal, frow, orow, act, normed, fvec, final, cot, *weights)


def split_out(total, keep_ref, send_ref, extra=None):
    low = total.astype(BF).reshape(PARTS, FB, D)
    half = PARTS // 2
    keep_ref[0, :, :FB] = low[:half]
    send_ref[0, :, :FB] = low[half:]
    if extra is not None:
        keep_ref[0, :, FB:] = extra[:half]
        send_ref[0, :, FB:] = extra[half:]


def outer_back_body(pieces, low_ref, act_ref, slope_ref, *refs):
    weights = refs[:pieces]
    keep_ref, send_ref, pre_ref, bias_ref = refs[pieces:]
    low = low_ref[...]
    split_out(dot_tn(low, act_ref[0]), keep_ref, send_ref)
    grad = dot_nn(low, join(weights, D // pieces)) * slope_ref[0]
    pre_ref[0] = grad.astype(BF)
    bias_ref[0] = jnp.broadcast_to(jnp.sum(grad, axis=0, keepdims=True), (8, D))


def outer_back(low, act, slope, weights):
    pieces = len(weights)
    half = PARTS // 2
    wide = pl.BlockSpec((1, half, FB, D), lambda j: (j, 0, 0, 0))
    block = pl.BlockSpec((1, ROWS, D), lambda j: (j, 0, 0))
    return call(
        functools.partial(outer_back_body, pieces),
        (4,),
        [full((ROWS, D)), block, block]
        + [pl.BlockSpec((1,) + w.shape[1:], lambda j: (j, 0, 0)) for w in weights],
        [wide, wide, block, pl.BlockSpec((1, 8, D), lambda j: (j, 0, 0))],
        [
            shape((4, half, FB, D)),
            shape((4, half, FB, D)),
            shape((4, ROWS, D)),
            shape((4, 8, D), F32),
        ],
    )(low, act, slope, *weights)


def inner_back_body(pieces, scal, frow_ref, pre_ref, next_ref, low_ref, grad_ref, unit_ref, scale_ref, fvec_ref, fin_ref, hid_ref, sums_ref, *refs):
    weights = refs[:pieces]
    one_ref, one_low_ref, keep_ref, send_ref, total_ref, all_ref = refs[pieces:]
    step = pl.program_id(0)

    @pl.when(step == 0)
    def _():
        total_ref[...] = grad_ref[...]

    @pl.when(step < 4)
    def _():
        total_ref[...] += dot_nt(pre_ref[0], join(weights, D // pieces))

    @pl.when(step == 3)
    def _():
        grad = total_ref[...]
        unit = unit_ref[...]
        back = norm_back(grad, fvec_ref[2:3], unit, scale_ref[:, :1])
        one_ref[...] = back
        one_low_ref[...] = back.astype(BF)
        all_ref[0:3] = sums_ref[0:3]
        all_ref[3:4] = jnp.sum(grad * unit, axis=0, keepdims=True)
        all_ref[4:5] = jnp.sum(grad, axis=0, keepdims=True)
        all_ref[5:6] = jnp.sum(back, axis=0, keepdims=True)
        all_ref[6:] = jnp.zeros((10, D), F32)

    @pl.when(step >= 4)
    def _():
        n = step - 4
        sums_low = dot_nt(all_ref[...].astype(BF), pick(scal, frow_ref[...], n))
        tile = jnp.concatenate([sums_low, jnp.zeros((16, 64), F32)], axis=1)
        hidden = hid_ref[pl.ds(n, 1), 0:1][0]
        hidden = jnp.concatenate(
            [hidden[:, 256 * k : 256 * (k + 1)] for k in range(3)] + [jnp.zeros((13, 256), F32)], axis=0
        )
        wide = jnp.concatenate([tile, hidden], axis=1).astype(BF)
        wide = jnp.broadcast_to(wide[None], (PARTS, 16, 512))
        fin = fin_ref[pl.ds(n, 1)][0].reshape(PARTS, OUT // PARTS, HL)
        fin = jnp.concatenate([fin, jnp.zeros((PARTS, OUT // PARTS, 64), BF)], axis=2)
        extra = jnp.concatenate([fin, wide], axis=2)
        split_out(dot_tn(low_ref[...], next_ref[0]), keep_ref, send_ref, extra)


def inner_back(scal, frow, pre, low, grad, unit, scale, fvec, fin, hid, sums, weights):
    pieces = len(weights)
    half = PARTS // 2
    early = lambda j: (jnp.minimum(j, 3), 0, 0)
    late = lambda j: (jnp.maximum(j - 4, 0), 0, 0)
    wide = pl.BlockSpec((1, half, FB + 16, D), lambda j: (jnp.maximum(j - 4, 0), 0, 0, 0))
    return call(
        functools.partial(inner_back_body, pieces),
        (8,),
        [
            SMEM,
            full((1, D)),
            pl.BlockSpec((1, ROWS, D), early),
            pl.BlockSpec((1, ROWS, D), late),
            full((ROWS, D)),
            full((ROWS, D)),
            full((ROWS, D)),
            full((ROWS, 128)),
            full((8, D)),
            full((4, OUT, HL)),
            full((4, 8, D)),
            full((8, D)),
        ]
        + [pl.BlockSpec((1,) + w.shape[1:], early) for w in weights],
        [full((ROWS, D)), full((ROWS, D)), wide, wide],
        [
            shape((ROWS, D), F32),
            shape((ROWS, D)),
            shape((4, half, FB + 16, D)),
            shape((4, half, FB + 16, D)),
        ],
        [pltpu.VMEM((ROWS, D), F32), pltpu.VMEM((16, D), F32)],
    )(scal, frow, pre, pre, low, grad, unit, scale, fvec, fin, hid, sums, *weights)


def attend_back_body(pieces, scal, frow_ref, kept_ref, xr_ref, kv_ref, q_ref, ctx_ref, ctx_f_ref, lse_ref, one_ref, low_ref, *refs):
    weights = refs[:pieces]
    keep_ref, send_ref, x0_ref, x2_ref, xb_ref, bias_ref, total_ref = refs[pieces:]
    step = pl.program_id(0)

    @pl.when(step == 0)
    def _():
        bias_ref[...] = allowed_bias(scal, kept_ref[:1])
        total_ref[:ROWS] = one_ref[...]
        total_ref[ROWS:] = jnp.zeros((ROWS, D), F32)

    weight = join(weights, D // pieces)
    low = low_ref[...]
    lane = lax.broadcasted_iota(jnp.int32, (1, 256), 1)
    grad_ctx = dot_nn(low, weight[:, 512:])
    grad_ctx = jnp.where(lane >= HD, grad_ctx, 0.0).astype(BF)
    keys, values = kv_ref[0, :, :256], kv_ref[0, :, 128:]
    queries = q_ref[0]
    products = grad_ctx.astype(F32) * ctx_f_ref[0]
    dq = jnp.zeros((ROWS, 256), F32)
    dk = jnp.zeros((KEYS, 256), F32)
    dv = jnp.zeros((KEYS, 256), F32)
    zero = jnp.zeros_like(queries)
    for h in range(3):
        own = jnp.where(lanes_of_head(h, 0), queries, zero)
        own_grad = jnp.where(lanes_of_head(h, HD), grad_ctx, zero)
        row_dot = jnp.sum(jnp.where(lanes_of_head(h, HD), products, 0.0), axis=1, keepdims=True)
        scores = dot_nt(own, keys) + bias_ref[...]
        prob = jnp.exp(scores - lse_ref[0, h][:, :1])
        dv = dv + dot_tn(prob.astype(BF), own_grad)
        grad_scores = (prob * (dot_nt(own_grad, values) - row_dot)).astype(BF)
        dq = jnp.where(lanes_of_head(h, 0), dot_nn(grad_scores, keys), dq)
        dk = dk + dot_tn(grad_scores, own)
    dq = dq * 0.125
    gap = jnp.zeros((KEYS, 128), F32)
    dkv = jnp.concatenate([dk, gap], axis=1) + jnp.concatenate([gap, dv], axis=1)
    q_sum = jnp.sum(dq, axis=0, keepdims=True)
    v_sum = jnp.sum(dv, axis=0, keepdims=True)
    dkv = dkv.astype(BF)
    dq = dq.astype(BF)
    packed = xr_ref[...]
    low_kv = dot_tn(packed, dkv)
    from_q = dot_tn(packed[:ROWS], dq)
    from_o = dot_tn(low, ctx_ref[0])
    gap = jnp.zeros((D, 128), F32)
    from_qo = jnp.concatenate([from_q, gap], axis=1) + jnp.concatenate([gap, from_o], axis=1)
    sums = jnp.concatenate([q_sum, v_sum, jnp.zeros((14, 256), F32)], axis=0)
    extra = jnp.concatenate([jnp.zeros((16, 256), F32), sums, jnp.zeros((16, 256), F32)], axis=1)
    extra = jnp.broadcast_to(extra.astype(BF)[None], (PARTS, 16, D))
    split_out(jnp.concatenate([low_kv, from_qo], axis=1), keep_ref, send_ref, extra)
    total_ref[...] += dot_nt(dkv, weight[:, :384])
    total_ref[:ROWS] += dot_nt(dq, weight[:, 384:640])

    @pl.when(step == 3)
    def _():
        grads = total_ref[...].astype(BF)
        frow = frow_ref[...]
        x0_ref[...] = dot_nt(pick(scal, frow, 0), grads)
        x2_ref[...] = dot_nt(pick(scal, frow, 1), grads)
        for n in range(2):
            part = dot_nt(pick(scal, frow, 2 + n), grads).astype(BF)
            xb_ref[n, :, :ROWS] = part[:, ROWS:]
            xb_ref[n, :, ROWS:] = part[:, :ROWS]


def attend_back(scal, frow, kept, packed, kv, queries, context, context_f, lse, one, low, weights):
    pieces = len(weights)
    half = PARTS // 2
    wide = pl.BlockSpec((1, half, FB + 16, D), lambda j: (j, 0, 0, 0))
    return call(
        functools.partial(attend_back_body, pieces),
        (4,),
        [
            SMEM,
            full((1, D)),
            full((8, KEYS)),
            full((KEYS, D)),
            pl.BlockSpec((1, KEYS, 384), lambda j: (j, 0, 0)),
            pl.BlockSpec((1, ROWS, 256), lambda j: (j, 0, 0)),
            pl.BlockSpec((1, ROWS, 256), lambda j: (j, 0, 0)),
            pl.BlockSpec((1, ROWS, 256), lambda j: (j, 0, 0)),
            pl.BlockSpec((1, 3, ROWS, 128), lambda j: (j, 0, 0, 0)),
            full((ROWS, D)),
            full((ROWS, D)),
        ]
        + [pl.BlockSpec((1,) + w.shape[1:], lambda j: (j, 0, 0)) for w in weights],
        [wide, wide, full((HL, KEYS)), full((HL, KEYS)), full((2, HL, KEYS))],
        [
            shape((4, half, FB + 16, D)),
            shape((4, half, FB + 16, D)),
            shape((HL, KEYS), F32),
            shape((HL, KEYS), F32),
            shape((2, HL, KEYS)),
        ],
        [pltpu.VMEM((ROWS, KEYS), F32), pltpu.VMEM((KEYS, D), F32)],
    )(scal, frow, kept, packed, kv, queries, context, context_f, lse, one, low, *weights)


def pack_out_body(order_ref, mask_ref, x_ref, vec_ref, x_out_ref, vec_out_ref, total_ref):
    step = pl.program_id(0)
    both = jnp.concatenate([x_ref[...], vec_ref[0]], axis=0)
    part = dot_nt(both, spread(order_ref[...]))

    @pl.when(step == 0)
    def _():
        total_ref[...] = part

    @pl.when(step > 0)
    def _():
        total_ref[...] += part

    @pl.when(step == 3)
    def _():
        x_out_ref[...] = total_ref[:HL]
        vec_out_ref[...] = jnp.transpose(total_ref[HL:] * mask_ref[...].astype(F32))


def pack_out(order_row, mask_row, grads, vecs):
    return call(
        pack_out_body,
        (4,),
        [
            pl.BlockSpec((1, ROWS), lambda b: (0, b)),
            full((1, TOK)),
            pl.BlockSpec((HL, ROWS), lambda b: (0, b)),
            pl.BlockSpec((1, OUT, ROWS), lambda b: (b, 0, 0)),
        ],
        [full((HL, TOK)), full((TOK, OUT))],
        [shape((HL, TOK), F32), shape((TOK, OUT), F32)],
        [pltpu.VMEM((HL + OUT, TOK), F32)],
    )(order_row, mask_row, grads, vecs)


def hi_lo(vector):
    high = vector.astype(BF)
    high = lax.optimization_barrier(high)
    return high, (vector - high.astype(F32)).astype(BF)


def extra_rows(final_t, q_bias, v_bias, inner_bias, features):
    q_hi, q_lo = hi_lo(jnp.pad(q_bias, (0, 64)))
    v_hi, v_lo = hi_lo(jnp.pad(v_bias, (64, 0)))
    in_hi, in_lo = hi_lo(inner_bias.reshape(3, 256))
    window = jnp.concatenate([jnp.stack([q_hi, q_lo, v_hi, v_lo]), in_hi, in_lo], axis=0)
    window = jnp.pad(window, ((0, 6), (0, 0)))
    f_hi, f_lo = hi_lo(jnp.pad(jnp.stack(features), ((0, 2), (0, 64))))
    final_t = jnp.pad(final_t, ((0, 16 - final_t.shape[0]), (0, 64)))
    return jnp.concatenate([final_t, window, jnp.concatenate([f_hi, f_lo], axis=0)], axis=1)


def relative(blocks, m):
    blocks = jnp.where((m & 2) > 0, jnp.concatenate([blocks[2:], blocks[:2]]), blocks)
    crossed = jnp.stack([blocks[1], blocks[0], blocks[3], blocks[2]])
    return jnp.where((m & 1) > 0, crossed, blocks)


def local(
    inputs,
    token_order,
    lengths,
    token_mask,
    cotangent,
    query_weight,
    key_weight,
    value_weight,
    output_weight,
    inner_weight,
    outer_weight,
    final_weight,
    query_bias,
    value_bias,
    output_bias,
    inner_bias,
    outer_bias,
    first_gain,
    first_shift,
    second_gain,
    second_shift,
):
    m, i = lax.axis_index("mp"), lax.axis_index("dp")
    n_dp = lax.axis_size("dp")
    rows = D // n_dp
    by_xor = n_dp == 8

    order, sizes = token_order[0], lengths[0]
    ends = jnp.cumsum(sizes)
    is_long = sizes == LONG
    start = jnp.sum(jnp.where(is_long, ends - sizes, 0))
    position = jnp.arange(LONG, dtype=jnp.int32)
    rest = jnp.where(position < start, order[:LONG], order[LONG:])
    blocks = jnp.concatenate([lax.dynamic_slice(order, (start,), (LONG,)), rest]).reshape(4, ROWS)
    order_row = relative(blocks, m).reshape(1, TOK)
    rest_ends = jnp.cumsum(jnp.where(is_long, 0, sizes))
    rank = jnp.cumsum(jnp.where(is_long, 0, 1))
    cut = [jnp.max(jnp.where((rank == n) & ~is_long, rest_ends, 0)) for n in (1, 2)]
    upper = m >= 2
    cuts = [jnp.where(upper, c, LONG) for c in cut]
    scal = jnp.stack([i, m, cuts[0], cuts[1]]).astype(jnp.int32)
    place = jnp.arange(D, dtype=jnp.int32)
    spot = jnp.arange(OUT, dtype=jnp.int32)
    if by_xor:
        block_of = lambda p: ((p & 3) * 2 + (p >> 2)) ^ i
        frow = block_of(place // rows) * rows + place % rows
        orow = block_of(spot // (OUT // 8)) * (OUT // 8) + spot % (OUT // 8)
    else:
        frow, orow = place, spot
    frow, orow = frow.reshape(1, D).astype(jnp.int32), orow.reshape(1, OUT).astype(jnp.int32)

    mask_row = token_mask.reshape(1, TOK)
    features, kept, cot = pack_in(order_row, inputs, mask_row, cotangent)
    near, away = features[:, :KEYS], features[:, KEYS:]
    x2 = swap(away, "mp", 2)
    x1 = swap(near, "mp", 1)
    x3 = swap(x2, "mp", 1)

    extra = extra_rows(
        final_weight.T,
        query_bias,
        value_bias,
        inner_bias,
        [output_bias, outer_bias, first_gain, first_shift, second_gain, second_shift],
    )
    heads = jnp.concatenate([key_weight, value_weight, query_weight, output_weight.T], axis=1)
    outer_own = jnp.concatenate([outer_weight.T, extra], axis=0)
    extra_low = jnp.stack([extra, swap(extra, "mp", 2)])
    extras = jnp.concatenate([extra_low, swap(extra_low, "mp", 1)], axis=0)
    head_pieces = gather_pieces(heads)
    inner_pieces = gather_pieces(inner_weight)
    outer_pieces = gather_pieces(outer_own)
    if by_xor:
        final = jnp.concatenate([p[:, rows : rows + OUT // n_dp, :HL] for p in outer_pieces], axis=1)
    else:
        stacked = outer_pieces[0].reshape(4, n_dp, rows + 16, D)
        final = stacked[:, :, rows : rows + OUT // n_dp, :HL].reshape(4, OUT, HL)
        outer_pieces = [stacked[:, :, :rows].reshape(4, D, D)]

    packed, fvec, kv, queries, context, context_f, lse, wo = attend(
        scal, frow, kept, (near, x2, x1, x3), extras, head_pieces
    )
    normed, unit, scale, normed_low, act, slope = inner(context, wo, packed, fvec, extras, inner_pieces)
    grad_two, two_low, vec, fin_grad, sums = outer(
        scal, frow, orow, act, normed, fvec, final, cot, outer_pieces
    )
    outer_keep, outer_send, pre, hid_sums = outer_back(two_low, act, slope, outer_pieces)
    grad_one, one_low, inner_keep, inner_send = inner_back(
        scal, frow, pre, normed_low, grad_two, unit, scale, fvec, fin_grad, hid_sums, sums, inner_pieces
    )
    head_keep, head_send, dx0, dx2, dxb = attend_back(
        scal, frow, kept, packed, kv, queries, context, context_f, lse, grad_one, one_low, head_pieces
    )
    vec_low = jnp.stack([vec, swap(vec, "mp", 1)])
    vecs = jnp.concatenate([vec_low, swap(vec_low, "mp", 2)], axis=0)

    outer_sum = reduce_pieces(outer_keep, outer_send)
    inner_sum = reduce_pieces(inner_keep, inner_send)
    head_sum = reduce_pieces(head_keep, head_send)

    dxr = swap(dxb, "mp", 1).astype(F32)
    far = swap((dx2 + dxr[1]).astype(BF), "mp", 2)
    grads = jnp.concatenate([(dx0 + dxr[0]).astype(BF), far], axis=1)
    inputs_grad, vectors = pack_out(order_row, mask_row, grads, vecs)

    tile = inner_sum[rows:]
    head_tile = head_sum[rows:]
    return (
        vectors,
        inputs_grad,
        head_sum[:rows, 384:576],
        head_sum[:rows, :HL],
        head_sum[:rows, HL:384],
        head_sum[:rows, 576:].T,
        inner_sum[:rows],
        outer_sum.T,
        tile[: OUT // n_dp, :HL].T,
        head_tile[0, 256 : 256 + HL],
        head_tile[1, 320:512],
        tile[5, 256 : 256 + HL],
        tile[:3, 512:].reshape(D),
        tile[2, 256 : 256 + HL],
        tile[3, 256 : 256 + HL],
        tile[4, 256 : 256 + HL],
        tile[0, 256 : 256 + HL],
        tile[1, 256 : 256 + HL],
    )


def solution(mesh):
    return jax.shard_map(
        local,
        mesh=mesh,
        in_specs=(
            P("mp", "dp"),
            P("dp", None),
            P("dp", None),
            P("dp"),
            P("dp", None),
            P("dp", "mp"),
            P("dp", "mp"),
            P("dp", "mp"),
            P("mp", "dp"),
            P("dp", "mp"),
            P("mp", "dp"),
            P("mp", "dp"),
            P("mp"),
            P("mp"),
            P("mp"),
            P("mp"),
            P("mp"),
            P("mp"),
            P("mp"),
            P("mp"),
            P("mp"),
        ),
        out_specs=(
            P("dp", None),
            P("mp", "dp"),
            P("dp", "mp"),
            P("dp", "mp"),
            P("dp", "mp"),
            P("mp", "dp"),
            P("dp", "mp"),
            P("mp", "dp"),
            P("mp", "dp"),
            P("mp"),
            P("mp"),
            P("mp"),
            P("mp"),
            P("mp"),
            P("mp"),
            P("mp"),
            P("mp"),
            P("mp"),
        ),
        check_vma=False,
    )
```

```python
import functools
import math

import jax
import jax.numpy as jnp
from jax import lax
from jax.experimental import pallas as pl
from jax.experimental.pallas import tpu as pltpu
from jax.sharding import PartitionSpec as P

D = 768
HD = 64
HL = 192
FB = 96
PARTS = 8
OUT = 128
TOK = 2048
ROWS = 512
KEYS = 1024
LONG = 1024
EPS = 1e-06
F32 = jnp.float32
BF = jnp.bfloat16
VMEM_LIMIT = 56 * 1024 * 1024


def dot_nn(a, b):
    return lax.dot_general(a, b, (((1,), (0,)), ((), ())), preferred_element_type=F32)


def dot_nt(a, b):
    return lax.dot_general(a, b, (((1,), (1,)), ((), ())), preferred_element_type=F32)


def dot_tn(a, b):
    return lax.dot_general(a, b, (((0,), (0,)), ((), ())), preferred_element_type=F32)


def swap(array, axis, bit):
    size = lax.axis_size(axis)
    return lax.ppermute(array, axis, [(a, a ^ bit) for a in range(size)])


def full(shape):
    zeros = (0,) * len(shape)
    return pl.BlockSpec(shape, lambda *_: zeros)


SMEM = pl.BlockSpec(memory_space=pltpu.SMEM)


def call(body, grid, in_specs, out_specs, out_shape, scratch=(), micros=10, aliases=None):
    return pl.pallas_call(
        body,
        grid=grid,
        in_specs=in_specs,
        out_specs=out_specs,
        out_shape=out_shape,
        scratch_shapes=list(scratch),
        input_output_aliases=aliases or {},
        compiler_params=pltpu.CompilerParams(
            dimension_semantics=("arbitrary",) * len(grid), vmem_limit_bytes=VMEM_LIMIT
        ),
        cost_estimate=pl.CostEstimate(flops=micros * 10**9, transcendentals=0, bytes_accessed=micros * 3 * 10**6),
    )


def shape(dims, dtype=BF):
    return jax.ShapeDtypeStruct(dims, dtype)


def sync(*values):
    return lax.optimization_barrier(values)


def over_plane(held):
    return swap(held, "dp", 2), swap(held, "dp", 4)


def over_corner(x_part, y_part):
    return swap(y_part[:2], "dp", 2), swap(x_part[2:], "dp", 4)


def plain_pieces(heads, ffn):
    n_dp = lax.axis_size("dp")
    rows = D // n_dp
    whole = lax.all_gather(ffn, "dp", axis=1)
    parts = [whole[:, :, n * rows : (n + 1) * rows].reshape(4, D, D) for n in (0, 1)]
    final = whole[:, :, 2 * rows : 2 * rows + OUT // n_dp, :HL].reshape(4, OUT, HL)
    return [lax.all_gather(heads, "dp", axis=1, tiled=True)], [jnp.concatenate(parts, axis=1)], final


def scatter_plain(both):
    n_dp = lax.axis_size("dp")
    rows = both.shape[2] // 16 * 16
    total = []
    for first in range(0, rows - FB + 1, FB):
        part = both[:, :, first : first + FB].reshape(4, D, D)
        total.append(lax.psum_scatter(part, "dp", scatter_dimension=1, tiled=True))
    final = both[:, :, rows - 16 :, :256].reshape(4, OUT, 256)
    final = lax.psum_scatter(final, "dp", scatter_dimension=1, tiled=True)
    final = jnp.pad(final, ((0, 0), (0, 16 - OUT // n_dp), (0, 0)))
    sums = lax.psum(both[:, 0, rows - 16 :, 256:], "dp")
    return jnp.concatenate(total + [jnp.concatenate([final, sums], axis=2)], axis=1)


def added(pairs, index):
    sums = [keep[index].astype(F32) + got[index].astype(F32) for keep, got in pairs]
    return sums[0] if len(sums) == 1 else jnp.concatenate(sums, axis=-2)


def plane_first(pairs):
    wide = [tuple(p.reshape((4, 2, 2) + p.shape[2:]) for p in pair) for pair in pairs]
    x_send = added(wide, (slice(0, 2), slice(None), 1)).astype(BF)
    y_send = added(wide, (slice(2, 4), 1)).astype(BF)
    return x_send, y_send


def plane_second(pairs, x_got, y_got):
    wide = [tuple(p.reshape((4, 2, 2) + p.shape[2:]) for p in pair) for pair in pairs]
    x_part = [
        added(wide, (slice(0, 2), n, 0)) + x_got[:, n].astype(F32) for n in range(2)
    ]
    y_part = [
        added(wide, (slice(2, 4), 0, n)) + y_got[:, n].astype(F32) for n in range(2)
    ]
    return x_part[0], x_part[1].astype(BF), y_part[0], y_part[1].astype(BF)


def feature_row(scal, by_xor):
    lane = lax.broadcasted_iota(jnp.int32, (1, D), 1)
    if not by_xor:
        return lane
    part = jnp.zeros((1, D), jnp.int32)
    for n in range(1, PARTS):
        part = part + jnp.where(lane >= n * FB, 1, 0)
    return (((part & 3) * 2 + (part >> 2)) ^ scal[0]) * FB + lane - part * FB


def final_row(scal, by_xor):
    lane = lax.broadcasted_iota(jnp.int32, (1, OUT), 1)
    if not by_xor:
        return lane
    part = lane >> 4
    return (((part & 3) * 2 + (part >> 2)) ^ scal[0]) * 16 + (lane & 15)


def pick(scal, frow, n):
    first = (scal[1] ^ ((n & 1) * 2 + (n >> 1))) * HL
    rows = lax.broadcasted_iota(jnp.int32, (HL, D), 0) + first
    return jnp.where(rows == frow, 1.0, 0.0).astype(BF)


def spread(order_row):
    rows = lax.broadcasted_iota(jnp.int32, (TOK, order_row.shape[1]), 0)
    return jnp.where(rows == order_row, 1.0, 0.0).astype(BF)


def pack_in_body(scal, order_ref, x_ref, mask_ref, cot_ref, out_ref, kept_ref, cot_out_ref, order_out_ref, canon_ref):
    block = pl.program_id(0)

    @pl.when(block == 0)
    def _():
        start, seen = jnp.int32(0), jnp.int32(0)
        for c in range(4):
            start = jnp.where(scal[2 + c] == LONG, seen, start)
            seen = seen + scal[2 + c]
        order = jnp.broadcast_to(order_ref[...], (8, TOK))
        canon_ref[:, :LONG] = pltpu.roll(order, (TOK - start) & (TOK - 1), 1)[:, :LONG]
        lane = lax.broadcasted_iota(jnp.int32, (8, LONG), 1)
        canon_ref[:, LONG:] = jnp.where(lane < start, order[:, :LONG], order[:, LONG:])
        for n in range(4):
            first = pl.multiple_of((scal[1] ^ n) * ROWS, ROWS)
            order_out_ref[:, n * ROWS : (n + 1) * ROWS] = canon_ref[:, pl.ds(first, ROWS)]

    one_hot = spread(order_out_ref[0:1, pl.ds(pl.multiple_of(block * ROWS, ROWS), ROWS)])
    out_ref[...] = dot_nn(x_ref[...], one_hot).astype(BF)
    mask = mask_ref[...].astype(F32)

    @pl.when(block < 2)
    def _():
        kept_ref[...] = dot_nn(jnp.broadcast_to(mask, (16, TOK)).astype(BF), one_hot)[:8]

    @pl.when(block == 0)
    def _():
        cot = (jnp.transpose(cot_ref[...].astype(F32)) * mask).astype(BF)
        cot_out_ref[...] = jnp.transpose(dot_nn(cot, one_hot))


def pack_in(scal, order, inputs, mask_row, cotangent):
    return call(
        pack_in_body,
        (4,),
        [SMEM, full((1, TOK)), full((HL, TOK)), full((1, TOK)), full((TOK, OUT))],
        [
            pl.BlockSpec((HL, ROWS), lambda b: (0, b)),
            pl.BlockSpec((8, ROWS), lambda b: (0, jnp.minimum(b, 1))),
            full((ROWS, OUT)),
            full((8, TOK)),
        ],
        [shape((HL, TOK)), shape((8, KEYS), F32), shape((ROWS, OUT), F32), shape((8, TOK), jnp.int32)],
        [pltpu.VMEM((8, TOK), jnp.int32)],
        micros=6,
    )(scal, order, inputs, mask_row, cotangent)


def join(refs, rows, first=0, last=D):
    parts = [ref[0, :rows, first:last] for ref in refs]
    return parts[0] if len(parts) == 1 else jnp.concatenate(parts, axis=0)


def lanes_of_head(h, shift):
    lane = lax.broadcasted_iota(jnp.int32, (1, 256), 1)
    return (lane >= shift + h * HD) & (lane < shift + (h + 1) * HD)


def allowed_bias(scal, kept):
    pair = scal[1] & 1
    end, count = jnp.int32(0), jnp.int32(0)
    cuts = [jnp.int32(LONG), jnp.int32(LONG)]
    for c in range(4):
        short = scal[2 + c] != LONG
        end = end + jnp.where(short, scal[2 + c], 0)
        count = count + jnp.where(short, 1, 0)
        cuts = [jnp.where(short & (count == n + 1) & (scal[1] >= 2), end, cuts[n]) for n in range(2)]
    q_pos = lax.broadcasted_iota(jnp.int32, (ROWS, 1), 0) + pair * ROWS
    k_pos = lax.broadcasted_iota(jnp.int32, (1, KEYS), 1) + pair * ROWS
    k_pos = k_pos & (KEYS - 1)
    q_seg = jnp.where(q_pos >= cuts[0], 1, 0) + jnp.where(q_pos >= cuts[1], 1, 0)
    k_seg = jnp.where(k_pos >= cuts[0], 1, 0) + jnp.where(k_pos >= cuts[1], 1, 0)
    k_seg = jnp.where(kept > 0.5, k_seg, k_seg + 8)
    return jnp.where((q_seg == k_seg) | (q_pos == k_pos), 0.0, -1e30)


def attend_body(pieces, scal, kept_ref, x0, x2, x1, x3, extra_ref, *refs):
    weights = refs[:pieces]
    xr_ref, fvec_ref, kv_ref, q_ref, ctx_ref, ctx_f_ref, lse_ref, wo_ref, bias_ref = refs[pieces:]
    step = pl.program_id(0)
    rows = D // pieces

    @pl.when(step == 0)
    def _():
        frow = feature_row(scal, pieces > 1)
        upper = jnp.zeros((ROWS, D), F32)
        lower = jnp.zeros((ROWS, D), F32)
        fvec = jnp.zeros((16, D), F32)
        for n, (ref, crossed) in enumerate(((x0, False), (x2, False), (x1, True), (x3, True))):
            chosen = pick(scal, frow, n)
            near, away = ref[:, :ROWS], ref[:, ROWS:]
            if crossed:
                near, away = away, near
            upper = upper + dot_tn(near, chosen)
            lower = lower + dot_tn(away, chosen)
            fvec = fvec + dot_nn(extra_ref[n, :, 512 : 512 + HL], chosen)
        xr_ref[:ROWS] = upper.astype(BF)
        xr_ref[ROWS:] = lower.astype(BF)
        fvec_ref[...] = fvec[:8] + fvec[8:]
        bias_ref[...] = allowed_bias(scal, kept_ref[:1])

    weight = join(weights, rows)
    wo_ref[0] = weight[:, 512:]
    window = extra_ref[pl.ds(step, 1), :, 256:512][0].astype(F32)
    q_bias = window[0:1] + window[1:2]
    v_bias = window[2:3] + window[3:4]
    lane = lax.broadcasted_iota(jnp.int32, (1, 256), 1)
    packed = xr_ref[...]
    kv = dot_nn(packed, weight[:, :384])
    kv_bias = jnp.concatenate([jnp.zeros((1, 128), F32), v_bias], axis=1)
    kv = (kv + kv_bias).astype(BF)
    queries = (dot_nn(packed[:ROWS], weight[:, 384:640]) + q_bias).astype(BF)
    queries = jnp.where(lane < HL, queries, jnp.zeros_like(queries)) * jnp.asarray(0.125, BF)
    kv_ref[0] = kv
    q_ref[0] = queries
    keys, values = kv[:, :256], kv[:, 128:]
    context = jnp.zeros((ROWS, 256), F32)
    for h in range(3):
        own = jnp.where(lanes_of_head(h, 0), queries, jnp.zeros_like(queries))
        scores = dot_nt(own, keys) + bias_ref[...]
        top = jnp.max(scores, axis=1, keepdims=True)
        weight_h = jnp.exp(scores - top)
        total = jnp.sum(weight_h, axis=1, keepdims=True)
        part = dot_nn(weight_h.astype(BF), values) / total
        context = jnp.where(lanes_of_head(h, HD), part, context)
        lse_ref[0, h] = jnp.broadcast_to(top + jnp.log(total), (ROWS, 128))
    ctx_ref[0] = context.astype(BF)
    ctx_f_ref[0] = context


def attend(scal, kept, xs, extra, weights):
    pieces = len(weights)
    return call(
        functools.partial(attend_body, pieces),
        (4,),
        [SMEM, full((8, KEYS))]
        + [full((HL, KEYS))] * 4
        + [full((4, 16, D))]
        + [pl.BlockSpec((1,) + w.shape[1:], lambda j: (j, 0, 0)) for w in weights],
        [
            full((KEYS, D)),
            full((8, D)),
            pl.BlockSpec((1, KEYS, 384), lambda j: (j, 0, 0)),
            pl.BlockSpec((1, ROWS, 256), lambda j: (j, 0, 0)),
            pl.BlockSpec((1, ROWS, 256), lambda j: (j, 0, 0)),
            pl.BlockSpec((1, ROWS, 256), lambda j: (j, 0, 0)),
            pl.BlockSpec((1, 3, ROWS, 128), lambda j: (j, 0, 0, 0)),
            pl.BlockSpec((1, D, 256), lambda j: (j, 0, 0)),
        ],
        [
            shape((KEYS, D)),
            shape((8, D), F32),
            shape((4, KEYS, 384)),
            shape((4, ROWS, 256)),
            shape((4, ROWS, 256)),
            shape((4, ROWS, 256), F32),
            shape((4, 3, ROWS, 128), F32),
            shape((4, D, 256)),
        ],
        [pltpu.VMEM((ROWS, KEYS), F32)],
        micros=23,
    )(scal, kept, *xs, extra, *weights)


def norm(residual, gain, shift):
    mean = jnp.mean(residual, axis=1, keepdims=True)
    spread_row = jnp.mean(residual * residual, axis=1, keepdims=True) - mean * mean
    scale = lax.rsqrt(spread_row + EPS)
    unit = (residual - mean) * scale
    return unit * gain + shift, unit, scale


def norm_back(grad, gain, unit, scale):
    scaled = grad * gain
    mean = jnp.mean(scaled, axis=1, keepdims=True)
    cross = jnp.mean(scaled * unit, axis=1, keepdims=True)
    return scale * (scaled - mean - unit * cross)


def inner_body(pieces, ctx_ref, wo_ref, xr_ref, fvec_ref, extra_ref, *refs):
    weights = refs[:pieces]
    normed_ref, unit_ref, scale_ref, low_ref, act_ref, slope_ref = refs[pieces:]
    step = pl.program_id(0)

    @pl.when(step == 0)
    def _():
        lane = lax.broadcasted_iota(jnp.int32, (1, 256), 1)
        total = xr_ref[...].astype(F32) + fvec_ref[0:1]
        for n in range(4):
            total = total + dot_nt(ctx_ref[n], wo_ref[n])
        normed, unit, scale = norm(total, fvec_ref[2:3], fvec_ref[3:4])
        normed_ref[...] = normed
        unit_ref[...] = unit
        scale_ref[...] = jnp.broadcast_to(scale, (ROWS, 128))
        low_ref[...] = normed.astype(BF)

    window = extra_ref[pl.ds(step, 1), :, 256:512][0].astype(F32)
    bias = jnp.concatenate([window[4 + n : 5 + n] + window[7 + n : 8 + n] for n in range(3)], axis=1)
    pre = dot_nn(low_ref[...], join(weights, D // pieces)) + bias
    half = 0.5 + 0.5 * lax.erf(pre * math.sqrt(0.5))
    act_ref[0] = (pre * half).astype(BF)
    slope_ref[0] = half + pre * (jnp.exp(pre * pre * -0.5) * (1.0 / math.sqrt(2.0 * math.pi)))


def inner(context, wo, packed, fvec, extra, weights):
    pieces = len(weights)
    return call(
        functools.partial(inner_body, pieces),
        (4,),
        [full((4, ROWS, 256)), full((4, D, 256)), full((ROWS, D)), full((8, D)), full((4, 16, D))]
        + [pl.BlockSpec((1, D // pieces, D), lambda j: (j, 0, 0)) for w in weights],
        [
            full((ROWS, D)),
            full((ROWS, D)),
            full((ROWS, 128)),
            full((ROWS, D)),
            pl.BlockSpec((1, ROWS, D), lambda j: (j, 0, 0)),
            pl.BlockSpec((1, ROWS, D), lambda j: (j, 0, 0)),
        ],
        [
            shape((ROWS, D), F32),
            shape((ROWS, D), F32),
            shape((ROWS, 128), F32),
            shape((ROWS, D)),
            shape((4, ROWS, D)),
            shape((4, ROWS, D), F32),
        ],
    )(context, wo, packed, fvec, extra, *weights)


def outer_body(pieces, scal, act_ref, normed_ref, fvec_ref, fin_ref, cot_ref, *refs):
    weights = refs[:pieces]
    grad_ref, low_ref, vec_ref, fin_grad_ref, sums_ref, total_ref = refs[pieces:]
    step = pl.program_id(0)
    part = dot_nt(act_ref[0], join(weights, D // pieces))

    @pl.when(step == 0)
    def _():
        total_ref[...] = normed_ref[...] + fvec_ref[1:2] + part

    @pl.when(step > 0)
    def _():
        total_ref[...] += part

    @pl.when(step == 3)
    def _():
        gain = fvec_ref[4:5]
        normed, unit, scale = norm(total_ref[...], gain, fvec_ref[5:6])
        low = normed.astype(BF)
        frow = feature_row(scal, pieces > 1)
        final = jnp.zeros((OUT, D), F32)
        for n in range(4):
            final = final + dot_nn(fin_ref[n], pick(scal, frow, n))
        columns = lax.broadcasted_iota(jnp.int32, (OUT, OUT), 0)
        place = jnp.where(columns == final_row(scal, pieces > 1), 1.0, 0.0).astype(BF)
        final = dot_nn(place, final.astype(BF)).astype(BF)
        projected = dot_nt(low, final)
        length = lax.rsqrt(jnp.sum(projected * projected, axis=1, keepdims=True) + EPS)
        units = projected * length
        vec_ref[...] = jnp.transpose(units).astype(BF)
        grads = cot_ref[...]
        grads = length * (grads - units * jnp.sum(grads * units, axis=1, keepdims=True))
        grads = grads.astype(BF)
        fin_grad = dot_tn(place, dot_tn(grads, low).astype(BF)).astype(BF)
        for n in range(4):
            fin_grad_ref[n] = dot_nt(fin_grad, pick(scal, frow, n)).astype(BF)
        grad = dot_nn(grads, final)
        back = norm_back(grad, gain, unit, scale)
        grad_ref[...] = back
        low_ref[...] = back.astype(BF)
        sums_ref[0:1] = jnp.sum(grad * unit, axis=0, keepdims=True)
        sums_ref[1:2] = jnp.sum(grad, axis=0, keepdims=True)
        sums_ref[2:3] = jnp.sum(back, axis=0, keepdims=True)
        sums_ref[3:] = jnp.zeros((5, D), F32)


def outer(scal, act, normed, fvec, final, cot, weights):
    pieces = len(weights)
    return call(
        functools.partial(outer_body, pieces),
        (4,),
        [SMEM]
        + [pl.BlockSpec((1, ROWS, D), lambda j: (j, 0, 0)), full((ROWS, D)), full((8, D))]
        + [full((4, OUT, HL)), full((ROWS, OUT))]
        + [pl.BlockSpec((1, D // pieces, D), lambda j: (j, 1, 0)) for w in weights],
        [
            full((ROWS, D)),
            full((ROWS, D)),
            full((OUT, ROWS)),
            full((4, OUT, HL)),
            full((8, D)),
        ],
        [
            shape((ROWS, D), F32),
            shape((ROWS, D)),
            shape((OUT, ROWS)),
            shape((4, OUT, HL)),
            shape((8, D), F32),
        ],
        [pltpu.VMEM((ROWS, D), F32)],
    )(scal, act, normed, fvec, final, cot, *weights)


def split_out(total, keep_ref, send_ref, extra=None):
    low = total.astype(BF).reshape(PARTS, FB, D)
    half = PARTS // 2
    keep_ref[0, :, :FB] = low[:half]
    send_ref[0, :, :FB] = low[half:]
    if extra is not None:
        keep_ref[0, :, FB:] = extra[:half]
        send_ref[0, :, FB:] = extra[half:]


def outer_back_body(pieces, low_ref, act_ref, slope_ref, *refs):
    weights = refs[:pieces]
    keep_ref, send_ref, pre_ref, bias_ref = refs[pieces:]
    low = low_ref[...]
    split_out(dot_tn(low, act_ref[0]), keep_ref, send_ref)
    grad = dot_nn(low, join(weights, D // pieces)) * slope_ref[0]
    pre_ref[0] = grad.astype(BF)
    bias_ref[0] = jnp.broadcast_to(jnp.sum(grad, axis=0, keepdims=True), (8, D))


def outer_back(low, act, slope, weights):
    pieces = len(weights)
    half = PARTS // 2
    wide = pl.BlockSpec((1, half, FB, D), lambda j: (j, 0, 0, 0))
    block = pl.BlockSpec((1, ROWS, D), lambda j: (j, 0, 0))
    return call(
        functools.partial(outer_back_body, pieces),
        (4,),
        [full((ROWS, D)), block, block]
        + [pl.BlockSpec((1, D // pieces, D), lambda j: (j, 1, 0)) for w in weights],
        [wide, wide, block, pl.BlockSpec((1, 8, D), lambda j: (j, 0, 0))],
        [
            shape((4, half, FB, D)),
            shape((4, half, FB, D)),
            shape((4, ROWS, D)),
            shape((4, 8, D), F32),
        ],
    )(low, act, slope, *weights)


def inner_back_body(pieces, scal, pre_ref, next_ref, low_ref, grad_ref, unit_ref, scale_ref, fvec_ref, fin_ref, hid_ref, sums_ref, *refs):
    weights = refs[:pieces]
    one_ref, one_low_ref, keep_ref, send_ref, total_ref, all_ref = refs[pieces:]
    step = pl.program_id(0)

    @pl.when(step == 0)
    def _():
        total_ref[...] = grad_ref[...]

    @pl.when(step < 4)
    def _():
        total_ref[...] += dot_nt(pre_ref[0], join(weights, D // pieces))

    @pl.when(step == 3)
    def _():
        grad = total_ref[...]
        unit = unit_ref[...]
        back = norm_back(grad, fvec_ref[2:3], unit, scale_ref[:, :1])
        one_ref[...] = back
        one_low_ref[...] = back.astype(BF)
        all_ref[0:3] = sums_ref[0:3]
        all_ref[3:4] = jnp.sum(grad * unit, axis=0, keepdims=True)
        all_ref[4:5] = jnp.sum(grad, axis=0, keepdims=True)
        all_ref[5:6] = jnp.sum(back, axis=0, keepdims=True)
        all_ref[6:] = jnp.zeros((10, D), F32)

    @pl.when(step >= 4)
    def _():
        n = step - 4
        sums_low = dot_nt(all_ref[...].astype(BF), pick(scal, feature_row(scal, pieces > 1), n))
        tile = jnp.concatenate([sums_low, jnp.zeros((16, 64), F32)], axis=1)
        hidden = hid_ref[pl.ds(n, 1), 0:1][0]
        hidden = jnp.concatenate(
            [hidden[:, 256 * k : 256 * (k + 1)] for k in range(3)] + [jnp.zeros((13, 256), F32)], axis=0
        )
        wide = jnp.concatenate([tile, hidden], axis=1).astype(BF)
        wide = jnp.broadcast_to(wide[None], (PARTS, 16, 512))
        fin = fin_ref[pl.ds(n, 1)][0].reshape(PARTS, OUT // PARTS, HL)
        fin = jnp.concatenate([fin, jnp.zeros((PARTS, OUT // PARTS, 64), BF)], axis=2)
        extra = jnp.concatenate([fin, wide], axis=2)
        split_out(dot_tn(low_ref[...], next_ref[0]), keep_ref, send_ref, extra)


def inner_back(scal, pre, low, grad, unit, scale, fvec, fin, hid, sums, weights):
    pieces = len(weights)
    half = PARTS // 2
    early = lambda j: (jnp.minimum(j, 3), 0, 0)
    late = lambda j: (jnp.maximum(j - 4, 0), 0, 0)
    wide = pl.BlockSpec((1, half, FB + 16, D), lambda j: (jnp.maximum(j - 4, 0), 0, 0, 0))
    return call(
        functools.partial(inner_back_body, pieces),
        (8,),
        [
            SMEM,
            pl.BlockSpec((1, ROWS, D), early),
            pl.BlockSpec((1, ROWS, D), late),
            full((ROWS, D)),
            full((ROWS, D)),
            full((ROWS, D)),
            full((ROWS, 128)),
            full((8, D)),
            full((4, OUT, HL)),
            full((4, 8, D)),
            full((8, D)),
        ]
        + [pl.BlockSpec((1, D // pieces, D), early) for w in weights],
        [full((ROWS, D)), full((ROWS, D)), wide, wide],
        [
            shape((ROWS, D), F32),
            shape((ROWS, D)),
            shape((4, half, FB + 16, D)),
            shape((4, half, FB + 16, D)),
        ],
        [pltpu.VMEM((ROWS, D), F32), pltpu.VMEM((16, D), F32)],
    )(scal, pre, pre, low, grad, unit, scale, fvec, fin, hid, sums, *weights)


def attend_back_body(pieces, first, count, scal, kept_ref, xr_ref, kv_ref, q_ref, ctx_ref, ctx_f_ref, lse_ref, one_ref, low_ref, *refs):
    weights = refs[:pieces]
    refs = refs[pieces + (2 if first else 0) :]
    keep_ref, send_ref = refs[:2]
    bias_ref, total_ref = refs[-2:]
    step = pl.program_id(0)

    @pl.when(step == 0)
    def _():
        bias_ref[...] = allowed_bias(scal, kept_ref[:1])
        total_ref[:ROWS] = one_ref[:ROWS]
        total_ref[ROWS:] = one_ref[ROWS:] if first else jnp.zeros((ROWS, D), F32)

    weight = join(weights, D // pieces)
    low = low_ref[...]
    lane = lax.broadcasted_iota(jnp.int32, (1, 256), 1)
    grad_ctx = dot_nn(low, weight[:, 512:])
    grad_ctx = jnp.where(lane >= HD, grad_ctx, 0.0).astype(BF)
    keys, values = kv_ref[0, :, :256], kv_ref[0, :, 128:]
    queries = q_ref[0]
    products = grad_ctx.astype(F32) * ctx_f_ref[0]
    dq = jnp.zeros((ROWS, 256), F32)
    dk = jnp.zeros((KEYS, 256), F32)
    dv = jnp.zeros((KEYS, 256), F32)
    zero = jnp.zeros_like(queries)
    for h in range(3):
        own = jnp.where(lanes_of_head(h, 0), queries, zero)
        own_grad = jnp.where(lanes_of_head(h, HD), grad_ctx, zero)
        row_dot = jnp.sum(jnp.where(lanes_of_head(h, HD), products, 0.0), axis=1, keepdims=True)
        scores = dot_nt(own, keys) + bias_ref[...]
        prob = jnp.exp(scores - lse_ref[0, h][:, :1])
        dv = dv + dot_tn(prob.astype(BF), own_grad)
        grad_scores = (prob * (dot_nt(own_grad, values) - row_dot)).astype(BF)
        dq = jnp.where(lanes_of_head(h, 0), dot_nn(grad_scores, keys), dq)
        dk = dk + dot_tn(grad_scores, own)
    dq = dq * 0.125
    gap = jnp.zeros((KEYS, 128), F32)
    dkv = jnp.concatenate([dk, gap], axis=1) + jnp.concatenate([gap, dv], axis=1)
    q_sum = jnp.sum(dq, axis=0, keepdims=True)
    v_sum = jnp.sum(dv, axis=0, keepdims=True)
    dkv = dkv.astype(BF)
    dq = dq.astype(BF)
    packed = xr_ref[...]
    low_kv = dot_tn(packed, dkv)
    from_q = dot_tn(packed[:ROWS], dq)
    from_o = dot_tn(low, ctx_ref[0])
    gap = jnp.zeros((D, 128), F32)
    from_qo = jnp.concatenate([from_q, gap], axis=1) + jnp.concatenate([gap, from_o], axis=1)
    sums = jnp.concatenate([q_sum, v_sum, jnp.zeros((14, 256), F32)], axis=0)
    extra = jnp.concatenate([jnp.zeros((16, 256), F32), sums, jnp.zeros((16, 256), F32)], axis=1)
    extra = jnp.broadcast_to(extra.astype(BF)[None], (PARTS, 16, D))
    split_out(jnp.concatenate([low_kv, from_qo], axis=1), keep_ref, send_ref, extra)
    total_ref[...] += dot_nt(dkv, weight[:, :384])
    total_ref[:ROWS] += dot_nt(dq, weight[:, 384:640])

    @pl.when(step == count - 1)
    def _():
        if first + count < 4:
            refs[2][...] = total_ref[...]
            return
        x0_ref, x2_ref, x1_ref, x3_ref = refs[2:6]
        grads = total_ref[...].astype(BF)
        frow = feature_row(scal, pieces > 1)
        x0_ref[...] = dot_nt(pick(scal, frow, 0), grads)
        x2_ref[...] = dot_nt(pick(scal, frow, 1), grads)
        for n, ref in ((2, x1_ref), (3, x3_ref)):
            part = dot_nt(pick(scal, frow, n), grads).astype(BF)
            ref[:, :ROWS] = part[:, ROWS:]
            ref[:, ROWS:] = part[:, :ROWS]


def attend_back(scal, kept, packed, kv, queries, context, context_f, lse, one, low, weights, first, count, held):
    pieces = len(weights)
    half = PARTS // 2
    at = lambda j: (j + first, 0, 0)
    wide = pl.BlockSpec((1, half, FB + 16, D), lambda j: (j + first, 0, 0, 0))
    n_in = 10 + pieces
    last = first + count == 4
    tall = shape((HL, KEYS), F32)
    return call(
        functools.partial(attend_back_body, pieces, first, count),
        (count,),
        [
            SMEM,
            full((8, KEYS)),
            full((KEYS, D)),
            pl.BlockSpec((1, KEYS, 384), at),
            pl.BlockSpec((1, ROWS, 256), at),
            pl.BlockSpec((1, ROWS, 256), at),
            pl.BlockSpec((1, ROWS, 256), at),
            pl.BlockSpec((1, 3, ROWS, 128), lambda j: (j + first, 0, 0, 0)),
            full(one.shape),
            full((ROWS, D)),
        ]
        + [pl.BlockSpec((1,) + w.shape[1:], at) for w in weights]
        + [pl.BlockSpec(memory_space=pl.ANY)] * len(held),
        [wide, wide] + ([full((HL, KEYS))] * 4 if last else [full((KEYS, D))]),
        [shape((4, half, FB + 16, D)), shape((4, half, FB + 16, D))]
        + ([tall, tall, shape((HL, KEYS)), shape((HL, KEYS))] if last else [shape((KEYS, D), F32)]),
        [pltpu.VMEM((ROWS, KEYS), F32), pltpu.VMEM((KEYS, D), F32)],
        micros=9 * count,
        aliases={n_in + n: n for n in range(len(held))},
    )(scal, kept, packed, kv, queries, context, context_f, lse, one, low, *weights, *held)


def pack_out_body(order_ref, mask_ref, x_ref, vec_ref, x_out_ref, vec_out_ref, total_ref):
    step = pl.program_id(0)
    both = jnp.concatenate([x_ref[...], vec_ref[0]], axis=0)
    part = dot_nt(both, spread(order_ref[:1]))

    @pl.when(step == 0)
    def _():
        total_ref[...] = part

    @pl.when(step > 0)
    def _():
        total_ref[...] += part

    @pl.when(step == 3)
    def _():
        x_out_ref[...] = total_ref[:HL]
        vec_out_ref[...] = jnp.transpose(total_ref[HL:] * mask_ref[...].astype(F32))


def pack_out(order, mask_row, grads, vecs):
    return call(
        pack_out_body,
        (4,),
        [
            pl.BlockSpec((8, ROWS), lambda b: (0, b)),
            full((1, TOK)),
            pl.BlockSpec((HL, ROWS), lambda b: (0, b)),
            pl.BlockSpec((1, OUT, ROWS), lambda b: (b, 0, 0)),
        ],
        [full((HL, TOK)), full((TOK, OUT))],
        [shape((HL, TOK), F32), shape((TOK, OUT), F32)],
        [pltpu.VMEM((HL + OUT, TOK), F32)],
        micros=8,
    )(order, mask_row, grads, vecs)


def halves(vector):
    high = vector.astype(BF)
    return high, (vector - high.astype(F32)).astype(BF)


def pack_weights_body(k_ref, v_ref, q_ref, o_ref, in_ref, out_ref, fin_ref, qb, vb, inb, ob, outb, g1, s1, g2, s2, heads_ref, ffn_ref):
    turned = lambda ref: jnp.transpose(ref[...].astype(F32)).astype(BF)
    heads_ref[:FB] = jnp.concatenate([k_ref[...], v_ref[...], q_ref[...], turned(o_ref)], axis=1)
    ffn_ref[:FB] = in_ref[...]
    ffn_ref[FB : 2 * FB] = out_ref[...]
    qb, vb, inb, ob, outb, g1, s1, g2, s2 = (ref[...].reshape(1, ref.shape[0]) for ref in (qb, vb, inb, ob, outb, g1, s1, g2, s2))
    gap = jnp.zeros((1, 64), F32)
    window = []
    for value in (jnp.concatenate([qb, gap], axis=1), jnp.concatenate([gap, vb], axis=1)):
        window += list(halves(value))
    hidden = [halves(inb[:, n * 256 : (n + 1) * 256]) for n in range(3)]
    window += [high for high, _ in hidden] + [low for _, low in hidden]
    window = jnp.concatenate(window + [jnp.zeros((6, 256), BF)], axis=0)
    features = [halves(jnp.concatenate([value, gap], axis=1)) for value in (ob, outb, g1, s1, g2, s2)]
    pad = [jnp.zeros((2, 256), BF)]
    features = jnp.concatenate([high for high, _ in features] + pad + [low for _, low in features] + pad, axis=0)
    final = jnp.concatenate([fin_ref[...], jnp.zeros((16, 64), BF)], axis=1)
    extra = jnp.concatenate([final, window, features], axis=1)
    heads_ref[FB:] = extra
    ffn_ref[2 * FB :] = extra


def pack_weights(weights, vectors):
    return call(
        pack_weights_body,
        (1,),
        [full(w.shape) for w in weights] + [full(v.shape) for v in vectors],
        [full((FB + 16, D)), full((2 * FB + 16, D))],
        [shape((FB + 16, D)), shape((2 * FB + 16, D))],
        micros=3,
    )(*weights, *vectors)


def ffn_out_body(a_ref, b_ref, in_ref, out_ref, fin_ref, ob, inb, outb, g1, s1, g2, s2):
    total = a_ref[...] + b_ref[...].astype(F32)
    out_ref[...] = total[:FB]
    in_ref[...] = total[FB : 2 * FB]
    tile = total[2 * FB :]
    fin_ref[...] = tile[:, :HL]
    for n, ref in ((5, ob), (2, outb), (3, g1), (4, s1), (0, g2), (1, s2)):
        ref[...] = tile[n : n + 1, 256 : 256 + HL].reshape(HL)
    inb[...] = jnp.concatenate([tile[n : n + 1, 512:] for n in range(3)], axis=1).reshape(D)


def ffn_out(a, b):
    dims = [(FB, D), (FB, D), (16, HL), (HL,), (D,)] + [(HL,)] * 5
    return call(
        ffn_out_body, (1,), [full(a.shape), full(b.shape)], [full(d) for d in dims], [shape(d, F32) for d in dims], micros=3
    )(a, b)


def heads_out_body(a_ref, b_ref, q_ref, k_ref, v_ref, o_ref, qb, vb):
    total = a_ref[...] + b_ref[...].astype(F32)
    k_ref[...] = total[:FB, :HL]
    v_ref[...] = total[:FB, HL:384]
    q_ref[...] = total[:FB, 384:576]
    o_ref[...] = jnp.transpose(total[:FB, 576:])
    qb[...] = total[FB : FB + 1, 256 : 256 + HL].reshape(HL)
    vb[...] = total[FB + 1 : FB + 2, 320:512].reshape(HL)


def heads_out(a, b):
    dims = [(FB, HL)] * 3 + [(HL, FB), (HL,), (HL,)]
    return call(
        heads_out_body, (1,), [full(a.shape), full(b.shape)], [full(d) for d in dims], [shape(d, F32) for d in dims], micros=3
    )(a, b)


def hi_lo(vector):
    high = vector.astype(BF)
    high = lax.optimization_barrier(high)
    return high, (vector - high.astype(F32)).astype(BF)


def extra_rows(final_t, q_bias, v_bias, inner_bias, features):
    q_hi, q_lo = hi_lo(jnp.pad(q_bias, (0, 64)))
    v_hi, v_lo = hi_lo(jnp.pad(v_bias, (64, 0)))
    in_hi, in_lo = hi_lo(inner_bias.reshape(3, 256))
    window = jnp.concatenate([jnp.stack([q_hi, q_lo, v_hi, v_lo]), in_hi, in_lo], axis=0)
    window = jnp.pad(window, ((0, 6), (0, 0)))
    f_hi, f_lo = hi_lo(jnp.pad(jnp.stack(features), ((0, 2), (0, 64))))
    final_t = jnp.pad(final_t, ((0, 16 - final_t.shape[0]), (0, 64)))
    return jnp.concatenate([final_t, window, jnp.concatenate([f_hi, f_lo], axis=0)], axis=1)


def local(
    inputs,
    token_order,
    lengths,
    token_mask,
    cotangent,
    query_weight,
    key_weight,
    value_weight,
    output_weight,
    inner_weight,
    outer_weight,
    final_weight,
    query_bias,
    value_bias,
    output_bias,
    inner_bias,
    outer_bias,
    first_gain,
    first_shift,
    second_gain,
    second_shift,
):
    m, i = lax.axis_index("mp"), lax.axis_index("dp")
    n_dp = lax.axis_size("dp")
    rows = D // n_dp
    by_xor = n_dp == 8
    scal = jnp.concatenate([jnp.stack([i, m]).astype(jnp.int32), lengths[0]])
    features_of = [output_bias, outer_bias, first_gain, first_shift, second_gain, second_shift]

    if by_xor:
        heads_own, ffn_own = pack_weights(
            [key_weight, value_weight, query_weight, output_weight, inner_weight, outer_weight.T, final_weight.T],
            [query_bias, value_bias, inner_bias] + features_of,
        )
    else:
        extra = extra_rows(final_weight.T, query_bias, value_bias, inner_bias, features_of)
        heads_own = jnp.concatenate([key_weight, value_weight, query_weight, output_weight.T], axis=1)
        heads_own = jnp.concatenate([heads_own, extra], axis=0)
        ffn_own = jnp.concatenate([inner_weight, outer_weight.T, extra], axis=0)

    mask_row = token_mask.reshape(1, TOK)
    heads_own, ffn_own, inputs = sync(heads_own, ffn_own, inputs)
    heads_got = swap(heads_own, "mp", 2)
    features, kept, cot, order = pack_in(scal, token_order, inputs, mask_row, cotangent)
    near, away = features[:, :KEYS], features[:, KEYS:]
    heads_got, ffn_own, near, away = sync(heads_got, ffn_own, near, away)

    heads_low = jnp.stack([heads_own, heads_got])
    heads_high = swap(heads_low, "mp", 1)
    ffn_got = swap(ffn_own, "mp", 2)
    heads_high, ffn_got = sync(heads_high, ffn_got)

    heads = jnp.concatenate([heads_low[:, :rows], heads_high[:, :rows]], axis=0)
    extras = jnp.concatenate([heads_low[:, rows:], heads_high[:, rows:]], axis=0)
    ffn_low = jnp.stack([ffn_own, ffn_got])
    ffn_high = swap(ffn_low, "mp", 1)
    if by_xor:
        head_x, head_y = over_plane(heads)
        ffn_high, head_x, head_y, near, away = sync(ffn_high, head_x, head_y, near, away)
        ffn = jnp.concatenate([ffn_low, ffn_high], axis=0)
        far_a, far_b = over_corner(head_x, head_y)
        ffn_x, ffn_y = over_plane(ffn)
        x2, x1 = swap(away, "mp", 2), swap(near, "mp", 1)
        head_pieces = [swap(p, "dp", 1) for p in (heads, head_x, head_y)]
        x2, x1, far_a, far_b, *head_pieces = sync(x2, x1, far_a, far_b, *head_pieces)
        x3 = swap(x2, "mp", 1)
        far = jnp.concatenate([far_a, far_b], axis=0)
        head_pieces = [heads, head_x, head_y, far] + head_pieces + [swap(far, "dp", 1)]
        x3, ffn_x, ffn_y, last = sync(x3, ffn_x, ffn_y, head_pieces[-1])
        head_pieces[-1] = last
        far_a, far_b = over_corner(ffn_x, ffn_y)
        ffn_pieces = [swap(p, "dp", 1) for p in (ffn, ffn_x, ffn_y)]
    else:
        ffn = jnp.concatenate([ffn_low, ffn_high], axis=0)
        x2, x1 = swap(away, "mp", 2), swap(near, "mp", 1)
        x3 = swap(x2, "mp", 1)
        head_pieces, ffn_pieces, final = plain_pieces(heads, ffn)

    packed, fvec, kv, queries, context, context_f, lse, wo = attend(
        scal, kept, (near, x2, x1, x3), extras, head_pieces
    )
    if by_xor:
        context, far_a, far_b, *ffn_pieces = sync(context, far_a, far_b, *ffn_pieces)
        far = jnp.concatenate([far_a, far_b], axis=0)
        ffn_pieces = [ffn, ffn_x, ffn_y, far] + ffn_pieces + [swap(far, "dp", 1)]
        final = jnp.concatenate([p[:, 2 * FB :, :HL] for p in ffn_pieces], axis=1)
    normed, unit, scale, normed_low, act, slope = inner(context, wo, packed, fvec, extras, ffn_pieces)
    grad_two, two_low, vec, fin_grad, sums = outer(scal, act, normed, fvec, final, cot, ffn_pieces)
    vec_got = swap(vec, "mp", 1)
    outer_keep, outer_send, pre, hid_sums = outer_back(two_low, act, slope, ffn_pieces)
    vec_got, outer_send, pre = sync(vec_got, outer_send, pre)
    vec_low = jnp.stack([vec, vec_got])
    vec_high = swap(vec_low, "mp", 2)
    saved = (kept, packed, kv, queries, context, context_f, lse)

    def inner_part(pre):
        return inner_back(scal, pre, normed_low, grad_two, unit, scale, fvec, fin_grad, hid_sums, sums, ffn_pieces)

    if by_xor:
        outer_got = swap(outer_send, "dp", 1)
        grad_one, one_low, inner_keep, inner_send = inner_part(pre)
        outer_got, vec_high, one_low, inner_send = sync(outer_got, vec_high, one_low, inner_send)
        inner_got = swap(inner_send, "dp", 1)
        head_keep, head_send, partial = attend_back(scal, *saved, grad_one, one_low, head_pieces, 0, 1, ())
        inner_got, partial = sync(inner_got, partial)
        pairs = ((outer_keep, outer_got), (inner_keep, inner_got))
        x_send, y_send = plane_first(pairs)
        partial, x_send, y_send = sync(partial, x_send, y_send)
        x_got, y_got = swap(x_send, "dp", 2), swap(y_send, "dp", 4)
        head_keep, head_send, dx0, dx2, dx1, dx3 = attend_back(
            scal, *saved, partial, one_low, head_pieces, 1, 3, (head_keep, head_send)
        )
        dx3, dx1, head_send, x_got, y_got = sync(dx3, dx1, head_send, x_got, y_got)
        dx3_got = swap(dx3, "mp", 1)
        head_got = swap(head_send, "dp", 1)
        upper, to_y, lower, to_x = plane_second(pairs, x_got, y_got)
        from_y, from_x = swap(to_y, "dp", 4), swap(to_x, "dp", 2)
        dx3_got, head_got, dx1 = sync(dx3_got, head_got, dx1)
        far = swap((dx2 + dx3_got.astype(F32)).astype(BF), "mp", 2)
        dx1_got = swap(dx1, "mp", 1)
        pairs = ((head_keep, head_got),)
        x_send, y_send = plane_first(pairs)
        x_got, y_got = swap(x_send, "dp", 2), swap(y_send, "dp", 4)
        from_y, from_x, dx1_got = sync(from_y, from_x, dx1_got)
        upper = upper + from_y.astype(F32)
        lower = (lower + from_x.astype(F32)).astype(BF)
        lower_got = swap(lower, "mp", 1)
        x_got, y_got, far = sync(x_got, y_got, far)
        grads = jnp.concatenate([(dx0 + dx1_got.astype(F32)).astype(BF), far], axis=1)
        h_upper, to_y, h_lower, to_x = plane_second(pairs, x_got, y_got)
        from_y, from_x = swap(to_y, "dp", 4), swap(to_x, "dp", 2)
        vecs = jnp.concatenate([vec_low, vec_high], axis=0)
        inputs_grad, vectors = pack_out(order, mask_row, grads, vecs)
        inputs_grad, lower_got, from_y, from_x = sync(inputs_grad, lower_got, from_y, from_x)
        upper = upper + lower_got.astype(F32)
        last = swap(upper[1].astype(BF), "mp", 2)
        h_upper = h_upper + from_y.astype(F32)
        h_lower = (h_lower + from_x.astype(F32)).astype(BF)
        lower_got = swap(h_lower, "mp", 1)
        last, lower_got = sync(last, lower_got)
        h_upper = h_upper + lower_got.astype(F32)
        h_last = swap(h_upper[1].astype(BF), "mp", 2)
        g_in, g_out, g_fin, g_ob, g_inb, g_outb, g_g1, g_s1, g_g2, g_s2 = ffn_out(upper[0], last)
        g_q, g_k, g_v, g_o, g_qb, g_vb = heads_out(h_upper[0], h_last)
        g_out, g_fin = g_out.T, g_fin.T
    else:
        grad_one, one_low, inner_keep, inner_send = inner_part(pre)
        head_keep, head_send, partial = attend_back(scal, *saved, grad_one, one_low, head_pieces, 0, 1, ())
        head_keep, head_send, dx0, dx2, dx1, dx3 = attend_back(
            scal, *saved, partial, one_low, head_pieces, 1, 3, (head_keep, head_send)
        )
        far = swap((dx2 + swap(dx3, "mp", 1).astype(F32)).astype(BF), "mp", 2)
        grads = jnp.concatenate([(dx0 + swap(dx1, "mp", 1).astype(F32)).astype(BF), far], axis=1)
        vecs = jnp.concatenate([vec_low, vec_high], axis=0)
        inputs_grad, vectors = pack_out(order, mask_row, grads, vecs)
        ends = []
        for keep, send in (
            (jnp.concatenate([outer_keep, inner_keep], axis=2), jnp.concatenate([outer_send, inner_send], axis=2)),
            (head_keep, head_send),
        ):
            total = scatter_plain(jnp.concatenate([keep, send], axis=1).astype(F32))
            upper = total[:2] + swap(total[2:].astype(BF), "mp", 1).astype(F32)
            ends.append(upper[0] + swap(upper[1].astype(BF), "mp", 2).astype(F32))
        ffn_sum, head_sum = ends
        tile, head_tile = ffn_sum[2 * rows :], head_sum[rows:]
        g_out, g_in, g_fin = ffn_sum[:rows].T, ffn_sum[rows : 2 * rows], tile[: OUT // n_dp, :HL].T
        g_g2, g_s2, g_outb, g_g1, g_s1, g_ob = (tile[n, 256 : 256 + HL] for n in range(6))
        g_inb = tile[:3, 512:].reshape(D)
        g_k, g_v, g_q, g_o = head_sum[:rows, :HL], head_sum[:rows, HL:384], head_sum[:rows, 384:576], head_sum[:rows, 576:].T
        g_qb, g_vb = head_tile[0, 256 : 256 + HL], head_tile[1, 320:512]
    return (
        vectors,
        inputs_grad,
        g_q,
        g_k,
        g_v,
        g_o,
        g_in,
        g_out,
        g_fin,
        g_qb,
        g_vb,
        g_ob,
        g_inb,
        g_outb,
        g_g1,
        g_s1,
        g_g2,
        g_s2,
    )


def solution(mesh):
    return jax.shard_map(
        local,
        mesh=mesh,
        in_specs=(
            P("mp", "dp"),
            P("dp", None),
            P("dp", None),
            P("dp"),
            P("dp", None),
            P("dp", "mp"),
            P("dp", "mp"),
            P("dp", "mp"),
            P("mp", "dp"),
            P("dp", "mp"),
            P("mp", "dp"),
            P("mp", "dp"),
            P("mp"),
            P("mp"),
            P("mp"),
            P("mp"),
            P("mp"),
            P("mp"),
            P("mp"),
            P("mp"),
            P("mp"),
        ),
        out_specs=(
            P("dp", None),
            P("mp", "dp"),
            P("dp", "mp"),
            P("dp", "mp"),
            P("dp", "mp"),
            P("mp", "dp"),
            P("dp", "mp"),
            P("mp", "dp"),
            P("mp", "dp"),
            P("mp"),
            P("mp"),
            P("mp"),
            P("mp"),
            P("mp"),
            P("mp"),
            P("mp"),
            P("mp"),
            P("mp"),
        ),
        check_vma=False,
    )
```

```python
import functools
import math

import jax
import jax.numpy as jnp
from jax import lax
from jax.experimental import pallas as pl
from jax.experimental.pallas import tpu as pltpu
from jax.sharding import PartitionSpec as P

D = 768
HD = 64
HL = 192
FB = 96
PARTS = 8
OUT = 128
TOK = 2048
ROWS = 512
KEYS = 1024
LONG = 1024
CHUNK = 256
EPS = 1e-06
F32 = jnp.float32
BF = jnp.bfloat16
VMEM_LIMIT = 56 * 1024 * 1024


def dot_nn(a, b):
    return lax.dot_general(a, b, (((1,), (0,)), ((), ())), preferred_element_type=F32)


def dot_nt(a, b):
    return lax.dot_general(a, b, (((1,), (1,)), ((), ())), preferred_element_type=F32)


def dot_tn(a, b):
    return lax.dot_general(a, b, (((0,), (0,)), ((), ())), preferred_element_type=F32)


def swap(array, axis, bit):
    size = lax.axis_size(axis)
    return lax.ppermute(array, axis, [(a, a ^ bit) for a in range(size)])


def full(shape):
    zeros = (0,) * len(shape)
    return pl.BlockSpec(shape, lambda *_: zeros)


SMEM = pl.BlockSpec(memory_space=pltpu.SMEM)


def call(body, grid, in_specs, out_specs, out_shape, scratch=(), micros=10, aliases=None):
    return pl.pallas_call(
        body,
        grid=grid,
        in_specs=in_specs,
        out_specs=out_specs,
        out_shape=out_shape,
        scratch_shapes=list(scratch),
        input_output_aliases=aliases or {},
        compiler_params=pltpu.CompilerParams(
            dimension_semantics=("arbitrary",) * len(grid), vmem_limit_bytes=VMEM_LIMIT
        ),
        cost_estimate=pl.CostEstimate(flops=micros * 10**9, transcendentals=0, bytes_accessed=micros * 3 * 10**6),
    )


def shape(dims, dtype=BF):
    return jax.ShapeDtypeStruct(dims, dtype)


def sync(*values):
    return lax.optimization_barrier(values)


def over_plane(held):
    return swap(held, "dp", 2), swap(held, "dp", 4)


def over_corner(x_part, y_part):
    return swap(y_part[:2], "dp", 2), swap(x_part[2:], "dp", 4)


def plain_pieces(heads, ffn):
    n_dp = lax.axis_size("dp")
    rows = D // n_dp
    whole = lax.all_gather(ffn, "dp", axis=1)
    parts = [whole[:, :, n * rows : (n + 1) * rows].reshape(4, D, D) for n in (0, 1)]
    final = whole[:, :, 2 * rows : 2 * rows + OUT // n_dp, :HL].reshape(4, OUT, HL)
    return [lax.all_gather(heads, "dp", axis=1, tiled=True)], [jnp.concatenate(parts, axis=1)], final


def scatter_plain(both):
    n_dp = lax.axis_size("dp")
    rows = both.shape[2]
    total = []
    for first in range(0, rows - FB + 1, FB):
        part = both[:, :, first : first + FB].reshape(4, D, D)
        total.append(lax.psum_scatter(part, "dp", scatter_dimension=1, tiled=True))
    if rows % FB == 0:
        return jnp.concatenate(total, axis=1)
    final = both[:, :, rows - 16 :, :256].reshape(4, OUT, 256)
    final = lax.psum_scatter(final, "dp", scatter_dimension=1, tiled=True)
    final = jnp.pad(final, ((0, 0), (0, 16 - OUT // n_dp), (0, 0)))
    sums = lax.psum(both[:, 0, rows - 16 :, 256:], "dp")
    return jnp.concatenate(total + [jnp.concatenate([final, sums], axis=2)], axis=1)


def added(pair, *index):
    return pair[0][index].astype(F32) + pair[1][index].astype(F32)


def by_plane(pair):
    return tuple(p.reshape((2, 2) + p.shape[1:]) for p in pair)


LOW, HIGH = slice(0, 2), slice(2, 4)


def plane_first(*pair):
    wide = by_plane(pair)
    return added(wide, slice(None), 1, LOW).astype(BF), added(wide, 1, slice(None), HIGH).astype(BF)


def plane_second(keep, got, x_got, y_got):
    wide = by_plane((keep, got))
    x_part = [added(wide, n, 0, LOW) + x_got[n].astype(F32) for n in range(2)]
    y_part = [added(wide, 0, n, HIGH) + y_got[n].astype(F32) for n in range(2)]
    return x_part[1].astype(BF), y_part[1].astype(BF), x_part[0], y_part[0]


def feature_row(scal, by_xor):
    lane = lax.broadcasted_iota(jnp.int32, (1, D), 1)
    if not by_xor:
        return lane
    part = jnp.zeros((1, D), jnp.int32)
    for n in range(1, PARTS):
        part = part + jnp.where(lane >= n * FB, 1, 0)
    return (((part & 3) * 2 + (part >> 2)) ^ scal[0]) * FB + lane - part * FB


def final_row(scal, by_xor):
    lane = lax.broadcasted_iota(jnp.int32, (1, OUT), 1)
    if not by_xor:
        return lane
    part = lane >> 4
    return (((part & 3) * 2 + (part >> 2)) ^ scal[0]) * 16 + (lane & 15)


def pick(scal, frow, n):
    first = (scal[1] ^ ((n & 1) * 2 + (n >> 1))) * HL
    rows = lax.broadcasted_iota(jnp.int32, (HL, D), 0) + first
    return jnp.where(rows == frow, 1.0, 0.0).astype(BF)


def spread(order_row):
    rows = lax.broadcasted_iota(jnp.int32, (TOK, order_row.shape[1]), 0)
    return jnp.where(rows == order_row, 1.0, 0.0).astype(BF)


def pack_in_body(scal, order_ref, x_ref, mask_ref, cot_ref, out_ref, kept_ref, cot_out_ref, order_out_ref, canon_ref):
    block = pl.program_id(0)

    @pl.when(block == 0)
    def _():
        start, seen = jnp.int32(0), jnp.int32(0)
        for c in range(4):
            start = jnp.where(scal[2 + c] == LONG, seen, start)
            seen = seen + scal[2 + c]
        order = jnp.broadcast_to(order_ref[...], (8, TOK))
        canon_ref[:, :LONG] = pltpu.roll(order, (TOK - start) & (TOK - 1), 1)[:, :LONG]
        lane = lax.broadcasted_iota(jnp.int32, (8, LONG), 1)
        canon_ref[:, LONG:] = jnp.where(lane < start, order[:, :LONG], order[:, LONG:])
        for n in range(4):
            first = pl.multiple_of((scal[1] ^ n) * ROWS, ROWS)
            order_out_ref[:, n * ROWS : (n + 1) * ROWS] = canon_ref[:, pl.ds(first, ROWS)]

    one_hot = spread(order_out_ref[0:1, pl.ds(pl.multiple_of(block * ROWS, ROWS), ROWS)])
    out_ref[...] = dot_nn(x_ref[...], one_hot).astype(BF)
    mask = mask_ref[...].astype(F32)

    @pl.when(block < 2)
    def _():
        kept_ref[...] = dot_nn(jnp.broadcast_to(mask, (16, TOK)).astype(BF), one_hot)[:8]

    @pl.when(block == 0)
    def _():
        cot = (jnp.transpose(cot_ref[...].astype(F32)) * mask).astype(BF)
        cot_out_ref[...] = jnp.transpose(dot_nn(cot, one_hot))


def pack_in(scal, order, inputs, mask_row, cotangent):
    return call(
        pack_in_body,
        (4,),
        [SMEM, full((1, TOK)), full((HL, TOK)), full((1, TOK)), full((TOK, OUT))],
        [
            pl.BlockSpec((HL, ROWS), lambda b: (0, b)),
            pl.BlockSpec((8, ROWS), lambda b: (0, jnp.minimum(b, 1))),
            full((ROWS, OUT)),
            full((8, TOK)),
        ],
        [shape((HL, TOK)), shape((8, KEYS), F32), shape((ROWS, OUT), F32), shape((8, TOK), jnp.int32)],
        [pltpu.VMEM((8, TOK), jnp.int32)],
        micros=6,
    )(scal, order, inputs, mask_row, cotangent)


def join(refs, rows, first=0, last=D):
    parts = [ref[0, :rows, first:last] for ref in refs]
    return parts[0] if len(parts) == 1 else jnp.concatenate(parts, axis=0)


def lanes_of_head(h, shift):
    lane = lax.broadcasted_iota(jnp.int32, (1, 256), 1)
    return (lane >= shift + h * HD) & (lane < shift + (h + 1) * HD)


def allowed_bias(scal, kept):
    pair = scal[1] & 1
    end, count = jnp.int32(0), jnp.int32(0)
    cuts = [jnp.int32(LONG), jnp.int32(LONG)]
    for c in range(4):
        short = scal[2 + c] != LONG
        end = end + jnp.where(short, scal[2 + c], 0)
        count = count + jnp.where(short, 1, 0)
        cuts = [jnp.where(short & (count == n + 1) & (scal[1] >= 2), end, cuts[n]) for n in range(2)]
    q_pos = lax.broadcasted_iota(jnp.int32, (ROWS, 1), 0) + pair * ROWS
    k_pos = lax.broadcasted_iota(jnp.int32, (1, KEYS), 1) + pair * ROWS
    k_pos = k_pos & (KEYS - 1)
    q_seg = jnp.where(q_pos >= cuts[0], 1, 0) + jnp.where(q_pos >= cuts[1], 1, 0)
    k_seg = jnp.where(k_pos >= cuts[0], 1, 0) + jnp.where(k_pos >= cuts[1], 1, 0)
    k_seg = jnp.where(kept > 0.5, k_seg, k_seg + 8)
    return jnp.where((q_seg == k_seg) | (q_pos == k_pos), 0.0, -1e30)


def attend_body(pieces, scal, kept_ref, x0, x2, x1, x3, extra_ref, *refs):
    weights = refs[:pieces]
    xr_ref, fvec_ref, kv_ref, q_ref, ctx_ref, ctx_f_ref, lse_ref, wo_ref, bias_ref = refs[pieces:]
    step = pl.program_id(0)
    rows = D // pieces

    @pl.when(step == 0)
    def _():
        frow = feature_row(scal, pieces > 1)
        upper = jnp.zeros((ROWS, D), F32)
        lower = jnp.zeros((ROWS, D), F32)
        fvec = jnp.zeros((16, D), F32)
        for n, (ref, crossed) in enumerate(((x0, False), (x2, False), (x1, True), (x3, True))):
            chosen = pick(scal, frow, n)
            near, away = ref[:, :ROWS], ref[:, ROWS:]
            if crossed:
                near, away = away, near
            upper = upper + dot_tn(near, chosen)
            lower = lower + dot_tn(away, chosen)
            fvec = fvec + dot_nn(extra_ref[n, :, 512 : 512 + HL], chosen)
        xr_ref[:ROWS] = upper.astype(BF)
        xr_ref[ROWS:] = lower.astype(BF)
        fvec_ref[...] = fvec[:8] + fvec[8:]
        bias_ref[...] = allowed_bias(scal, kept_ref[:1])

    weight = join(weights, rows)
    wo_ref[0] = weight[:, 512:]
    window = extra_ref[pl.ds(step, 1), :, 256:512][0].astype(F32)
    q_bias = window[0:1] + window[1:2]
    v_bias = window[2:3] + window[3:4]
    lane = lax.broadcasted_iota(jnp.int32, (1, 256), 1)
    packed = xr_ref[...]
    kv = dot_nn(packed, weight[:, :384])
    kv_bias = jnp.concatenate([jnp.zeros((1, 128), F32), v_bias], axis=1)
    kv = (kv + kv_bias).astype(BF)
    queries = (dot_nn(packed[:ROWS], weight[:, 384:640]) + q_bias).astype(BF)
    queries = jnp.where(lane < HL, queries, jnp.zeros_like(queries)) * jnp.asarray(0.125, BF)
    kv_ref[0] = kv
    q_ref[0] = queries
    keys, values = kv[:, :256], kv[:, 128:]
    context = jnp.zeros((ROWS, 256), F32)
    for h in range(3):
        own = jnp.where(lanes_of_head(h, 0), queries, jnp.zeros_like(queries))
        scores = dot_nt(own, keys) + bias_ref[...]
        top = jnp.max(scores, axis=1, keepdims=True)
        weight_h = jnp.exp(scores - top)
        total = jnp.sum(weight_h, axis=1, keepdims=True)
        part = dot_nn(weight_h.astype(BF), values) / total
        context = jnp.where(lanes_of_head(h, HD), part, context)
        lse_ref[0, h] = jnp.broadcast_to(top + jnp.log(total), (ROWS, 128))
    ctx_ref[0] = context.astype(BF)
    ctx_f_ref[0] = context


def attend(scal, kept, xs, extra, weights):
    pieces = len(weights)
    return call(
        functools.partial(attend_body, pieces),
        (4,),
        [SMEM, full((8, KEYS))]
        + [full((HL, KEYS))] * 4
        + [full((4, 16, D))]
        + [pl.BlockSpec((1,) + w.shape[1:], lambda j: (j, 0, 0)) for w in weights],
        [
            full((KEYS, D)),
            full((8, D)),
            pl.BlockSpec((1, KEYS, 384), lambda j: (j, 0, 0)),
            pl.BlockSpec((1, ROWS, 256), lambda j: (j, 0, 0)),
            pl.BlockSpec((1, ROWS, 256), lambda j: (j, 0, 0)),
            pl.BlockSpec((1, ROWS, 256), lambda j: (j, 0, 0)),
            pl.BlockSpec((1, 3, ROWS, 128), lambda j: (j, 0, 0, 0)),
            pl.BlockSpec((1, D, 256), lambda j: (j, 0, 0)),
        ],
        [
            shape((KEYS, D)),
            shape((8, D), F32),
            shape((4, KEYS, 384)),
            shape((4, ROWS, 256)),
            shape((4, ROWS, 256)),
            shape((4, ROWS, 256), F32),
            shape((4, 3, ROWS, 128), F32),
            shape((4, D, 256)),
        ],
        [pltpu.VMEM((ROWS, KEYS), F32)],
        micros=23,
    )(scal, kept, *xs, extra, *weights)


def over_rows(body, carried=()):
    def step(r, carried):
        return body(pl.ds(pl.multiple_of(r * CHUNK, CHUNK), CHUNK), carried)

    return lax.fori_loop(0, ROWS // CHUNK, step, carried)


def norm(residual, gain, shift):
    mean = jnp.mean(residual, axis=1, keepdims=True)
    spread_row = jnp.mean(residual * residual, axis=1, keepdims=True) - mean * mean
    scale = lax.rsqrt(spread_row + EPS)
    unit = (residual - mean) * scale
    return unit * gain + shift, unit, scale


def norm_back(grad, gain, unit, scale):
    scaled = grad * gain
    mean = jnp.mean(scaled, axis=1, keepdims=True)
    cross = jnp.mean(scaled * unit, axis=1, keepdims=True)
    return scale * (scaled - mean - unit * cross)


def inner_body(pieces, ctx_ref, wo_ref, xr_ref, fvec_ref, extra_ref, *refs):
    weights = refs[:pieces]
    normed_ref, unit_ref, scale_ref, low_ref, act_ref, slope_ref = refs[pieces:]
    step = pl.program_id(0)

    @pl.when(step == 0)
    def _():
        lane = lax.broadcasted_iota(jnp.int32, (1, 256), 1)
        total = xr_ref[...].astype(F32) + fvec_ref[0:1]
        for n in range(4):
            total = total + dot_nt(ctx_ref[n], wo_ref[n])
        normed_ref[...] = total

        def rows_of(rows, carried):
            normed, unit, scale = norm(normed_ref[rows, :], fvec_ref[2:3], fvec_ref[3:4])
            normed_ref[rows, :] = normed
            unit_ref[rows, :] = unit
            scale_ref[rows, :] = jnp.broadcast_to(scale, (CHUNK, 128))
            low_ref[rows, :] = normed.astype(BF)
            return carried

        over_rows(rows_of)

    window = extra_ref[pl.ds(step, 1), :, 256:512][0].astype(F32)
    bias = jnp.concatenate([window[4 + n : 5 + n] + window[7 + n : 8 + n] for n in range(3)], axis=1)
    pre = dot_nn(low_ref[...], join(weights, D // pieces)) + bias
    half = 0.5 + 0.5 * lax.erf(pre * math.sqrt(0.5))
    act_ref[0] = (pre * half).astype(BF)
    slope_ref[0] = half + pre * (jnp.exp(pre * pre * -0.5) * (1.0 / math.sqrt(2.0 * math.pi)))


def inner(context, wo, packed, fvec, extra, weights):
    pieces = len(weights)
    return call(
        functools.partial(inner_body, pieces),
        (4,),
        [full((4, ROWS, 256)), full((4, D, 256)), full((ROWS, D)), full((8, D)), full((4, 16, D))]
        + [pl.BlockSpec((1, D // pieces, D), lambda j: (j, 0, 0)) for w in weights],
        [
            full((ROWS, D)),
            full((ROWS, D)),
            full((ROWS, 128)),
            full((ROWS, D)),
            pl.BlockSpec((1, ROWS, D), lambda j: (j, 0, 0)),
            pl.BlockSpec((1, ROWS, D), lambda j: (j, 0, 0)),
        ],
        [
            shape((ROWS, D), F32),
            shape((ROWS, D), F32),
            shape((ROWS, 128), F32),
            shape((ROWS, D)),
            shape((4, ROWS, D)),
            shape((4, ROWS, D), F32),
        ],
    )(context, wo, packed, fvec, extra, *weights)


def outer_body(pieces, scal, act_ref, normed_ref, fvec_ref, fin_ref, cot_ref, *refs):
    weights = refs[:pieces]
    grad_ref, low_ref, vec_ref, fin_grad_ref, sums_ref, total_ref, unit_ref, scale_ref = refs[pieces:]
    step = pl.program_id(0)
    part = dot_nt(act_ref[0], join(weights, D // pieces))

    @pl.when(step == 0)
    def _():
        total_ref[...] = normed_ref[...] + fvec_ref[1:2] + part

    @pl.when(step > 0)
    def _():
        total_ref[...] += part

    @pl.when(step == 3)
    def _():
        gain = fvec_ref[4:5]

        def rows_of(rows, carried):
            normed, unit, scale = norm(total_ref[rows, :], gain, fvec_ref[5:6])
            unit_ref[rows, :] = unit
            scale_ref[rows, :] = jnp.broadcast_to(scale, (CHUNK, 128))
            low_ref[rows, :] = normed.astype(BF)
            return carried

        over_rows(rows_of)
        low = low_ref[...]
        frow = feature_row(scal, pieces > 1)
        final = jnp.zeros((OUT, D), F32)
        for n in range(4):
            final = final + dot_nn(fin_ref[n], pick(scal, frow, n))
        columns = lax.broadcasted_iota(jnp.int32, (OUT, OUT), 0)
        place = jnp.where(columns == final_row(scal, pieces > 1), 1.0, 0.0).astype(BF)
        final = dot_nn(place, final.astype(BF)).astype(BF)
        projected = dot_nt(low, final)
        length = lax.rsqrt(jnp.sum(projected * projected, axis=1, keepdims=True) + EPS)
        units = projected * length
        vec_ref[...] = jnp.transpose(units).astype(BF)
        grads = cot_ref[...]
        grads = length * (grads - units * jnp.sum(grads * units, axis=1, keepdims=True))
        grads = grads.astype(BF)
        fin_grad = dot_tn(place, dot_tn(grads, low).astype(BF)).astype(BF)
        for n in range(4):
            fin_grad_ref[n] = dot_nt(fin_grad, pick(scal, frow, n)).astype(BF)
        total_ref[...] = dot_nn(grads, final)

        def rows_back(rows, carried):
            grad, unit = total_ref[rows, :], unit_ref[rows, :]
            back = norm_back(grad, gain, unit, scale_ref[rows, :1])
            grad_ref[rows, :] = back
            low_ref[rows, :] = back.astype(BF)
            sums = (grad * unit, grad, back)
            return tuple(c + jnp.sum(t, axis=0, keepdims=True) for c, t in zip(carried, sums))

        sums = over_rows(rows_back, (jnp.zeros((1, D), F32),) * 3)
        for n in range(3):
            sums_ref[n : n + 1] = sums[n]
        sums_ref[3:] = jnp.zeros((5, D), F32)


def outer(scal, act, normed, fvec, final, cot, weights):
    pieces = len(weights)
    return call(
        functools.partial(outer_body, pieces),
        (4,),
        [SMEM]
        + [pl.BlockSpec((1, ROWS, D), lambda j: (j, 0, 0)), full((ROWS, D)), full((8, D))]
        + [full((4, OUT, HL)), full((ROWS, OUT))]
        + [pl.BlockSpec((1, D // pieces, D), lambda j: (j, 1, 0)) for w in weights],
        [
            full((ROWS, D)),
            full((ROWS, D)),
            full((OUT, ROWS)),
            full((4, OUT, HL)),
            full((8, D)),
        ],
        [
            shape((ROWS, D), F32),
            shape((ROWS, D)),
            shape((OUT, ROWS)),
            shape((4, OUT, HL)),
            shape((8, D), F32),
        ],
        [pltpu.VMEM((ROWS, D), F32), pltpu.VMEM((ROWS, D), F32), pltpu.VMEM((ROWS, 128), F32)],
    )(scal, act, normed, fvec, final, cot, *weights)


def split_out(total, keep_ref, send_ref, first=0):
    low = total.astype(BF).reshape(PARTS, FB, D)
    half = PARTS // 2
    keep_ref[:, 0, first : first + FB] = low[:half]
    send_ref[:, 0, first : first + FB] = low[half:]


def outer_back_body(pieces, low_ref, act_ref, slope_ref, normed_ref, *refs):
    weights = refs[:pieces]
    keep_ref, send_ref, pre_ref, bias_ref = refs[pieces:]
    low = low_ref[...]
    grad = dot_nn(low, join(weights, D // pieces)) * slope_ref[0]
    split_out(dot_tn(low, act_ref[0]), keep_ref, send_ref)
    grad_low = grad.astype(BF)
    pre_ref[0] = grad_low
    bias_ref[0] = jnp.broadcast_to(jnp.sum(grad, axis=0, keepdims=True), (8, D))
    split_out(dot_tn(normed_ref[...], grad_low), keep_ref, send_ref, FB)


def outer_back(low, act, slope, normed, weights):
    pieces = len(weights)
    half = PARTS // 2
    wide = pl.BlockSpec((half, 1, 2 * FB, D), lambda j: (0, j, 0, 0))
    block = pl.BlockSpec((1, ROWS, D), lambda j: (j, 0, 0))
    return call(
        functools.partial(outer_back_body, pieces),
        (4,),
        [full((ROWS, D)), block, block, full((ROWS, D))]
        + [pl.BlockSpec((1, D // pieces, D), lambda j: (j, 1, 0)) for w in weights],
        [wide, wide, block, pl.BlockSpec((1, 8, D), lambda j: (j, 0, 0))],
        [
            shape((half, 4, 2 * FB, D)),
            shape((half, 4, 2 * FB, D)),
            shape((4, ROWS, D)),
            shape((4, 8, D), F32),
        ],
        micros=15,
    )(low, act, slope, normed, *weights)


def inner_back_body(pieces, pre_ref, grad_ref, unit_ref, scale_ref, fvec_ref, sums_ref, *refs):
    weights = refs[:pieces]
    one_ref, one_low_ref, all_ref, total_ref = refs[pieces:]
    step = pl.program_id(0)
    part = dot_nt(pre_ref[0], join(weights, D // pieces))

    @pl.when(step == 0)
    def _():
        total_ref[...] = grad_ref[...] + part

    @pl.when(step > 0)
    def _():
        total_ref[...] += part

    @pl.when(step == 3)
    def _():
        def rows_back(rows, carried):
            grad, unit = total_ref[rows, :], unit_ref[rows, :]
            back = norm_back(grad, fvec_ref[2:3], unit, scale_ref[rows, :1])
            one_ref[rows, :] = back
            one_low_ref[rows, :] = back.astype(BF)
            sums = (grad * unit, grad, back)
            return tuple(c + jnp.sum(t, axis=0, keepdims=True) for c, t in zip(carried, sums))

        all_ref[0:3] = sums_ref[0:3]
        sums = over_rows(rows_back, (jnp.zeros((1, D), F32),) * 3)
        for n in range(3):
            all_ref[3 + n : 4 + n] = sums[n]
        all_ref[6:] = jnp.zeros((2, D), F32)


def inner_back(pre, grad, unit, scale, fvec, sums, weights):
    pieces = len(weights)
    at = lambda j: (j, 0, 0)
    return call(
        functools.partial(inner_back_body, pieces),
        (4,),
        [
            pl.BlockSpec((1, ROWS, D), at),
            full((ROWS, D)),
            full((ROWS, D)),
            full((ROWS, 128)),
            full((8, D)),
            full((8, D)),
        ]
        + [pl.BlockSpec((1, D // pieces, D), at) for w in weights],
        [full((ROWS, D)), full((ROWS, D)), full((8, D))],
        [shape((ROWS, D), F32), shape((ROWS, D)), shape((8, D), F32)],
        [pltpu.VMEM((ROWS, D), F32)],
        micros=9,
    )(pre, grad, unit, scale, fvec, sums, *weights)


def small_sums(scal, by_xor, n, q_sum, v_sum, all_ref, fin_ref, hid_ref):
    sums = dot_nt(all_ref[...].astype(BF), pick(scal, feature_row(scal, by_xor), n))
    sums = jnp.concatenate([sums, jnp.zeros((8, 64), F32)], axis=1)
    heads = jnp.concatenate([q_sum, v_sum, jnp.zeros((6, 256), F32)], axis=0)
    hidden = hid_ref[0, 0:1]
    hidden = [hidden[:, 256 * k : 256 * (k + 1)] for k in range(3)]
    hidden = jnp.concatenate(hidden + [jnp.zeros((13, 256), F32)], axis=0)
    wide = jnp.concatenate([jnp.concatenate([sums, heads], axis=0), hidden], axis=1).astype(BF)
    final = fin_ref[0].reshape(PARTS, OUT // PARTS, HL)
    final = jnp.concatenate([final, jnp.zeros((PARTS, OUT // PARTS, 64), BF)], axis=2)
    return jnp.concatenate([final, jnp.broadcast_to(wide[None], (PARTS, 16, 512))], axis=2)


def attend_back_body(pieces, first, count, scal, kept_ref, xr_ref, kv_ref, q_ref, ctx_ref, ctx_f_ref, lse_ref, one_ref, low_ref, all_ref, fin_ref, hid_ref, *refs):
    weights = refs[:pieces]
    refs = refs[pieces + (2 if first else 0) :]
    keep_ref, send_ref = refs[:2]
    bias_ref, total_ref = refs[-2:]
    step = pl.program_id(0)

    @pl.when(step == 0)
    def _():
        bias_ref[...] = allowed_bias(scal, kept_ref[:1])
        total_ref[:ROWS] = one_ref[:ROWS]
        total_ref[ROWS:] = one_ref[ROWS:] if first else jnp.zeros((ROWS, D), F32)

    weight = join(weights, D // pieces)
    low = low_ref[...]
    lane = lax.broadcasted_iota(jnp.int32, (1, 256), 1)
    grad_ctx = dot_nn(low, weight[:, 512:])
    grad_ctx = jnp.where(lane >= HD, grad_ctx, 0.0).astype(BF)
    keys, values = kv_ref[0, :, :256], kv_ref[0, :, 128:]
    queries = q_ref[0]
    products = grad_ctx.astype(F32) * ctx_f_ref[0]
    dq = jnp.zeros((ROWS, 256), F32)
    dk = jnp.zeros((KEYS, 256), F32)
    dv = jnp.zeros((KEYS, 256), F32)
    zero = jnp.zeros_like(queries)
    for h in range(3):
        own = jnp.where(lanes_of_head(h, 0), queries, zero)
        own_grad = jnp.where(lanes_of_head(h, HD), grad_ctx, zero)
        row_dot = jnp.sum(jnp.where(lanes_of_head(h, HD), products, 0.0), axis=1, keepdims=True)
        scores = dot_nt(own, keys) + bias_ref[...]
        prob = jnp.exp(scores - lse_ref[0, h][:, :1])
        dv = dv + dot_tn(prob.astype(BF), own_grad)
        grad_scores = (prob * (dot_nt(own_grad, values) - row_dot)).astype(BF)
        dq = jnp.where(lanes_of_head(h, 0), dot_nn(grad_scores, keys), dq)
        dk = dk + dot_tn(grad_scores, own)
    dq = dq * 0.125
    gap = jnp.zeros((KEYS, 128), F32)
    dkv = jnp.concatenate([dk, gap], axis=1) + jnp.concatenate([gap, dv], axis=1)
    q_sum = jnp.sum(dq, axis=0, keepdims=True)
    v_sum = jnp.sum(dv, axis=0, keepdims=True)
    dkv = dkv.astype(BF)
    dq = dq.astype(BF)
    packed = xr_ref[...]
    low_kv = dot_tn(packed, dkv)
    from_q = dot_tn(packed[:ROWS], dq)
    from_o = dot_tn(low, ctx_ref[0])
    gap = jnp.zeros((D, 128), F32)
    from_qo = jnp.concatenate([from_q, gap], axis=1) + jnp.concatenate([gap, from_o], axis=1)
    split_out(jnp.concatenate([low_kv, from_qo], axis=1), keep_ref, send_ref)
    extra = small_sums(scal, pieces > 1, first + step, q_sum, v_sum, all_ref, fin_ref, hid_ref)
    keep_ref[:, 0, FB:] = extra[: PARTS // 2]
    send_ref[:, 0, FB:] = extra[PARTS // 2 :]
    total_ref[...] += dot_nt(dkv, weight[:, :384])
    total_ref[:ROWS] += dot_nt(dq, weight[:, 384:640])

    @pl.when(step == count - 1)
    def _():
        if first + count < 4:
            refs[2][...] = total_ref[...]
            return
        x0_ref, x2_ref, x1_ref, x3_ref = refs[2:6]
        grads = total_ref[...].astype(BF)
        frow = feature_row(scal, pieces > 1)
        x0_ref[...] = dot_nt(pick(scal, frow, 0), grads)
        x2_ref[...] = dot_nt(pick(scal, frow, 1), grads)
        for n, ref in ((2, x1_ref), (3, x3_ref)):
            part = dot_nt(pick(scal, frow, n), grads).astype(BF)
            ref[:, :ROWS] = part[:, ROWS:]
            ref[:, ROWS:] = part[:, :ROWS]


def attend_back(scal, kept, packed, kv, queries, context, context_f, lse, one, low, small, weights, first, count, held):
    pieces = len(weights)
    half = PARTS // 2
    at = lambda j: (j + first, 0, 0)
    wide = pl.BlockSpec((half, 1, FB + 16, D), lambda j: (0, j + first, 0, 0))
    n_in = 13 + pieces
    last = first + count == 4
    return call(
        functools.partial(attend_back_body, pieces, first, count),
        (count,),
        [
            SMEM,
            full((8, KEYS)),
            full((KEYS, D)),
            pl.BlockSpec((1, KEYS, 384), at),
            pl.BlockSpec((1, ROWS, 256), at),
            pl.BlockSpec((1, ROWS, 256), at),
            pl.BlockSpec((1, ROWS, 256), at),
            pl.BlockSpec((1, 3, ROWS, 128), lambda j: (j + first, 0, 0, 0)),
            full(one.shape),
            full((ROWS, D)),
            full((8, D)),
            pl.BlockSpec((1, OUT, HL), at),
            pl.BlockSpec((1, 8, D), at),
        ]
        + [pl.BlockSpec((1,) + w.shape[1:], at) for w in weights]
        + [pl.BlockSpec(memory_space=pl.ANY)] * len(held),
        [wide, wide] + ([full((HL, KEYS))] * 4 if last else [full((KEYS, D))]),
        [shape((half, 4, FB + 16, D)), shape((half, 4, FB + 16, D))]
        + ([shape((HL, KEYS), F32)] * 2 + [shape((HL, KEYS))] * 2 if last else [shape((KEYS, D), F32)]),
        [pltpu.VMEM((ROWS, KEYS), F32), pltpu.VMEM((KEYS, D), F32)],
        micros=9 * count,
        aliases={n_in + n: n for n in range(len(held))},
    )(scal, kept, packed, kv, queries, context, context_f, lse, one, low, *small, *weights, *held)


def pack_vec_body(order_ref, mask_ref, vec_ref, out_ref, total_ref):
    step = pl.program_id(0)
    part = dot_nt(vec_ref[0], spread(order_ref[:1]))

    @pl.when(step == 0)
    def _():
        total_ref[...] = part

    @pl.when(step > 0)
    def _():
        total_ref[...] += part

    @pl.when(step == 3)
    def _():
        out_ref[...] = jnp.transpose(total_ref[...] * mask_ref[...].astype(F32))


def pack_vec(order, mask_row, vecs):
    return call(
        pack_vec_body,
        (4,),
        [
            pl.BlockSpec((8, ROWS), lambda b: (0, b)),
            full((1, TOK)),
            pl.BlockSpec((1, OUT, ROWS), lambda b: (b, 0, 0)),
        ],
        full((TOK, OUT)),
        shape((TOK, OUT), F32),
        [pltpu.VMEM((OUT, TOK), F32)],
        micros=5,
    )(order, mask_row, vecs)


def pack_x_body(order_ref, x0_ref, x1_ref, far_ref, out_ref):
    step = pl.program_id(0)
    near = (x0_ref[...] + x1_ref[...].astype(F32)).astype(BF)
    part = dot_nt(jnp.where(step < 2, near, far_ref[...]), spread(order_ref[:1]))

    @pl.when(step == 0)
    def _():
        out_ref[...] = part

    @pl.when(step > 0)
    def _():
        out_ref[...] += part


def pack_x(order, *parts):
    return call(
        pack_x_body,
        (4,),
        [pl.BlockSpec((8, ROWS), lambda b: (0, b))]
        + [pl.BlockSpec((HL, ROWS), lambda b: (0, b & 1)) for _ in parts],
        full((HL, TOK)),
        shape((HL, TOK), F32),
        micros=5,
    )(order, *parts)


def halves(vector):
    high = vector.astype(BF)
    return high, (vector - high.astype(F32)).astype(BF)


def pack_weights_body(k_ref, v_ref, q_ref, o_ref, in_ref, out_ref, fin_ref, qb, vb, inb, ob, outb, g1, s1, g2, s2, heads_ref, ffn_ref):
    turned = lambda ref: jnp.transpose(ref[...].astype(F32)).astype(BF)
    heads_ref[:FB] = jnp.concatenate([k_ref[...], v_ref[...], q_ref[...], turned(o_ref)], axis=1)
    ffn_ref[:FB] = in_ref[...]
    ffn_ref[FB : 2 * FB] = out_ref[...]
    qb, vb, inb, ob, outb, g1, s1, g2, s2 = (ref[...].reshape(1, ref.shape[0]) for ref in (qb, vb, inb, ob, outb, g1, s1, g2, s2))
    gap = jnp.zeros((1, 64), F32)
    window = []
    for value in (jnp.concatenate([qb, gap], axis=1), jnp.concatenate([gap, vb], axis=1)):
        window += list(halves(value))
    hidden = [halves(inb[:, n * 256 : (n + 1) * 256]) for n in range(3)]
    window += [high for high, _ in hidden] + [low for _, low in hidden]
    window = jnp.concatenate(window + [jnp.zeros((6, 256), BF)], axis=0)
    features = [halves(jnp.concatenate([value, gap], axis=1)) for value in (ob, outb, g1, s1, g2, s2)]
    pad = [jnp.zeros((2, 256), BF)]
    features = jnp.concatenate([high for high, _ in features] + pad + [low for _, low in features] + pad, axis=0)
    final = jnp.concatenate([fin_ref[...], jnp.zeros((16, 64), BF)], axis=1)
    extra = jnp.concatenate([final, window, features], axis=1)
    heads_ref[FB:] = extra


def pack_weights(weights, vectors):
    return call(
        pack_weights_body,
        (1,),
        [full(w.shape) for w in weights] + [full(v.shape) for v in vectors],
        [full((FB + 16, D)), full((2 * FB, D))],
        [shape((FB + 16, D)), shape((2 * FB, D))],
        micros=3,
    )(*weights, *vectors)


def ffn_out_body(a_ref, b_ref, out_ref, in_ref):
    total = a_ref[...] + b_ref[...].astype(F32)
    out_ref[...] = total[:FB]
    in_ref[...] = total[FB:]


def ffn_out(a, b):
    both = [full((FB, D))] * 2
    return call(ffn_out_body, (1,), [full(a.shape), full(b.shape)], both, [shape((FB, D), F32)] * 2, micros=3)(a, b)


def heads_out_body(a_ref, b_ref, q_ref, k_ref, v_ref, o_ref, fin_ref, inb, qb, vb, ob, outb, g1, s1, g2, s2):
    total = a_ref[...] + b_ref[...].astype(F32)
    k_ref[...] = total[:FB, :HL]
    v_ref[...] = total[:FB, HL:384]
    q_ref[...] = total[:FB, 384:576]
    o_ref[...] = jnp.transpose(total[:FB, 576:])
    tile = total[FB:]
    fin_ref[...] = tile[:, :HL]
    qb[...] = tile[8:9, 256 : 256 + HL].reshape(HL)
    vb[...] = tile[9:10, 320:512].reshape(HL)
    for n, ref in ((5, ob), (2, outb), (3, g1), (4, s1), (0, g2), (1, s2)):
        ref[...] = tile[n : n + 1, 256 : 256 + HL].reshape(HL)
    inb[...] = jnp.concatenate([tile[n : n + 1, 512:] for n in range(3)], axis=1).reshape(D)


def heads_out(a, b):
    dims = [(FB, HL)] * 3 + [(HL, FB), (16, HL), (D,)] + [(HL,)] * 8
    return call(
        heads_out_body, (1,), [full(a.shape), full(b.shape)], [full(d) for d in dims], [shape(d, F32) for d in dims], micros=3
    )(a, b)


def hi_lo(vector):
    high = vector.astype(BF)
    high = lax.optimization_barrier(high)
    return high, (vector - high.astype(F32)).astype(BF)


def extra_rows(final_t, q_bias, v_bias, inner_bias, features):
    q_hi, q_lo = hi_lo(jnp.pad(q_bias, (0, 64)))
    v_hi, v_lo = hi_lo(jnp.pad(v_bias, (64, 0)))
    in_hi, in_lo = hi_lo(inner_bias.reshape(3, 256))
    window = jnp.concatenate([jnp.stack([q_hi, q_lo, v_hi, v_lo]), in_hi, in_lo], axis=0)
    window = jnp.pad(window, ((0, 6), (0, 0)))
    f_hi, f_lo = hi_lo(jnp.pad(jnp.stack(features), ((0, 2), (0, 64))))
    final_t = jnp.pad(final_t, ((0, 16 - final_t.shape[0]), (0, 64)))
    return jnp.concatenate([final_t, window, jnp.concatenate([f_hi, f_lo], axis=0)], axis=1)


def local(
    inputs,
    token_order,
    lengths,
    token_mask,
    cotangent,
    query_weight,
    key_weight,
    value_weight,
    output_weight,
    inner_weight,
    outer_weight,
    final_weight,
    query_bias,
    value_bias,
    output_bias,
    inner_bias,
    outer_bias,
    first_gain,
    first_shift,
    second_gain,
    second_shift,
):
    m, i = lax.axis_index("mp"), lax.axis_index("dp")
    n_dp = lax.axis_size("dp")
    rows = D // n_dp
    by_xor = n_dp == 8
    scal = jnp.concatenate([jnp.stack([i, m]).astype(jnp.int32), lengths[0]])
    features_of = [output_bias, outer_bias, first_gain, first_shift, second_gain, second_shift]

    if by_xor:
        heads_own, ffn_own = pack_weights(
            [key_weight, value_weight, query_weight, output_weight, inner_weight, outer_weight.T, final_weight.T],
            [query_bias, value_bias, inner_bias] + features_of,
        )
    else:
        extra = extra_rows(final_weight.T, query_bias, value_bias, inner_bias, features_of)
        heads_own = jnp.concatenate([key_weight, value_weight, query_weight, output_weight.T], axis=1)
        heads_own = jnp.concatenate([heads_own, extra], axis=0)
        ffn_own = jnp.concatenate([inner_weight, outer_weight.T], axis=0)

    mask_row = token_mask.reshape(1, TOK)
    heads_own, ffn_own, inputs = sync(heads_own, ffn_own, inputs)
    heads_got = [swap(heads_own, "mp", bit) for bit in (2, 1, 3)]
    features, kept, cot, order = pack_in(scal, token_order, inputs, mask_row, cotangent)
    near, away = features[:, :KEYS], features[:, KEYS:]
    ffn_own, near, away = sync(ffn_own, near, away)
    ffn_got = [swap(ffn_own, "mp", bit) for bit in (2, 1, 3)]
    heads_got = sync(*heads_got)
    heads = jnp.stack([h[:rows] for h in (heads_own, *heads_got)])
    extras = jnp.stack([h[rows:] for h in (heads_own, *heads_got)])
    if by_xor:
        heads, near, away = sync(heads, near, away)
        head_x, head_y = over_plane(heads)
        head_x, head_y = sync(head_x, head_y)
        far_a, far_b = sync(*over_corner(head_x, head_y))
        far_a, far_b, ffn_got, near, away, heads, head_x, head_y = sync(
            far_a, far_b, ffn_got, near, away, heads, head_x, head_y
        )
        x1, x2 = swap(near, "mp", 1), swap(away, "mp", 2)
        ffn = jnp.stack([ffn_own, *ffn_got])
        ffn = jnp.concatenate([ffn, extras], axis=1)
        ffn_x, ffn_y = over_plane(ffn)
        far = jnp.concatenate([far_a, far_b], axis=0)
        head_pieces = [heads, head_x, head_y, far]
        head_pieces += [swap(p, "dp", 1) for p in head_pieces]
        x1, x2, *head_pieces = sync(x1, x2, *head_pieces)
        x3 = swap(x2, "mp", 1)
        x3, ffn_x, ffn_y = sync(x3, ffn_x, ffn_y)
        far_a, far_b = over_corner(ffn_x, ffn_y)
        ffn_pieces = [swap(p, "dp", 1) for p in (ffn, ffn_x, ffn_y)]
    else:
        ffn = jnp.concatenate([jnp.stack([ffn_own, *ffn_got]), extras], axis=1)
        x1, x2 = swap(near, "mp", 1), swap(away, "mp", 2)
        x3 = swap(x2, "mp", 1)
        head_pieces, ffn_pieces, final = plain_pieces(heads, ffn)

    packed, fvec, kv, queries, context, context_f, lse, wo = attend(
        scal, kept, (near, x2, x1, x3), extras, head_pieces
    )
    if by_xor:
        context, far_a, far_b, *ffn_pieces = sync(context, far_a, far_b, *ffn_pieces)
        far = jnp.concatenate([far_a, far_b], axis=0)
        ffn_pieces = [ffn, ffn_x, ffn_y, far] + ffn_pieces + [swap(far, "dp", 1)]
        final = jnp.concatenate([p[:, 2 * FB :, :HL] for p in ffn_pieces], axis=1)
    normed, unit, scale, normed_low, act, slope = inner(context, wo, packed, fvec, extras, ffn_pieces)
    grad_two, two_low, vec, fin_grad, sums = outer(scal, act, normed, fvec, final, cot, ffn_pieces)
    vec_got = swap(vec, "mp", 1)
    ffn_keep, ffn_send, pre, hid_sums = outer_back(two_low, act, slope, normed_low, ffn_pieces)
    vec_got, ffn_send, pre = sync(vec_got, ffn_send, pre)
    vec_low = jnp.stack([vec, vec_got])
    vec_high = swap(vec_low, "mp", 2)
    saved = (kept, packed, kv, queries, context, context_f, lse)

    def heads_back(one, low, first, count, held):
        small = (all_sums, fin_grad, hid_sums)
        return attend_back(scal, *saved, one, low, small, head_pieces, first, count, held)

    if by_xor:
        ffn_got = swap(ffn_send, "dp", 1)
        grad_one, one_low, all_sums = inner_back(pre, grad_two, unit, scale, fvec, sums, ffn_pieces)
        ffn_got, one_low = sync(ffn_got, one_low)
        pair = (ffn_keep, ffn_got)
        x_send, y_send = plane_first(*pair)
        one_low, x_send, y_send = sync(one_low, x_send, y_send)
        x_got, y_got = swap(x_send, "dp", 2), swap(y_send, "dp", 4)
        head_keep, head_send, dx0, dx2, dx1, dx3 = heads_back(grad_one, one_low, 0, 4, ())
        dx1, dx3, head_send, x_got, y_got, vec_high = sync(dx1, dx3, head_send, x_got, y_got, vec_high)

        dx3_got = swap(dx3, "mp", 1)
        head_got = swap(head_send, "dp", 1)
        to_y, to_x, upper, lower = plane_second(*pair, x_got, y_got)
        from_y, from_x = swap(to_y, "dp", 4), swap(to_x, "dp", 2)
        vecs = jnp.concatenate([vec_low, vec_high], axis=0)
        dx3_got, head_got, dx1, vecs = sync(dx3_got, head_got, dx1, vecs)
        to_far = (dx2 + dx3_got.astype(F32)).astype(BF)
        far, dx1_got = swap(to_far, "mp", 2), swap(dx1, "mp", 1)
        pair = (head_keep, head_got)
        x_send, y_send = plane_first(*pair)
        x_send, y_send, vecs = sync(x_send, y_send, vecs)
        x_got, y_got = swap(x_send, "dp", 2), swap(y_send, "dp", 4)
        vectors = pack_vec(order, mask_row, vecs)
        from_y, from_x, vectors = sync(from_y, from_x, vectors)
        upper = upper + from_y.astype(F32)
        lower = (lower + from_x.astype(F32)).astype(BF)
        lower_got = swap(lower, "mp", 1)
        x_got, y_got, dx1_got, far = sync(x_got, y_got, dx1_got, far)
        to_y, to_x, h_upper, h_lower = plane_second(*pair, x_got, y_got)
        to_y, to_x, dx1_got = sync(to_y, to_x, dx1_got)
        from_y, from_x = swap(to_y, "dp", 4), swap(to_x, "dp", 2)
        inputs_grad = pack_x(order, dx0, dx1_got, far)
        from_y, from_x, lower_got, inputs_grad = sync(from_y, from_x, lower_got, inputs_grad)
        h_upper = h_upper + from_y.astype(F32)
        h_lower = (h_lower + from_x.astype(F32)).astype(BF)
        h_lower_got = swap(h_lower, "mp", 1)
        upper = upper + lower_got.astype(F32)
        last = swap(upper[1].astype(BF), "mp", 2)
        h_lower_got, last = sync(h_lower_got, last)
        h_upper = h_upper + h_lower_got.astype(F32)
        h_last = swap(h_upper[1].astype(BF), "mp", 2)
        g_out, g_in = ffn_out(upper[0], last)
        g_q, g_k, g_v, g_o, g_fin, g_inb, g_qb, g_vb, g_ob, g_outb, g_g1, g_s1, g_g2, g_s2 = heads_out(h_upper[0], h_last)
        g_out, g_fin = g_out.T, g_fin.T
    else:
        grad_one, one_low, all_sums = inner_back(pre, grad_two, unit, scale, fvec, sums, ffn_pieces)
        head_keep, head_send, dx0, dx2, dx1, dx3 = heads_back(grad_one, one_low, 0, 4, ())
        far = swap((dx2 + swap(dx3, "mp", 1).astype(F32)).astype(BF), "mp", 2)
        inputs_grad = pack_x(order, dx0, swap(dx1, "mp", 1), far)
        vectors = pack_vec(order, mask_row, jnp.concatenate([vec_low, vec_high], axis=0))
        ends = []
        for keep, send in ((ffn_keep, ffn_send), (head_keep, head_send)):
            total = scatter_plain(jnp.concatenate([keep, send], axis=0).transpose(1, 0, 2, 3).astype(F32))
            upper = total[:2] + swap(total[2:].astype(BF), "mp", 1).astype(F32)
            ends.append(upper[0] + swap(upper[1].astype(BF), "mp", 2).astype(F32))
        ffn_sum, head_sum = ends
        tile = head_sum[rows:]
        g_out, g_in, g_fin = ffn_sum[:rows].T, ffn_sum[rows:], tile[: OUT // n_dp, :HL].T
        g_g2, g_s2, g_outb, g_g1, g_s1, g_ob = (tile[n, 256 : 256 + HL] for n in range(6))
        g_inb = tile[:3, 512:].reshape(D)
        g_k, g_v, g_q, g_o = head_sum[:rows, :HL], head_sum[:rows, HL:384], head_sum[:rows, 384:576], head_sum[:rows, 576:].T
        g_qb, g_vb = tile[8, 256 : 256 + HL], tile[9, 320:512]
    return (
        vectors,
        inputs_grad,
        g_q,
        g_k,
        g_v,
        g_o,
        g_in,
        g_out,
        g_fin,
        g_qb,
        g_vb,
        g_ob,
        g_inb,
        g_outb,
        g_g1,
        g_s1,
        g_g2,
        g_s2,
    )


def solution(mesh):
    return jax.shard_map(
        local,
        mesh=mesh,
        in_specs=(
            P("mp", "dp"),
            P("dp", None),
            P("dp", None),
            P("dp"),
            P("dp", None),
            P("dp", "mp"),
            P("dp", "mp"),
            P("dp", "mp"),
            P("mp", "dp"),
            P("dp", "mp"),
            P("mp", "dp"),
            P("mp", "dp"),
            P("mp"),
            P("mp"),
            P("mp"),
            P("mp"),
            P("mp"),
            P("mp"),
            P("mp"),
            P("mp"),
            P("mp"),
        ),
        out_specs=(
            P("dp", None),
            P("mp", "dp"),
            P("dp", "mp"),
            P("dp", "mp"),
            P("dp", "mp"),
            P("mp", "dp"),
            P("dp", "mp"),
            P("mp", "dp"),
            P("mp", "dp"),
            P("mp"),
            P("mp"),
            P("mp"),
            P("mp"),
            P("mp"),
            P("mp"),
            P("mp"),
            P("mp"),
            P("mp"),
        ),
        check_vma=False,
    )
```

```python
import functools
import math

import jax
import jax.numpy as jnp
from jax import lax
from jax.experimental import pallas as pl
from jax.experimental.pallas import tpu as pltpu
from jax.sharding import PartitionSpec as P

D = 768
HD = 64
HL = 192
FB = 96
PARTS = 8
OUT = 128
TOK = 2048
ROWS = 512
KEYS = 1024
LONG = 1024
CHUNK = 64
EPS = 1e-06
F32 = jnp.float32
BF = jnp.bfloat16


def dot_nn(a, b):
    return lax.dot_general(a, b, (((1,), (0,)), ((), ())), preferred_element_type=F32)


def dot_nt(a, b):
    return lax.dot_general(a, b, (((1,), (1,)), ((), ())), preferred_element_type=F32)


def dot_tn(a, b):
    return lax.dot_general(a, b, (((0,), (0,)), ((), ())), preferred_element_type=F32)


def swap(array, axis, bit):
    size = lax.axis_size(axis)
    return lax.ppermute(array, axis, [(a, a ^ bit) for a in range(size)])


def full(shape):
    zeros = (0,) * len(shape)
    return pl.BlockSpec(shape, lambda *_: zeros)


SMEM = pl.BlockSpec(memory_space=pltpu.SMEM)


def call(body, grid, in_specs, out_specs, out_shape, scratch=(), micros=10, aliases=None, limit=16):
    return pl.pallas_call(
        body,
        grid=grid,
        in_specs=in_specs,
        out_specs=out_specs,
        out_shape=out_shape,
        scratch_shapes=list(scratch),
        input_output_aliases=aliases or {},
        compiler_params=pltpu.CompilerParams(
            dimension_semantics=("arbitrary",) * len(grid), vmem_limit_bytes=limit * 1024 * 1024
        ),
        cost_estimate=pl.CostEstimate(flops=micros * 10**9, transcendentals=0, bytes_accessed=micros * 3 * 10**6),
    )


def shape(dims, dtype=BF):
    return jax.ShapeDtypeStruct(dims, dtype)


def sync(*values):
    return lax.optimization_barrier(values)


def over_plane(held):
    return swap(held, "dp", 2), swap(held, "dp", 4)


def over_corner(x_part, y_part):
    return swap(y_part[:2], "dp", 2), swap(x_part[2:], "dp", 4)


def plain_pieces(heads, ffn):
    n_dp = lax.axis_size("dp")
    rows = D // n_dp
    whole = lax.all_gather(ffn, "dp", axis=1)
    parts = [whole[:, :, n * rows : (n + 1) * rows].reshape(4, D, D) for n in (0, 1)]
    final = whole[:, :, 2 * rows : 2 * rows + OUT // n_dp, :HL].reshape(4, OUT, HL)
    return [lax.all_gather(heads, "dp", axis=1, tiled=True)], [jnp.concatenate(parts, axis=1)], final


def scatter_plain(both):
    n_dp = lax.axis_size("dp")
    rows = both.shape[2]
    total = []
    for first in range(0, rows - FB + 1, FB):
        part = both[:, :, first : first + FB].reshape(4, D, D)
        total.append(lax.psum_scatter(part, "dp", scatter_dimension=1, tiled=True))
    if rows % FB == 0:
        return jnp.concatenate(total, axis=1)
    final = both[:, :, rows - 16 :, :256].reshape(4, OUT, 256)
    final = lax.psum_scatter(final, "dp", scatter_dimension=1, tiled=True)
    final = jnp.pad(final, ((0, 0), (0, 16 - OUT // n_dp), (0, 0)))
    sums = lax.psum(both[:, 0, rows - 16 :, 256:], "dp")
    return jnp.concatenate(total + [jnp.concatenate([final, sums], axis=2)], axis=1)


def added(pair, *index):
    return pair[0][index].astype(F32) + pair[1][index].astype(F32)


def by_plane(pair):
    return tuple(p.reshape((2, 2) + p.shape[1:]) for p in pair)


LOW, HIGH = slice(0, 2), slice(2, 4)


def plane_first(*pair):
    wide = by_plane(pair)
    return added(wide, slice(None), 1, LOW).astype(BF), added(wide, 1, slice(None), HIGH).astype(BF)


def plane_second(keep, got, x_got, y_got):
    wide = by_plane((keep, got))
    x_part = [added(wide, n, 0, LOW) + x_got[n].astype(F32) for n in range(2)]
    y_part = [added(wide, 0, n, HIGH) + y_got[n].astype(F32) for n in range(2)]
    return x_part[1].astype(BF), y_part[1].astype(BF), x_part[0], y_part[0]


def feature_row(scal, by_xor):
    lane = lax.broadcasted_iota(jnp.int32, (1, D), 1)
    if not by_xor:
        return lane
    part = jnp.zeros((1, D), jnp.int32)
    for n in range(1, PARTS):
        part = part + jnp.where(lane >= n * FB, 1, 0)
    return (((part & 3) * 2 + (part >> 2)) ^ scal[0]) * FB + lane - part * FB


def final_row(scal, by_xor):
    lane = lax.broadcasted_iota(jnp.int32, (1, OUT), 1)
    if not by_xor:
        return lane
    part = lane >> 4
    return (((part & 3) * 2 + (part >> 2)) ^ scal[0]) * 16 + (lane & 15)


def pick(scal, frow, n):
    first = (scal[1] ^ ((n & 1) * 2 + (n >> 1))) * HL
    rows = lax.broadcasted_iota(jnp.int32, (HL, D), 0) + first
    return jnp.where(rows == frow, 1.0, 0.0).astype(BF)


def spread(order_row):
    rows = lax.broadcasted_iota(jnp.int32, (TOK, order_row.shape[1]), 0)
    return jnp.where(rows == order_row, 1.0, 0.0).astype(BF)


def pack_in_body(scal, order_ref, x_ref, mask_ref, cot_ref, out_ref, kept_ref, cot_out_ref, order_out_ref, canon_ref):
    block = pl.program_id(0)

    @pl.when(block == 0)
    def _():
        start, seen = jnp.int32(0), jnp.int32(0)
        for c in range(4):
            start = jnp.where(scal[2 + c] == LONG, seen, start)
            seen = seen + scal[2 + c]
        order = jnp.broadcast_to(order_ref[...], (8, TOK))
        canon_ref[:, :LONG] = pltpu.roll(order, (TOK - start) & (TOK - 1), 1)[:, :LONG]
        lane = lax.broadcasted_iota(jnp.int32, (8, LONG), 1)
        canon_ref[:, LONG:] = jnp.where(lane < start, order[:, :LONG], order[:, LONG:])
        for n in range(4):
            first = pl.multiple_of((scal[1] ^ n) * ROWS, ROWS)
            order_out_ref[:, n * ROWS : (n + 1) * ROWS] = canon_ref[:, pl.ds(first, ROWS)]

    one_hot = spread(order_out_ref[0:1, pl.ds(pl.multiple_of(block * ROWS, ROWS), ROWS)])
    out_ref[...] = dot_nn(x_ref[...], one_hot).astype(BF)
    mask = mask_ref[...].astype(F32)

    @pl.when(block < 2)
    def _():
        kept_ref[...] = dot_nn(jnp.broadcast_to(mask, (16, TOK)).astype(BF), one_hot)[:8]

    @pl.when(block == 0)
    def _():
        cot = (jnp.transpose(cot_ref[...].astype(F32)) * mask).astype(BF)
        cot_out_ref[...] = jnp.transpose(dot_nn(cot, one_hot))


def pack_in(scal, order, inputs, mask_row, cotangent):
    return call(
        pack_in_body,
        (4,),
        [SMEM, full((1, TOK)), full((HL, TOK)), full((1, TOK)), full((TOK, OUT))],
        [
            pl.BlockSpec((HL, ROWS), lambda b: (0, b)),
            pl.BlockSpec((8, ROWS), lambda b: (0, jnp.minimum(b, 1))),
            full((ROWS, OUT)),
            full((8, TOK)),
        ],
        [shape((HL, TOK)), shape((8, KEYS), F32), shape((ROWS, OUT), F32), shape((8, TOK), jnp.int32)],
        [pltpu.VMEM((8, TOK), jnp.int32)],
        micros=6,
    )(scal, order, inputs, mask_row, cotangent)


def join(refs, rows, first=0, last=D):
    parts = [ref[0, :rows, first:last] for ref in refs]
    return parts[0] if len(parts) == 1 else jnp.concatenate(parts, axis=0)


def lanes_of_head(h, shift):
    lane = lax.broadcasted_iota(jnp.int32, (1, 256), 1)
    return (lane >= shift + h * HD) & (lane < shift + (h + 1) * HD)


def allowed_bias(scal, kept):
    pair = scal[1] & 1
    end, count = jnp.int32(0), jnp.int32(0)
    cuts = [jnp.int32(LONG), jnp.int32(LONG)]
    for c in range(4):
        short = scal[2 + c] != LONG
        end = end + jnp.where(short, scal[2 + c], 0)
        count = count + jnp.where(short, 1, 0)
        cuts = [jnp.where(short & (count == n + 1) & (scal[1] >= 2), end, cuts[n]) for n in range(2)]
    q_pos = lax.broadcasted_iota(jnp.int32, (ROWS, 1), 0) + pair * ROWS
    k_pos = lax.broadcasted_iota(jnp.int32, (1, KEYS), 1) + pair * ROWS
    k_pos = k_pos & (KEYS - 1)
    q_seg = jnp.where(q_pos >= cuts[0], 1, 0) + jnp.where(q_pos >= cuts[1], 1, 0)
    k_seg = jnp.where(k_pos >= cuts[0], 1, 0) + jnp.where(k_pos >= cuts[1], 1, 0)
    k_seg = jnp.where(kept > 0.5, k_seg, k_seg + 8)
    return jnp.where((q_seg == k_seg) | (q_pos == k_pos), 0.0, -1e30)


def attend_body(pieces, scal, kept_ref, x0, x2, x1, x3, extra_ref, *refs):
    weights = refs[:pieces]
    xr_ref, fvec_ref, kv_ref, q_ref, ctx_ref, ctx_f_ref, wo_ref, bias_ref = refs[pieces:]
    step = pl.program_id(0)
    rows = D // pieces

    @pl.when(step == 0)
    def _():
        frow = feature_row(scal, pieces > 1)
        upper = jnp.zeros((ROWS, D), F32)
        lower = jnp.zeros((ROWS, D), F32)
        fvec = jnp.zeros((16, D), F32)
        for n, (ref, crossed) in enumerate(((x0, False), (x2, False), (x1, True), (x3, True))):
            chosen = pick(scal, frow, n)
            near, away = ref[:, :ROWS], ref[:, ROWS:]
            if crossed:
                near, away = away, near
            upper = upper + dot_tn(near, chosen)
            lower = lower + dot_tn(away, chosen)
            fvec = fvec + dot_nn(extra_ref[n, :, 512 : 512 + HL], chosen)
        xr_ref[:ROWS] = upper.astype(BF)
        xr_ref[ROWS:] = lower.astype(BF)
        fvec_ref[...] = fvec[:8] + fvec[8:]
        bias_ref[...] = allowed_bias(scal, kept_ref[:1])

    weight = join(weights, rows)
    wo_ref[0] = weight[:, 512:]
    window = extra_ref[pl.ds(step, 1), :, 256:512][0].astype(F32)
    q_bias = window[0:1] + window[1:2]
    v_bias = window[2:3] + window[3:4]
    lane = lax.broadcasted_iota(jnp.int32, (1, 256), 1)
    packed = xr_ref[...]
    kv = dot_nn(packed, weight[:, :384])
    kv_bias = jnp.concatenate([jnp.zeros((1, 128), F32), v_bias], axis=1)
    kv = (kv + kv_bias).astype(BF)
    queries = (dot_nn(packed[:ROWS], weight[:, 384:640]) + q_bias).astype(BF)
    queries = jnp.where(lane < HL, queries, jnp.zeros_like(queries)) * jnp.asarray(0.125, BF)
    kv_ref[0] = kv
    q_ref[0] = queries
    keys, values = kv[:, :256], kv[:, 128:]
    context = jnp.zeros((ROWS, 256), F32)
    totals = jnp.zeros((ROWS, 256), F32)
    for h in range(3):
        own = jnp.where(lanes_of_head(h, 0), queries, jnp.zeros_like(queries))
        scores = dot_nt(own, keys) + bias_ref[...]
        top = jnp.max(scores, axis=1, keepdims=True)
        weight_h = jnp.exp(scores - top)
        total = jnp.sum(weight_h, axis=1, keepdims=True)
        part = dot_nn(weight_h.astype(BF), values) / total
        context = jnp.where(lanes_of_head(h, HD), part, context)
        totals = jnp.where(lane == h, top + jnp.log(total), totals)
    ctx_ref[0] = context.astype(BF)
    ctx_f_ref[0] = context + totals


def attend(scal, kept, xs, extra, weights):
    pieces = len(weights)
    return call(
        functools.partial(attend_body, pieces),
        (4,),
        [SMEM, full((8, KEYS))]
        + [full((HL, KEYS))] * 4
        + [full((4, 16, D))]
        + [pl.BlockSpec((1,) + w.shape[1:], lambda j: (j, 0, 0)) for w in weights],
        [
            full((KEYS, D)),
            full((8, D)),
            pl.BlockSpec((1, KEYS, 384), lambda j: (j, 0, 0)),
            pl.BlockSpec((1, ROWS, 256), lambda j: (j, 0, 0)),
            pl.BlockSpec((1, ROWS, 256), lambda j: (j, 0, 0)),
            pl.BlockSpec((1, ROWS, 256), lambda j: (j, 0, 0)),
            pl.BlockSpec((1, D, 256), lambda j: (j, 0, 0)),
        ],
        [
            shape((KEYS, D)),
            shape((8, D), F32),
            shape((4, KEYS, 384)),
            shape((4, ROWS, 256)),
            shape((4, ROWS, 256)),
            shape((4, ROWS, 256), F32),
            shape((4, D, 256)),
        ],
        [pltpu.VMEM((ROWS, KEYS), F32)],
        micros=23,
        limit=16,
    )(scal, kept, *xs, extra, *weights)


def over_rows(body, carried=()):
    def step(r, carried):
        return body(pl.ds(pl.multiple_of(r * CHUNK, CHUNK), CHUNK), carried)

    return lax.fori_loop(0, ROWS // CHUNK, step, carried)


def norm(residual, gain, shift):
    mean = jnp.mean(residual, axis=1, keepdims=True)
    spread_row = jnp.mean(residual * residual, axis=1, keepdims=True) - mean * mean
    scale = lax.rsqrt(spread_row + EPS)
    unit = (residual - mean) * scale
    return unit * gain + shift, unit, scale


def norm_back(grad, gain, unit, scale):
    scaled = grad * gain
    mean = jnp.mean(scaled, axis=1, keepdims=True)
    cross = jnp.mean(scaled * unit, axis=1, keepdims=True)
    return scale * (scaled - mean - unit * cross)


def split_out(total, keep_ref, send_ref, first=0):
    low = total.astype(BF).reshape(PARTS, FB, D)
    half = PARTS // 2
    keep_ref[:, 0, first : first + FB] = low[:half]
    send_ref[:, 0, first : first + FB] = low[half:]


ERFC = (-0.82215223, 1.48851587, -1.13520398, 0.27886807, -0.18628806, 0.09678418, 0.37409196, 1.00002368, -1.26551223)


def gelu_parts(pre):
    square = pre * pre * -0.5
    t = 1.0 / (1.0 + jnp.abs(pre) * (0.5 * math.sqrt(0.5)))
    poly = 0.17087277 * t
    for c in ERFC[:-1]:
        poly = (poly + c) * t
    tail = 0.5 * t * jnp.exp(square + (poly + ERFC[-1]))
    half = jnp.where(pre >= 0, 1.0 - tail, tail)
    return pre * half, half + pre * (jnp.exp(square) * (1.0 / math.sqrt(2.0 * math.pi)))


def hidden_body(pieces, scal, ctx_ref, wo_ref, xr_ref, fvec_ref, extra_ref, fin_ref, cot_ref, *refs):
    inner_w, outer_w, refs = refs[:pieces], refs[pieces : 2 * pieces], refs[2 * pieces :]
    unit_ref, scale_ref, grad_ref, vec_ref, fin_grad_ref, sums_ref, keep_ref, send_ref, pre_ref, bias_ref = refs[:10]
    act_ref, slope_ref, normed_ref, first_ref, low_ref, total_ref, unit_two_ref, scale_two_ref = refs[10:]
    step = pl.program_id(0)
    at = pl.ds(step & 3, 1)

    @pl.when(step == 0)
    def _():
        total = xr_ref[...].astype(F32) + fvec_ref[0:1]
        for n in range(4):
            total = total + dot_nt(ctx_ref[n], wo_ref[n])
        normed_ref[...] = total

        def rows_of(rows, carried):
            normed, unit, scale = norm(normed_ref[rows, :], fvec_ref[2:3], fvec_ref[3:4])
            normed_ref[rows, :] = normed
            unit_ref[rows, :] = unit
            scale_ref[rows, :] = jnp.broadcast_to(scale, (CHUNK, 128))
            first_ref[rows, :] = normed.astype(BF)
            return carried

        over_rows(rows_of)

    @pl.when(step < 4)
    def _():
        window = extra_ref[at, :, 256:512][0].astype(F32)
        bias = jnp.concatenate([window[4 + n : 5 + n] + window[7 + n : 8 + n] for n in range(3)], axis=1)
        act, slope = gelu_parts(dot_nn(first_ref[...], join(inner_w, D // pieces)) + bias)
        act_ref[at] = act.astype(BF)[None]
        slope_ref[at] = slope[None]

    @pl.when((step >= 4) & (step < 8))
    def _():
        part = dot_nt(act_ref[at][0], join(outer_w, D // pieces))

        @pl.when(step == 4)
        def _():
            total_ref[...] = normed_ref[...] + fvec_ref[1:2] + part

        @pl.when(step > 4)
        def _():
            total_ref[...] += part

    @pl.when(step == 7)
    def _():
        gain = fvec_ref[4:5]

        def rows_of(rows, carried):
            normed, unit, scale = norm(total_ref[rows, :], gain, fvec_ref[5:6])
            unit_two_ref[rows, :] = unit
            scale_two_ref[rows, :] = jnp.broadcast_to(scale, (CHUNK, 128))
            low_ref[rows, :] = normed.astype(BF)
            return carried

        over_rows(rows_of)
        low = low_ref[...]
        frow = feature_row(scal, pieces > 1)
        final = jnp.zeros((OUT, D), F32)
        for n in range(4):
            final = final + dot_nn(fin_ref[n], pick(scal, frow, n))
        columns = lax.broadcasted_iota(jnp.int32, (OUT, OUT), 0)
        place = jnp.where(columns == final_row(scal, pieces > 1), 1.0, 0.0).astype(BF)
        final = dot_nn(place, final.astype(BF)).astype(BF)
        projected = dot_nt(low, final)
        length = lax.rsqrt(jnp.sum(projected * projected, axis=1, keepdims=True) + EPS)
        units = projected * length
        vec_ref[...] = jnp.transpose(units).astype(BF)
        grads = cot_ref[...]
        grads = length * (grads - units * jnp.sum(grads * units, axis=1, keepdims=True))
        grads = grads.astype(BF)
        fin_grad = dot_tn(place, dot_tn(grads, low).astype(BF)).astype(BF)
        for n in range(4):
            fin_grad_ref[n] = dot_nt(fin_grad, pick(scal, frow, n)).astype(BF)
        total_ref[...] = dot_nn(grads, final)

        def rows_back(rows, carried):
            grad, unit = total_ref[rows, :], unit_two_ref[rows, :]
            back = norm_back(grad, gain, unit, scale_two_ref[rows, :1])
            grad_ref[rows, :] = back
            low_ref[rows, :] = back.astype(BF)
            sums = (grad * unit, grad, back)
            return tuple(c + jnp.sum(t, axis=0, keepdims=True) for c, t in zip(carried, sums))

        sums = over_rows(rows_back, (jnp.zeros((1, D), F32),) * 3)
        for n in range(3):
            sums_ref[n : n + 1] = sums[n]
        sums_ref[3:] = jnp.zeros((5, D), F32)

    @pl.when(step >= 8)
    def _():
        low = low_ref[...]
        grad = dot_nn(low, join(outer_w, D // pieces)) * slope_ref[at][0]
        split_out(dot_tn(low, act_ref[at][0]), keep_ref, send_ref)
        grad_low = grad.astype(BF)
        pre_ref[0] = grad_low
        bias_ref[0] = jnp.broadcast_to(jnp.sum(grad, axis=0, keepdims=True), (8, D))
        split_out(dot_tn(first_ref[...], grad_low), keep_ref, send_ref, FB)


def hidden(scal, context, wo, packed, fvec, extra, final, cot, inner_w, outer_w):
    pieces = len(inner_w)
    half = PARTS // 2
    late = lambda j: (jnp.maximum(j - 8, 0), 0, 0)
    wide = pl.BlockSpec((half, 1, 2 * FB, D), lambda j: (0, jnp.maximum(j - 8, 0), 0, 0))
    return call(
        functools.partial(hidden_body, pieces),
        (12,),
        [SMEM, full((4, ROWS, 256)), full((4, D, 256)), full((ROWS, D)), full((8, D)), full((4, 16, D))]
        + [full((4, OUT, HL)), full((ROWS, OUT))]
        + [pl.BlockSpec((1, D // pieces, D), lambda j: (jnp.minimum(j, 3), 0, 0)) for _ in inner_w]
        + [pl.BlockSpec((1, D // pieces, D), lambda j: (jnp.where(j < 4, 0, j & 3), 1, 0)) for _ in outer_w],
        [full((ROWS, D)), full((ROWS, 128)), full((ROWS, D)), full((OUT, ROWS)), full((4, OUT, HL)), full((8, D))]
        + [wide, wide, pl.BlockSpec((1, ROWS, D), late), pl.BlockSpec((1, 8, D), late)],
        [
            shape((ROWS, D), F32),
            shape((ROWS, 128), F32),
            shape((ROWS, D), F32),
            shape((OUT, ROWS)),
            shape((4, OUT, HL)),
            shape((8, D), F32),
            shape((half, 4, 2 * FB, D)),
            shape((half, 4, 2 * FB, D)),
            shape((4, ROWS, D)),
            shape((4, 8, D), F32),
        ],
        [
            pltpu.VMEM((4, ROWS, D), BF),
            pltpu.VMEM((4, ROWS, D), F32),
            pltpu.VMEM((ROWS, D), F32),
            pltpu.VMEM((ROWS, D), BF),
            pltpu.VMEM((ROWS, D), BF),
            pltpu.VMEM((ROWS, D), F32),
            pltpu.VMEM((ROWS, D), F32),
            pltpu.VMEM((ROWS, 128), F32),
        ],
        micros=30,
        limit=24,
    )(scal, context, wo, packed, fvec, extra, final, cot, *inner_w, *outer_w)


def inner_back_body(pieces, pre_ref, grad_ref, unit_ref, scale_ref, fvec_ref, sums_ref, *refs):
    weights = refs[:pieces]
    one_ref, one_low_ref, all_ref, total_ref = refs[pieces:]
    step = pl.program_id(0)
    part = dot_nt(pre_ref[0], join(weights, D // pieces))

    @pl.when(step == 0)
    def _():
        total_ref[...] = grad_ref[...] + part

    @pl.when(step > 0)
    def _():
        total_ref[...] += part

    @pl.when(step == 3)
    def _():
        def rows_back(rows, carried):
            grad, unit = total_ref[rows, :], unit_ref[rows, :]
            back = norm_back(grad, fvec_ref[2:3], unit, scale_ref[rows, :1])
            one_ref[rows, :] = back
            one_low_ref[rows, :] = back.astype(BF)
            sums = (grad * unit, grad, back)
            return tuple(c + jnp.sum(t, axis=0, keepdims=True) for c, t in zip(carried, sums))

        all_ref[0:3] = sums_ref[0:3]
        sums = over_rows(rows_back, (jnp.zeros((1, D), F32),) * 3)
        for n in range(3):
            all_ref[3 + n : 4 + n] = sums[n]
        all_ref[6:] = jnp.zeros((2, D), F32)


def inner_back(pre, grad, unit, scale, fvec, sums, weights):
    pieces = len(weights)
    at = lambda j: (j, 0, 0)
    return call(
        functools.partial(inner_back_body, pieces),
        (4,),
        [
            pl.BlockSpec((1, ROWS, D), at),
            full((ROWS, D)),
            full((ROWS, D)),
            full((ROWS, 128)),
            full((8, D)),
            full((8, D)),
        ]
        + [pl.BlockSpec((1, D // pieces, D), at) for w in weights],
        [full((ROWS, D)), full((ROWS, D)), full((8, D))],
        [shape((ROWS, D), F32), shape((ROWS, D)), shape((8, D), F32)],
        [pltpu.VMEM((ROWS, D), F32)],
        micros=9,
        limit=10,
    )(pre, grad, unit, scale, fvec, sums, *weights)


def small_sums(scal, by_xor, n, q_sum, v_sum, all_ref, fin_ref, hid_ref):
    sums = dot_nt(all_ref[...].astype(BF), pick(scal, feature_row(scal, by_xor), n))
    sums = jnp.concatenate([sums, jnp.zeros((8, 64), F32)], axis=1)
    heads = jnp.concatenate([q_sum, v_sum, jnp.zeros((6, 256), F32)], axis=0)
    hidden = hid_ref[0, 0:1]
    hidden = [hidden[:, 256 * k : 256 * (k + 1)] for k in range(3)]
    hidden = jnp.concatenate(hidden + [jnp.zeros((13, 256), F32)], axis=0)
    wide = jnp.concatenate([jnp.concatenate([sums, heads], axis=0), hidden], axis=1).astype(BF)
    final = fin_ref[0].reshape(PARTS, OUT // PARTS, HL)
    final = jnp.concatenate([final, jnp.zeros((PARTS, OUT // PARTS, 64), BF)], axis=2)
    return jnp.concatenate([final, jnp.broadcast_to(wide[None], (PARTS, 16, 512))], axis=2)


def attend_back_body(pieces, first, count, scal, kept_ref, xr_ref, kv_ref, q_ref, ctx_ref, ctx_f_ref, one_ref, low_ref, all_ref, fin_ref, hid_ref, *refs):
    weights = refs[:pieces]
    refs = refs[pieces + (2 if first else 0) :]
    keep_ref, send_ref = refs[:2]
    bias_ref, total_ref = refs[-2:]
    step = pl.program_id(0)

    @pl.when(step == 0)
    def _():
        bias_ref[...] = allowed_bias(scal, kept_ref[:1])
        total_ref[:ROWS] = one_ref[:ROWS]
        total_ref[ROWS:] = one_ref[ROWS:] if first else jnp.zeros((ROWS, D), F32)

    weight = join(weights, D // pieces)
    low = low_ref[...]
    lane = lax.broadcasted_iota(jnp.int32, (1, 256), 1)
    grad_ctx = dot_nn(low, weight[:, 512:])
    grad_ctx = jnp.where(lane >= HD, grad_ctx, 0.0).astype(BF)
    keys, values = kv_ref[0, :, :256], kv_ref[0, :, 128:]
    queries = q_ref[0]
    products = grad_ctx.astype(F32) * ctx_f_ref[0]
    dq = jnp.zeros((ROWS, 256), F32)
    dk = jnp.zeros((KEYS, 256), F32)
    dv = jnp.zeros((KEYS, 256), F32)
    zero = jnp.zeros_like(queries)
    for h in range(3):
        own = jnp.where(lanes_of_head(h, 0), queries, zero)
        own_grad = jnp.where(lanes_of_head(h, HD), grad_ctx, zero)
        row_dot = jnp.sum(jnp.where(lanes_of_head(h, HD), products, 0.0), axis=1, keepdims=True)
        scores = dot_nt(own, keys) + bias_ref[...]
        prob = jnp.exp(scores - ctx_f_ref[0, :, h : h + 1])
        dv = dv + dot_tn(prob.astype(BF), own_grad)
        grad_scores = (prob * (dot_nt(own_grad, values) - row_dot)).astype(BF)
        dq = jnp.where(lanes_of_head(h, 0), dot_nn(grad_scores, keys), dq)
        dk = dk + dot_tn(grad_scores, own)
    dq = dq * 0.125
    gap = jnp.zeros((KEYS, 128), F32)
    dkv = jnp.concatenate([dk, gap], axis=1) + jnp.concatenate([gap, dv], axis=1)
    q_sum = jnp.sum(dq, axis=0, keepdims=True)
    v_sum = jnp.sum(dv, axis=0, keepdims=True)
    dkv = dkv.astype(BF)
    dq = dq.astype(BF)
    packed = xr_ref[...]
    low_kv = dot_tn(packed, dkv)
    from_q = dot_tn(packed[:ROWS], dq)
    from_o = dot_tn(low, ctx_ref[0])
    gap = jnp.zeros((D, 128), F32)
    from_qo = jnp.concatenate([from_q, gap], axis=1) + jnp.concatenate([gap, from_o], axis=1)
    split_out(jnp.concatenate([low_kv, from_qo], axis=1), keep_ref, send_ref)
    extra = small_sums(scal, pieces > 1, first + step, q_sum, v_sum, all_ref, fin_ref, hid_ref)
    keep_ref[:, 0, FB:] = extra[: PARTS // 2]
    send_ref[:, 0, FB:] = extra[PARTS // 2 :]
    total_ref[...] += dot_nt(dkv, weight[:, :384])
    total_ref[:ROWS] += dot_nt(dq, weight[:, 384:640])

    @pl.when(step == count - 1)
    def _():
        if first + count < 4:
            refs[2][...] = total_ref[...]
            return
        x0_ref, x2_ref, x1_ref, x3_ref = refs[2:6]
        grads = total_ref[...].astype(BF)
        frow = feature_row(scal, pieces > 1)
        x0_ref[...] = dot_nt(pick(scal, frow, 0), grads)
        x2_ref[...] = dot_nt(pick(scal, frow, 1), grads)
        for n, ref in ((2, x1_ref), (3, x3_ref)):
            part = dot_nt(pick(scal, frow, n), grads).astype(BF)
            ref[:, :ROWS] = part[:, ROWS:]
            ref[:, ROWS:] = part[:, :ROWS]


def attend_back(scal, kept, packed, kv, queries, context, context_f, one, low, small, weights, first, count, held):
    pieces = len(weights)
    half = PARTS // 2
    at = lambda j: (j + first, 0, 0)
    wide = pl.BlockSpec((half, 1, FB + 16, D), lambda j: (0, j + first, 0, 0))
    n_in = 12 + pieces
    last = first + count == 4
    return call(
        functools.partial(attend_back_body, pieces, first, count),
        (count,),
        [
            SMEM,
            full((8, KEYS)),
            full((KEYS, D)),
            pl.BlockSpec((1, KEYS, 384), at),
            pl.BlockSpec((1, ROWS, 256), at),
            pl.BlockSpec((1, ROWS, 256), at),
            pl.BlockSpec((1, ROWS, 256), at),
            full(one.shape),
            full((ROWS, D)),
            full((8, D)),
            pl.BlockSpec((1, OUT, HL), at),
            pl.BlockSpec((1, 8, D), at),
        ]
        + [pl.BlockSpec((1,) + w.shape[1:], at) for w in weights]
        + [pl.BlockSpec(memory_space=pl.ANY)] * len(held),
        [wide, wide] + ([full((HL, KEYS))] * 4 if last else [full((KEYS, D))]),
        [shape((half, 4, FB + 16, D)), shape((half, 4, FB + 16, D))]
        + ([shape((HL, KEYS), F32)] * 2 + [shape((HL, KEYS))] * 2 if last else [shape((KEYS, D), F32)]),
        [pltpu.VMEM((ROWS, KEYS), F32), pltpu.VMEM((KEYS, D), F32)],
        micros=9 * count,
        limit=24,
        aliases={n_in + n: n for n in range(len(held))},
    )(scal, kept, packed, kv, queries, context, context_f, one, low, *small, *weights, *held)


def pack_vec_body(order_ref, mask_ref, vec_ref, out_ref, total_ref):
    step = pl.program_id(0)
    part = dot_nt(vec_ref[0], spread(order_ref[:1]))

    @pl.when(step == 0)
    def _():
        total_ref[...] = part

    @pl.when(step > 0)
    def _():
        total_ref[...] += part

    @pl.when(step == 3)
    def _():
        out_ref[...] = jnp.transpose(total_ref[...] * mask_ref[...].astype(F32))


def pack_vec(order, mask_row, vecs):
    return call(
        pack_vec_body,
        (4,),
        [
            pl.BlockSpec((8, ROWS), lambda b: (0, b)),
            full((1, TOK)),
            pl.BlockSpec((1, OUT, ROWS), lambda b: (b, 0, 0)),
        ],
        full((TOK, OUT)),
        shape((TOK, OUT), F32),
        [pltpu.VMEM((OUT, TOK), F32)],
        micros=5,
    )(order, mask_row, vecs)


def pack_x_body(order_ref, x0_ref, x1_ref, far_ref, out_ref):
    step = pl.program_id(0)
    near = (x0_ref[...] + x1_ref[...].astype(F32)).astype(BF)
    part = dot_nt(jnp.where(step < 2, near, far_ref[...]), spread(order_ref[:1]))

    @pl.when(step == 0)
    def _():
        out_ref[...] = part

    @pl.when(step > 0)
    def _():
        out_ref[...] += part


def pack_x(order, *parts):
    return call(
        pack_x_body,
        (4,),
        [pl.BlockSpec((8, ROWS), lambda b: (0, b))]
        + [pl.BlockSpec((HL, ROWS), lambda b: (0, b & 1)) for _ in parts],
        full((HL, TOK)),
        shape((HL, TOK), F32),
        micros=5,
    )(order, *parts)


def halves(vector):
    high = vector.astype(BF)
    return high, (vector - high.astype(F32)).astype(BF)


def pack_weights_body(k_ref, v_ref, q_ref, o_ref, in_ref, out_ref, fin_ref, qb, vb, inb, ob, outb, g1, s1, g2, s2, heads_ref, ffn_ref):
    turned = lambda ref: jnp.transpose(ref[...].astype(F32)).astype(BF)
    heads_ref[:FB] = jnp.concatenate([k_ref[...], v_ref[...], q_ref[...], turned(o_ref)], axis=1)
    ffn_ref[:FB] = in_ref[...]
    ffn_ref[FB : 2 * FB] = out_ref[...]
    qb, vb, inb, ob, outb, g1, s1, g2, s2 = (ref[...].reshape(1, ref.shape[0]) for ref in (qb, vb, inb, ob, outb, g1, s1, g2, s2))
    gap = jnp.zeros((1, 64), F32)
    window = []
    for value in (jnp.concatenate([qb, gap], axis=1), jnp.concatenate([gap, vb], axis=1)):
        window += list(halves(value))
    hidden = [halves(inb[:, n * 256 : (n + 1) * 256]) for n in range(3)]
    window += [high for high, _ in hidden] + [low for _, low in hidden]
    window = jnp.concatenate(window + [jnp.zeros((6, 256), BF)], axis=0)
    features = [halves(jnp.concatenate([value, gap], axis=1)) for value in (ob, outb, g1, s1, g2, s2)]
    pad = [jnp.zeros((2, 256), BF)]
    features = jnp.concatenate([high for high, _ in features] + pad + [low for _, low in features] + pad, axis=0)
    final = jnp.concatenate([fin_ref[...], jnp.zeros((16, 64), BF)], axis=1)
    extra = jnp.concatenate([final, window, features], axis=1)
    heads_ref[FB:] = extra


def pack_weights(weights, vectors):
    return call(
        pack_weights_body,
        (1,),
        [full(w.shape) for w in weights] + [full(v.shape) for v in vectors],
        [full((FB + 16, D)), full((2 * FB, D))],
        [shape((FB + 16, D)), shape((2 * FB, D))],
        micros=3,
        limit=56,
    )(*weights, *vectors)


def ffn_out_body(a_ref, b_ref, out_ref, in_ref):
    total = a_ref[...] + b_ref[...].astype(F32)
    out_ref[...] = total[:FB]
    in_ref[...] = total[FB:]


def ffn_out(a, b):
    both = [full((FB, D))] * 2
    return call(ffn_out_body, (1,), [full(a.shape), full(b.shape)], both, [shape((FB, D), F32)] * 2, micros=3)(a, b)


def heads_out_body(a_ref, b_ref, q_ref, k_ref, v_ref, o_ref, fin_ref, inb, qb, vb, ob, outb, g1, s1, g2, s2):
    total = a_ref[...] + b_ref[...].astype(F32)
    k_ref[...] = total[:FB, :HL]
    v_ref[...] = total[:FB, HL:384]
    q_ref[...] = total[:FB, 384:576]
    o_ref[...] = jnp.transpose(total[:FB, 576:])
    tile = total[FB:]
    fin_ref[...] = tile[:, :HL]
    qb[...] = tile[8:9, 256 : 256 + HL].reshape(HL)
    vb[...] = tile[9:10, 320:512].reshape(HL)
    for n, ref in ((5, ob), (2, outb), (3, g1), (4, s1), (0, g2), (1, s2)):
        ref[...] = tile[n : n + 1, 256 : 256 + HL].reshape(HL)
    inb[...] = jnp.concatenate([tile[n : n + 1, 512:] for n in range(3)], axis=1).reshape(D)


def heads_out(a, b):
    dims = [(FB, HL)] * 3 + [(HL, FB), (16, HL), (D,)] + [(HL,)] * 8
    return call(
        heads_out_body, (1,), [full(a.shape), full(b.shape)], [full(d) for d in dims], [shape(d, F32) for d in dims], micros=3
    )(a, b)


def hi_lo(vector):
    high = vector.astype(BF)
    high = lax.optimization_barrier(high)
    return high, (vector - high.astype(F32)).astype(BF)


def extra_rows(final_t, q_bias, v_bias, inner_bias, features):
    q_hi, q_lo = hi_lo(jnp.pad(q_bias, (0, 64)))
    v_hi, v_lo = hi_lo(jnp.pad(v_bias, (64, 0)))
    in_hi, in_lo = hi_lo(inner_bias.reshape(3, 256))
    window = jnp.concatenate([jnp.stack([q_hi, q_lo, v_hi, v_lo]), in_hi, in_lo], axis=0)
    window = jnp.pad(window, ((0, 6), (0, 0)))
    f_hi, f_lo = hi_lo(jnp.pad(jnp.stack(features), ((0, 2), (0, 64))))
    final_t = jnp.pad(final_t, ((0, 16 - final_t.shape[0]), (0, 64)))
    return jnp.concatenate([final_t, window, jnp.concatenate([f_hi, f_lo], axis=0)], axis=1)


def local(
    inputs,
    token_order,
    lengths,
    token_mask,
    cotangent,
    query_weight,
    key_weight,
    value_weight,
    output_weight,
    inner_weight,
    outer_weight,
    final_weight,
    query_bias,
    value_bias,
    output_bias,
    inner_bias,
    outer_bias,
    first_gain,
    first_shift,
    second_gain,
    second_shift,
):
    m, i = lax.axis_index("mp"), lax.axis_index("dp")
    n_dp = lax.axis_size("dp")
    rows = D // n_dp
    by_xor = n_dp == 8
    scal = jnp.concatenate([jnp.stack([i, m]).astype(jnp.int32), lengths[0]])
    features_of = [output_bias, outer_bias, first_gain, first_shift, second_gain, second_shift]

    if by_xor:
        heads_own, ffn_own = pack_weights(
            [key_weight, value_weight, query_weight, output_weight, inner_weight, outer_weight.T, final_weight.T],
            [query_bias, value_bias, inner_bias] + features_of,
        )
    else:
        extra = extra_rows(final_weight.T, query_bias, value_bias, inner_bias, features_of)
        heads_own = jnp.concatenate([key_weight, value_weight, query_weight, output_weight.T], axis=1)
        heads_own = jnp.concatenate([heads_own, extra], axis=0)
        ffn_own = jnp.concatenate([inner_weight, outer_weight.T], axis=0)

    mask_row = token_mask.reshape(1, TOK)
    heads_own, ffn_own, inputs = sync(heads_own, ffn_own, inputs)
    heads_got = [swap(heads_own, "mp", bit) for bit in (2, 1, 3)]
    features, kept, cot, order = pack_in(scal, token_order, inputs, mask_row, cotangent)
    near, away = features[:, :KEYS], features[:, KEYS:]
    ffn_own, near, away = sync(ffn_own, near, away)
    ffn_got = [swap(ffn_own, "mp", bit) for bit in (2, 1, 3)]
    heads_got = sync(*heads_got)
    heads = jnp.stack([h[:rows] for h in (heads_own, *heads_got)])
    extras = jnp.stack([h[rows:] for h in (heads_own, *heads_got)])
    if by_xor:
        heads, near, away = sync(heads, near, away)
        head_x, head_y = over_plane(heads)
        head_x, head_y = sync(head_x, head_y)
        far_a, far_b = sync(*over_corner(head_x, head_y))
        far_a, far_b, ffn_got, near, away, heads, head_x, head_y = sync(
            far_a, far_b, ffn_got, near, away, heads, head_x, head_y
        )
        x1, x2 = swap(near, "mp", 1), swap(away, "mp", 2)
        ffn = jnp.stack([ffn_own, *ffn_got])
        ffn = jnp.concatenate([ffn, extras], axis=1)
        ffn_x, ffn_y = over_plane(ffn)
        far = jnp.concatenate([far_a, far_b], axis=0)
        head_pieces = [heads, head_x, head_y, far]
        head_pieces += [swap(p, "dp", 1) for p in head_pieces]
        x1, x2, *head_pieces = sync(x1, x2, *head_pieces)
        x3 = swap(x2, "mp", 1)
        x3, ffn_x, ffn_y = sync(x3, ffn_x, ffn_y)
        far_a, far_b = over_corner(ffn_x, ffn_y)
        ffn_pieces = [swap(p, "dp", 1) for p in (ffn, ffn_x, ffn_y)]
    else:
        ffn = jnp.concatenate([jnp.stack([ffn_own, *ffn_got]), extras], axis=1)
        x1, x2 = swap(near, "mp", 1), swap(away, "mp", 2)
        x3 = swap(x2, "mp", 1)
        head_pieces, ffn_pieces, final = plain_pieces(heads, ffn)

    packed, fvec, kv, queries, context, context_f, wo = attend(
        scal, kept, (near, x2, x1, x3), extras, head_pieces
    )
    if by_xor:
        context, far_a, far_b, *ffn_pieces = sync(context, far_a, far_b, *ffn_pieces)
        far = jnp.concatenate([far_a, far_b], axis=0)
        ffn_pieces = [ffn, ffn_x, ffn_y, far] + ffn_pieces + [swap(far, "dp", 1)]
        final = jnp.concatenate([p[:, 2 * FB :, :HL] for p in ffn_pieces], axis=1)
    unit, scale, grad_two, vec, fin_grad, sums, ffn_keep, ffn_send, pre, hid_sums = hidden(
        scal, context, wo, packed, fvec, extras, final, cot, ffn_pieces, ffn_pieces
    )
    vec_got = swap(vec, "mp", 1)
    saved = (kept, packed, kv, queries, context, context_f)

    def heads_back(one, low, first, count, held):
        small = (all_sums, fin_grad, hid_sums)
        return attend_back(scal, *saved, one, low, small, head_pieces, first, count, held)

    if by_xor:
        ffn_got = swap(ffn_send, "dp", 1)
        grad_one, one_low, all_sums = inner_back(pre, grad_two, unit, scale, fvec, sums, ffn_pieces)
        ffn_got, vec_got, one_low = sync(ffn_got, vec_got, one_low)
        pair = (ffn_keep, ffn_got)
        x_send, y_send = plane_first(*pair)
        one_low, x_send, y_send = sync(one_low, x_send, y_send)
        x_got, y_got = swap(x_send, "dp", 2), swap(y_send, "dp", 4)
        vec_low = jnp.stack([vec, vec_got])
        vec_high = swap(vec_low, "mp", 2)
        head_keep, head_send, dx0, dx2, dx1, dx3 = heads_back(grad_one, one_low, 0, 4, ())
        dx1, dx3, head_send, x_got, y_got, vec_high = sync(dx1, dx3, head_send, x_got, y_got, vec_high)

        dx3_got = swap(dx3, "mp", 1)
        head_got = swap(head_send, "dp", 1)
        to_y, to_x, upper, lower = plane_second(*pair, x_got, y_got)
        from_y, from_x = swap(to_y, "dp", 4), swap(to_x, "dp", 2)
        vecs = jnp.concatenate([vec_low, vec_high], axis=0)
        dx3_got, head_got, dx1, vecs = sync(dx3_got, head_got, dx1, vecs)
        to_far = (dx2 + dx3_got.astype(F32)).astype(BF)
        far, dx1_got = swap(to_far, "mp", 2), swap(dx1, "mp", 1)
        pair = (head_keep, head_got)
        x_send, y_send = plane_first(*pair)
        x_send, y_send, vecs = sync(x_send, y_send, vecs)
        x_got, y_got = swap(x_send, "dp", 2), swap(y_send, "dp", 4)
        vectors = pack_vec(order, mask_row, vecs)
        from_y, from_x, vectors = sync(from_y, from_x, vectors)
        upper = upper + from_y.astype(F32)
        lower = (lower + from_x.astype(F32)).astype(BF)
        lower_got = swap(lower, "mp", 1)
        x_got, y_got, dx1_got, far = sync(x_got, y_got, dx1_got, far)
        to_y, to_x, h_upper, h_lower = plane_second(*pair, x_got, y_got)
        to_y, to_x, dx1_got = sync(to_y, to_x, dx1_got)
        from_y, from_x = swap(to_y, "dp", 4), swap(to_x, "dp", 2)
        inputs_grad = pack_x(order, dx0, dx1_got, far)
        from_y, from_x, lower_got, inputs_grad = sync(from_y, from_x, lower_got, inputs_grad)
        h_upper = h_upper + from_y.astype(F32)
        h_lower = (h_lower + from_x.astype(F32)).astype(BF)
        h_lower_got = swap(h_lower, "mp", 1)
        upper = upper + lower_got.astype(F32)
        last = swap(upper[1].astype(BF), "mp", 2)
        h_lower_got, last = sync(h_lower_got, last)
        h_upper = h_upper + h_lower_got.astype(F32)
        h_last = swap(h_upper[1].astype(BF), "mp", 2)
        g_out, g_in = ffn_out(upper[0], last)
        g_q, g_k, g_v, g_o, g_fin, g_inb, g_qb, g_vb, g_ob, g_outb, g_g1, g_s1, g_g2, g_s2 = heads_out(h_upper[0], h_last)
        g_out, g_fin = g_out.T, g_fin.T
    else:
        grad_one, one_low, all_sums = inner_back(pre, grad_two, unit, scale, fvec, sums, ffn_pieces)
        head_keep, head_send, dx0, dx2, dx1, dx3 = heads_back(grad_one, one_low, 0, 4, ())
        far = swap((dx2 + swap(dx3, "mp", 1).astype(F32)).astype(BF), "mp", 2)
        inputs_grad = pack_x(order, dx0, swap(dx1, "mp", 1), far)
        vec_low = jnp.stack([vec, vec_got])
        vectors = pack_vec(order, mask_row, jnp.concatenate([vec_low, swap(vec_low, "mp", 2)], axis=0))
        ends = []
        for keep, send in ((ffn_keep, ffn_send), (head_keep, head_send)):
            total = scatter_plain(jnp.concatenate([keep, send], axis=0).transpose(1, 0, 2, 3).astype(F32))
            upper = total[:2] + swap(total[2:].astype(BF), "mp", 1).astype(F32)
            ends.append(upper[0] + swap(upper[1].astype(BF), "mp", 2).astype(F32))
        ffn_sum, head_sum = ends
        tile = head_sum[rows:]
        g_out, g_in, g_fin = ffn_sum[:rows].T, ffn_sum[rows:], tile[: OUT // n_dp, :HL].T
        g_g2, g_s2, g_outb, g_g1, g_s1, g_ob = (tile[n, 256 : 256 + HL] for n in range(6))
        g_inb = tile[:3, 512:].reshape(D)
        g_k, g_v, g_q, g_o = head_sum[:rows, :HL], head_sum[:rows, HL:384], head_sum[:rows, 384:576], head_sum[:rows, 576:].T
        g_qb, g_vb = tile[8, 256 : 256 + HL], tile[9, 320:512]
    return (
        vectors,
        inputs_grad,
        g_q,
        g_k,
        g_v,
        g_o,
        g_in,
        g_out,
        g_fin,
        g_qb,
        g_vb,
        g_ob,
        g_inb,
        g_outb,
        g_g1,
        g_s1,
        g_g2,
        g_s2,
    )


def solution(mesh):
    return jax.shard_map(
        local,
        mesh=mesh,
        in_specs=(
            P("mp", "dp"),
            P("dp", None),
            P("dp", None),
            P("dp"),
            P("dp", None),
            P("dp", "mp"),
            P("dp", "mp"),
            P("dp", "mp"),
            P("mp", "dp"),
            P("dp", "mp"),
            P("mp", "dp"),
            P("mp", "dp"),
            P("mp"),
            P("mp"),
            P("mp"),
            P("mp"),
            P("mp"),
            P("mp"),
            P("mp"),
            P("mp"),
            P("mp"),
        ),
        out_specs=(
            P("dp", None),
            P("mp", "dp"),
            P("dp", "mp"),
            P("dp", "mp"),
            P("dp", "mp"),
            P("mp", "dp"),
            P("dp", "mp"),
            P("mp", "dp"),
            P("mp", "dp"),
            P("mp"),
            P("mp"),
            P("mp"),
            P("mp"),
            P("mp"),
            P("mp"),
            P("mp"),
            P("mp"),
            P("mp"),
        ),
        check_vma=False,
    )
```

```python
import functools
import math

import jax
import jax.numpy as jnp
from jax import lax
from jax.experimental import pallas as pl
from jax.experimental.pallas import tpu as pltpu
from jax.sharding import PartitionSpec as P

D = 768
HD = 64
HL = 192
FB = 96
PARTS = 8
OUT = 128
TOK = 2048
ROWS = 512
KEYS = 1024
LONG = 1024
CHUNK = 64
EPS = 1e-06
F32 = jnp.float32
BF = jnp.bfloat16


def dot_nn(a, b):
    return lax.dot_general(a, b, (((1,), (0,)), ((), ())), preferred_element_type=F32)


def dot_nt(a, b):
    return lax.dot_general(a, b, (((1,), (1,)), ((), ())), preferred_element_type=F32)


def dot_tn(a, b):
    return lax.dot_general(a, b, (((0,), (0,)), ((), ())), preferred_element_type=F32)


def swap(array, axis, bit):
    size = lax.axis_size(axis)
    return lax.ppermute(array, axis, [(a, a ^ bit) for a in range(size)])


def full(shape):
    zeros = (0,) * len(shape)
    return pl.BlockSpec(shape, lambda *_: zeros)


SMEM = pl.BlockSpec(memory_space=pltpu.SMEM)


def call(body, grid, in_specs, out_specs, out_shape, scratch=(), micros=10, aliases=None, limit=12):
    return pl.pallas_call(
        body,
        grid=grid,
        in_specs=in_specs,
        out_specs=out_specs,
        out_shape=out_shape,
        scratch_shapes=list(scratch),
        input_output_aliases=aliases or {},
        compiler_params=pltpu.CompilerParams(
            dimension_semantics=("arbitrary",) * len(grid), vmem_limit_bytes=limit * 1024 * 1024
        ),
        cost_estimate=pl.CostEstimate(flops=micros * 4 * 10**9, transcendentals=0, bytes_accessed=micros * 12 * 10**6),
    )


def shape(dims, dtype=BF):
    return jax.ShapeDtypeStruct(dims, dtype)


def sync(*values):
    return lax.optimization_barrier(values)


def over_plane(held):
    return swap(held, "dp", 2), swap(held, "dp", 4)


def over_corner(x_part, y_part):
    return swap(y_part[:2], "dp", 2), swap(x_part[2:], "dp", 4)


def plain_pieces(heads, ffn):
    n_dp = lax.axis_size("dp")
    rows = D // n_dp
    whole = lax.all_gather(ffn, "dp", axis=1)
    parts = [whole[:, :, n * rows : (n + 1) * rows].reshape(4, D, D) for n in (0, 1)]
    final = whole[:, :, 2 * rows : 2 * rows + OUT // n_dp, :HL].reshape(4, OUT, HL)
    return [lax.all_gather(heads, "dp", axis=1, tiled=True)], [jnp.concatenate(parts, axis=1)], final


def scatter_plain(both):
    n_dp = lax.axis_size("dp")
    rows = both.shape[2]
    total = []
    for first in range(0, rows - FB + 1, FB):
        part = both[:, :, first : first + FB].reshape(4, D, D)
        total.append(lax.psum_scatter(part, "dp", scatter_dimension=1, tiled=True))
    if rows % FB == 0:
        return jnp.concatenate(total, axis=1)
    final = both[:, :, rows - 16 :, :256].reshape(4, OUT, 256)
    final = lax.psum_scatter(final, "dp", scatter_dimension=1, tiled=True)
    final = jnp.pad(final, ((0, 0), (0, 16 - OUT // n_dp), (0, 0)))
    sums = lax.psum(both[:, 0, rows - 16 :, 256:], "dp")
    return jnp.concatenate(total + [jnp.concatenate([final, sums], axis=2)], axis=1)


def added(pair, *index):
    return pair[0][index].astype(F32) + pair[1][index].astype(F32)


def by_plane(pair):
    return tuple(p.reshape((2, 2) + p.shape[1:]) for p in pair)


LOW, HIGH = slice(0, 2), slice(2, 4)


def plane_first(*pair):
    wide = by_plane(pair)
    return added(wide, slice(None), 1, LOW).astype(BF), added(wide, 1, slice(None), HIGH).astype(BF)


def plane_second(keep, got, x_got, y_got):
    wide = by_plane((keep, got))
    x_part = [added(wide, n, 0, LOW) + x_got[n].astype(F32) for n in range(2)]
    y_part = [added(wide, 0, n, HIGH) + y_got[n].astype(F32) for n in range(2)]
    return x_part[1].astype(BF), y_part[1].astype(BF), x_part[0], y_part[0]


def feature_row(scal, by_xor):
    lane = lax.broadcasted_iota(jnp.int32, (1, D), 1)
    if not by_xor:
        return lane
    part = jnp.zeros((1, D), jnp.int32)
    for n in range(1, PARTS):
        part = part + jnp.where(lane >= n * FB, 1, 0)
    return (((part & 3) * 2 + (part >> 2)) ^ scal[0]) * FB + lane - part * FB


def final_row(scal, by_xor):
    lane = lax.broadcasted_iota(jnp.int32, (1, OUT), 1)
    if not by_xor:
        return lane
    part = lane >> 4
    return (((part & 3) * 2 + (part >> 2)) ^ scal[0]) * 16 + (lane & 15)


def pick(scal, frow, n):
    first = (scal[1] ^ ((n & 1) * 2 + (n >> 1))) * HL
    rows = lax.broadcasted_iota(jnp.int32, (HL, D), 0) + first
    return jnp.where(rows == frow, 1.0, 0.0).astype(BF)


def spread(order_row):
    rows = lax.broadcasted_iota(jnp.int32, (TOK, order_row.shape[1]), 0)
    return jnp.where(rows == order_row, 1.0, 0.0).astype(BF)


def pack_in_body(scal, order_ref, x_ref, mask_ref, cot_ref, out_ref, kept_ref, cot_out_ref, order_out_ref, canon_ref):
    block = pl.program_id(0)

    @pl.when(block == 0)
    def _():
        start, seen = jnp.int32(0), jnp.int32(0)
        for c in range(4):
            start = jnp.where(scal[2 + c] == LONG, seen, start)
            seen = seen + scal[2 + c]
        order = jnp.broadcast_to(order_ref[...], (8, TOK))
        canon_ref[:, :LONG] = pltpu.roll(order, (TOK - start) & (TOK - 1), 1)[:, :LONG]
        lane = lax.broadcasted_iota(jnp.int32, (8, LONG), 1)
        canon_ref[:, LONG:] = jnp.where(lane < start, order[:, :LONG], order[:, LONG:])
        for n in range(4):
            first = pl.multiple_of((scal[1] ^ n) * ROWS, ROWS)
            order_out_ref[:, n * ROWS : (n + 1) * ROWS] = canon_ref[:, pl.ds(first, ROWS)]

    one_hot = spread(order_out_ref[0:1, pl.ds(pl.multiple_of(block * ROWS, ROWS), ROWS)])
    out_ref[...] = dot_nn(x_ref[...], one_hot).astype(BF)
    mask = mask_ref[...].astype(F32)

    @pl.when(block < 2)
    def _():
        kept_ref[...] = dot_nn(jnp.broadcast_to(mask, (16, TOK)).astype(BF), one_hot)[:8]

    @pl.when(block == 0)
    def _():
        cot = (jnp.transpose(cot_ref[...].astype(F32)) * mask).astype(BF)
        cot_out_ref[...] = jnp.transpose(dot_nn(cot, one_hot))


def pack_in(scal, order, inputs, mask_row, cotangent):
    return call(
        pack_in_body,
        (4,),
        [SMEM, full((1, TOK)), full((HL, TOK)), full((1, TOK)), full((TOK, OUT))],
        [
            pl.BlockSpec((HL, ROWS), lambda b: (0, b)),
            pl.BlockSpec((8, ROWS), lambda b: (0, jnp.minimum(b, 1))),
            full((ROWS, OUT)),
            full((8, TOK)),
        ],
        [shape((HL, TOK)), shape((8, KEYS), F32), shape((ROWS, OUT), F32), shape((8, TOK), jnp.int32)],
        [pltpu.VMEM((8, TOK), jnp.int32)],
        micros=6,
    )(scal, order, inputs, mask_row, cotangent)


def join(refs, rows, first=0, last=D):
    parts = [ref[0, :rows, first:last] for ref in refs]
    return parts[0] if len(parts) == 1 else jnp.concatenate(parts, axis=0)


def lanes_of_head(h, shift):
    lane = lax.broadcasted_iota(jnp.int32, (1, 256), 1)
    return (lane >= shift + h * HD) & (lane < shift + (h + 1) * HD)


def allowed_bias(scal, kept):
    pair = scal[1] & 1
    end, count = jnp.int32(0), jnp.int32(0)
    cuts = [jnp.int32(LONG), jnp.int32(LONG)]
    for c in range(4):
        short = scal[2 + c] != LONG
        end = end + jnp.where(short, scal[2 + c], 0)
        count = count + jnp.where(short, 1, 0)
        cuts = [jnp.where(short & (count == n + 1) & (scal[1] >= 2), end, cuts[n]) for n in range(2)]
    q_pos = lax.broadcasted_iota(jnp.int32, (ROWS, 1), 0) + pair * ROWS
    k_pos = lax.broadcasted_iota(jnp.int32, (1, KEYS), 1) + pair * ROWS
    k_pos = k_pos & (KEYS - 1)
    q_seg = jnp.where(q_pos >= cuts[0], 1, 0) + jnp.where(q_pos >= cuts[1], 1, 0)
    k_seg = jnp.where(k_pos >= cuts[0], 1, 0) + jnp.where(k_pos >= cuts[1], 1, 0)
    k_seg = jnp.where(kept > 0.5, k_seg, k_seg + 8)
    return jnp.where((q_seg == k_seg) | (q_pos == k_pos), 0.0, -1e30)


def prepare_body(by_xor, scal, kept_ref, x0, x2, x1, extra_ref, part_ref, fvec_ref, bias_ref):
    frow = feature_row(scal, by_xor)
    upper = jnp.zeros((ROWS, D), F32)
    lower = jnp.zeros((ROWS, D), F32)
    fvec = jnp.zeros((16, D), F32)
    for n in range(4):
        chosen = pick(scal, frow, n)
        fvec = fvec + dot_nn(extra_ref[n, :, 512 : 512 + HL], chosen)
        if n < 3:
            ref = (x0, x2, x1)[n]
            near, away = (ref[:, ROWS:], ref[:, :ROWS]) if n == 2 else (ref[:, :ROWS], ref[:, ROWS:])
            upper = upper + dot_tn(near, chosen)
            lower = lower + dot_tn(away, chosen)
    part_ref[:ROWS] = upper.astype(BF)
    part_ref[ROWS:] = lower.astype(BF)
    fvec_ref[...] = fvec[:8] + fvec[8:]
    bias_ref[...] = allowed_bias(scal, kept_ref[:1])


def prepare(by_xor, scal, kept, x0, x2, x1, extra):
    dims = [(KEYS, D), (8, D), (ROWS, KEYS)]
    return call(
        functools.partial(prepare_body, by_xor),
        (1,),
        [SMEM, full((8, KEYS))] + [full((HL, KEYS))] * 3 + [full((4, 16, D))],
        [full(d) for d in dims],
        [shape(dims[0]), shape(dims[1], F32), shape(dims[2], F32)],
        micros=0,
    )(scal, kept, x0, x2, x1, extra)


def attend_body(pieces, scal, part_ref, bias_ref, x3, extra_ref, *refs):
    weights = refs[:pieces]
    xr_ref, kv_ref, q_ref, ctx_ref, lse_ref, wo_ref = refs[pieces:]
    step = pl.program_id(0)
    rows = D // pieces

    @pl.when(step == 0)
    def _():
        chosen = pick(scal, feature_row(scal, pieces > 1), 3)
        xr_ref[:ROWS] = (part_ref[:ROWS].astype(F32) + dot_tn(x3[:, ROWS:], chosen)).astype(BF)
        xr_ref[ROWS:] = (part_ref[ROWS:].astype(F32) + dot_tn(x3[:, :ROWS], chosen)).astype(BF)

    weight = join(weights, rows)
    wo_ref[0] = weight[:, 512:]
    window = extra_ref[pl.ds(step, 1), :, 256:512][0].astype(F32)
    q_bias = window[0:1] + window[1:2]
    v_bias = window[2:3] + window[3:4]
    lane = lax.broadcasted_iota(jnp.int32, (1, 256), 1)
    packed = xr_ref[...]
    kv = dot_nn(packed, weight[:, :384])
    kv_bias = jnp.concatenate([jnp.zeros((1, 128), F32), v_bias], axis=1)
    kv = (kv + kv_bias).astype(BF)
    queries = (dot_nn(packed[:ROWS], weight[:, 384:640]) + q_bias).astype(BF)
    queries = jnp.where(lane < HL, queries, jnp.zeros_like(queries)) * jnp.asarray(0.125, BF)
    kv_ref[0] = kv
    q_ref[0] = queries
    keys, values = kv[:, :256], kv[:, 128:]
    context = jnp.zeros((ROWS, 256), F32)
    totals = jnp.zeros((ROWS, 128), F32)
    for h in range(3):
        own = jnp.where(lanes_of_head(h, 0), queries, jnp.zeros_like(queries))
        scores = dot_nt(own, keys) + bias_ref[...]
        top = jnp.max(scores, axis=1, keepdims=True)
        weight_h = jnp.exp(scores - top)
        total = jnp.sum(weight_h, axis=1, keepdims=True)
        part = dot_nn(weight_h.astype(BF), values) / total
        context = jnp.where(lanes_of_head(h, HD), part, context)
        totals = jnp.where(lane[:, :128] == h, top + jnp.log(total), totals)
    ctx_ref[0] = context.astype(BF)
    lse_ref[0] = jnp.transpose(totals)[:8]


def attend(scal, part, bias, x3, extra, weights):
    pieces = len(weights)
    return call(
        functools.partial(attend_body, pieces),
        (4,),
        [SMEM, full((KEYS, D)), full((ROWS, KEYS)), full((HL, KEYS)), full((4, 16, D))]
        + [pl.BlockSpec((1,) + w.shape[1:], lambda j: (j, 0, 0)) for w in weights],
        [
            full((KEYS, D)),
            pl.BlockSpec((1, KEYS, 384), lambda j: (j, 0, 0)),
            pl.BlockSpec((1, ROWS, 256), lambda j: (j, 0, 0)),
            pl.BlockSpec((1, ROWS, 256), lambda j: (j, 0, 0)),
            pl.BlockSpec((1, 8, ROWS), lambda j: (j, 0, 0)),
            pl.BlockSpec((1, D, 256), lambda j: (j, 0, 0)),
        ],
        [
            shape((KEYS, D)),
            shape((4, KEYS, 384)),
            shape((4, ROWS, 256)),
            shape((4, ROWS, 256)),
            shape((4, 8, ROWS), F32),
            shape((4, D, 256)),
        ],
        micros=23,
        limit=14,
    )(scal, part, bias, x3, extra, *weights)


def over_rows(body, carried=()):
    def step(r, carried):
        return body(pl.ds(pl.multiple_of(r * CHUNK, CHUNK), CHUNK), carried)

    return lax.fori_loop(0, ROWS // CHUNK, step, carried)


def norm(residual, gain, shift):
    mean = jnp.mean(residual, axis=1, keepdims=True)
    spread_row = jnp.mean(residual * residual, axis=1, keepdims=True) - mean * mean
    scale = lax.rsqrt(spread_row + EPS)
    unit = (residual - mean) * scale
    return unit * gain + shift, unit, scale


def norm_back(grad, gain, unit, scale):
    scaled = grad * gain
    mean = jnp.mean(scaled, axis=1, keepdims=True)
    cross = jnp.mean(scaled * unit, axis=1, keepdims=True)
    return scale * (scaled - mean - unit * cross)


def split_out(total, keep_ref, send_ref, first=0):
    low = total.astype(BF).reshape(PARTS, FB, D)
    half = PARTS // 2
    keep_ref[:, 0, first : first + FB] = low[:half]
    send_ref[:, 0, first : first + FB] = low[half:]


ERFC = (-0.82215223, 1.48851587, -1.13520398, 0.27886807, -0.18628806, 0.09678418, 0.37409196, 1.00002368, -1.26551223)


def gelu_parts(pre):
    square = pre * pre * -0.5
    t = 1.0 / (1.0 + jnp.abs(pre) * (0.5 * math.sqrt(0.5)))
    poly = 0.17087277 * t
    for c in ERFC[:-1]:
        poly = (poly + c) * t
    tail = 0.5 * t * jnp.exp(square + (poly + ERFC[-1]))
    half = jnp.where(pre >= 0, 1.0 - tail, tail)
    return pre * half, half + pre * (jnp.exp(square) * (1.0 / math.sqrt(2.0 * math.pi)))


def first_norm_body(ctx_ref, wo_ref, xr_ref, fvec_ref, unit_ref, scale_ref, low_ref):
    total = xr_ref[...].astype(F32) + fvec_ref[0:1]
    for n in range(4):
        total = total + dot_nt(ctx_ref[n], wo_ref[n])
    unit_ref[...] = total

    def rows_of(rows, carried):
        normed, unit, scale = norm(unit_ref[rows, :], fvec_ref[2:3], fvec_ref[3:4])
        unit_ref[rows, :] = unit
        scale_ref[rows, :] = jnp.broadcast_to(scale, (CHUNK, 128))
        low_ref[rows, :] = normed.astype(BF)
        return carried

    over_rows(rows_of)


def first_norm(context, wo, packed, fvec):
    dims = [(ROWS, D), (ROWS, 128), (ROWS, D)]
    return call(
        first_norm_body,
        (1,),
        [full((4, ROWS, 256)), full((4, D, 256)), full((ROWS, D)), full((8, D))],
        [full(d) for d in dims],
        [shape(d, F32) for d in dims[:2]] + [shape(dims[2])],
        micros=3,
    )(context, wo, packed, fvec)


def hidden_body(pieces, scal, unit_ref, first_ref, fvec_ref, extra_ref, fin_ref, cot_ref, *refs):
    inner_w, outer_w, refs = refs[:pieces], refs[pieces : 2 * pieces], refs[2 * pieces :]
    grad_ref, vec_ref, fin_grad_ref, sums_ref, keep_ref, send_ref, pre_ref, bias_ref = refs[:8]
    act_ref, slope_ref, low_ref, total_ref, unit_two_ref, scale_two_ref = refs[8:]
    step = pl.program_id(0)
    at = pl.ds(step & 3, 1)

    @pl.when(step < 4)
    def _():
        window = extra_ref[at, :, 256:512][0].astype(F32)
        bias = jnp.concatenate([window[4 + n : 5 + n] + window[7 + n : 8 + n] for n in range(3)], axis=1)
        act, slope = gelu_parts(dot_nn(first_ref[...], join(inner_w, D // pieces)) + bias)
        act_ref[at] = act.astype(BF)[None]
        slope_ref[at] = slope.astype(BF)[None]

    @pl.when((step >= 4) & (step < 8))
    def _():
        part = dot_nt(act_ref[at][0], join(outer_w, D // pieces))

        @pl.when(step == 4)
        def _():
            total_ref[...] = unit_ref[...] * fvec_ref[2:3] + fvec_ref[3:4] + fvec_ref[1:2] + part

        @pl.when(step > 4)
        def _():
            total_ref[...] += part

    @pl.when(step == 7)
    def _():
        gain = fvec_ref[4:5]

        def rows_of(rows, carried):
            normed, unit, scale = norm(total_ref[rows, :], gain, fvec_ref[5:6])
            unit_two_ref[rows, :] = unit
            scale_two_ref[rows, :] = jnp.broadcast_to(scale, (CHUNK, 128))
            low_ref[rows, :] = normed.astype(BF)
            return carried

        over_rows(rows_of)
        low = low_ref[...]
        frow = feature_row(scal, pieces > 1)
        final = jnp.zeros((OUT, D), F32)
        for n in range(4):
            final = final + dot_nn(fin_ref[n], pick(scal, frow, n))
        columns = lax.broadcasted_iota(jnp.int32, (OUT, OUT), 0)
        place = jnp.where(columns == final_row(scal, pieces > 1), 1.0, 0.0).astype(BF)
        final = dot_nn(place, final.astype(BF)).astype(BF)
        projected = dot_nt(low, final)
        length = lax.rsqrt(jnp.sum(projected * projected, axis=1, keepdims=True) + EPS)
        units = projected * length
        vec_ref[...] = jnp.transpose(units).astype(BF)
        grads = cot_ref[...]
        grads = length * (grads - units * jnp.sum(grads * units, axis=1, keepdims=True))
        grads = grads.astype(BF)
        fin_grad = dot_tn(place, dot_tn(grads, low).astype(BF)).astype(BF)
        for n in range(4):
            fin_grad_ref[n] = dot_nt(fin_grad, pick(scal, frow, n)).astype(BF)
        total_ref[...] = dot_nn(grads, final)

        def rows_back(rows, carried):
            grad, unit = total_ref[rows, :], unit_two_ref[rows, :]
            back = norm_back(grad, gain, unit, scale_two_ref[rows, :1])
            grad_ref[rows, :] = back
            low_ref[rows, :] = back.astype(BF)
            sums = (grad * unit, grad, back)
            return tuple(c + jnp.sum(t, axis=0, keepdims=True) for c, t in zip(carried, sums))

        sums = over_rows(rows_back, (jnp.zeros((1, D), F32),) * 3)
        for n in range(3):
            sums_ref[n : n + 1] = sums[n]
        sums_ref[3:] = jnp.zeros((5, D), F32)

    @pl.when(step >= 8)
    def _():
        low = low_ref[...]
        grad = dot_nn(low, join(outer_w, D // pieces)) * slope_ref[at][0].astype(F32)
        split_out(dot_tn(low, act_ref[at][0]), keep_ref, send_ref)
        grad_low = grad.astype(BF)
        pre_ref[0] = grad_low
        bias_ref[0] = jnp.broadcast_to(jnp.sum(grad, axis=0, keepdims=True), (8, D))
        split_out(dot_tn(first_ref[...], grad_low), keep_ref, send_ref, FB)


def hidden(scal, unit, low, fvec, extra, final, cot, inner_w, outer_w):
    pieces = len(inner_w)
    half = PARTS // 2
    late = lambda j: (jnp.maximum(j - 8, 0), 0, 0)
    wide = pl.BlockSpec((half, 1, 2 * FB, D), lambda j: (0, jnp.maximum(j - 8, 0), 0, 0))
    return call(
        functools.partial(hidden_body, pieces),
        (12,),
        [SMEM, full((ROWS, D)), full((ROWS, D)), full((8, D)), full((4, 16, D))]
        + [full((4, OUT, HL)), full((ROWS, OUT))]
        + [pl.BlockSpec((1, D // pieces, D), lambda j: (jnp.minimum(j, 3), 0, 0)) for _ in inner_w]
        + [pl.BlockSpec((1, D // pieces, D), lambda j: (jnp.where(j < 4, 0, j & 3), 1, 0)) for _ in outer_w],
        [full((ROWS, D)), full((OUT, ROWS)), full((4, OUT, HL)), full((8, D))]
        + [wide, wide, pl.BlockSpec((1, ROWS, D), late), pl.BlockSpec((1, 8, D), late)],
        [
            shape((ROWS, D), F32),
            shape((OUT, ROWS)),
            shape((4, OUT, HL)),
            shape((8, D), F32),
            shape((half, 4, 2 * FB, D)),
            shape((half, 4, 2 * FB, D)),
            shape((4, ROWS, D)),
            shape((4, 8, D), F32),
        ],
        [
            pltpu.VMEM((4, ROWS, D), BF),
            pltpu.VMEM((4, ROWS, D), BF),
            pltpu.VMEM((ROWS, D), BF),
            pltpu.VMEM((ROWS, D), F32),
            pltpu.VMEM((ROWS, D), F32),
            pltpu.VMEM((ROWS, 128), F32),
        ],
        micros=30,
        limit=18,
    )(scal, unit, low, fvec, extra, final, cot, *inner_w, *outer_w)


def inner_back_body(pieces, pre_ref, grad_ref, unit_ref, scale_ref, fvec_ref, sums_ref, *refs):
    weights = refs[:pieces]
    one_ref, one_low_ref, all_ref, total_ref = refs[pieces:]
    step = pl.program_id(0)
    part = dot_nt(pre_ref[0], join(weights, D // pieces))

    @pl.when(step == 0)
    def _():
        total_ref[...] = grad_ref[...] + part

    @pl.when(step > 0)
    def _():
        total_ref[...] += part

    @pl.when(step == 3)
    def _():
        def rows_back(rows, carried):
            grad, unit = total_ref[rows, :], unit_ref[rows, :]
            back = norm_back(grad, fvec_ref[2:3], unit, scale_ref[rows, :1])
            one_ref[rows, :] = back
            one_low_ref[rows, :] = back.astype(BF)
            sums = (grad * unit, grad, back)
            return tuple(c + jnp.sum(t, axis=0, keepdims=True) for c, t in zip(carried, sums))

        all_ref[0:3] = sums_ref[0:3]
        sums = over_rows(rows_back, (jnp.zeros((1, D), F32),) * 3)
        for n in range(3):
            all_ref[3 + n : 4 + n] = sums[n]
        all_ref[6:] = jnp.zeros((2, D), F32)


def inner_back(pre, grad, unit, scale, fvec, sums, weights):
    pieces = len(weights)
    at = lambda j: (j, 0, 0)
    return call(
        functools.partial(inner_back_body, pieces),
        (4,),
        [
            pl.BlockSpec((1, ROWS, D), at),
            full((ROWS, D)),
            full((ROWS, D)),
            full((ROWS, 128)),
            full((8, D)),
            full((8, D)),
        ]
        + [pl.BlockSpec((1, D // pieces, D), at) for w in weights],
        [full((ROWS, D)), full((ROWS, D)), full((8, D))],
        [shape((ROWS, D), F32), shape((ROWS, D)), shape((8, D), F32)],
        [pltpu.VMEM((ROWS, D), F32)],
        micros=9,
        limit=10,
    )(pre, grad, unit, scale, fvec, sums, *weights)


def small_sums(scal, by_xor, n, q_sum, v_sum, all_ref, fin_ref, hid_ref):
    sums = dot_nt(all_ref[...].astype(BF), pick(scal, feature_row(scal, by_xor), n))
    sums = jnp.concatenate([sums, jnp.zeros((8, 64), F32)], axis=1)
    heads = jnp.concatenate([q_sum, v_sum, jnp.zeros((6, 256), F32)], axis=0)
    hidden = hid_ref[0, 0:1]
    hidden = [hidden[:, 256 * k : 256 * (k + 1)] for k in range(3)]
    hidden = jnp.concatenate(hidden + [jnp.zeros((13, 256), F32)], axis=0)
    wide = jnp.concatenate([jnp.concatenate([sums, heads], axis=0), hidden], axis=1).astype(BF)
    final = fin_ref[0].reshape(PARTS, OUT // PARTS, HL)
    final = jnp.concatenate([final, jnp.zeros((PARTS, OUT // PARTS, 64), BF)], axis=2)
    return jnp.concatenate([final, jnp.broadcast_to(wide[None], (PARTS, 16, 512))], axis=2)


def attend_back_body(pieces, first, count, scal, kept_ref, xr_ref, kv_ref, q_ref, ctx_ref, lse_ref, one_ref, low_ref, all_ref, fin_ref, hid_ref, *refs):
    weights = refs[:pieces]
    refs = refs[pieces + (2 if first else 0) :]
    keep_ref, send_ref = refs[:2]
    bias_ref, total_ref = refs[-2:]
    step = pl.program_id(0)

    @pl.when(step == 0)
    def _():
        bias_ref[...] = allowed_bias(scal, kept_ref[:1])
        total_ref[:ROWS] = one_ref[:ROWS]
        total_ref[ROWS:] = one_ref[ROWS:] if first else jnp.zeros((ROWS, D), F32)

    weight = join(weights, D // pieces)
    low = low_ref[...]
    lane = lax.broadcasted_iota(jnp.int32, (1, 256), 1)
    grad_ctx = dot_nn(low, weight[:, 512:])
    grad_ctx = jnp.where(lane >= HD, grad_ctx, 0.0).astype(BF)
    keys, values = kv_ref[0, :, :256], kv_ref[0, :, 128:]
    queries = q_ref[0]
    products = grad_ctx.astype(F32) * ctx_ref[0].astype(F32)
    totals = jnp.transpose(lse_ref[0])
    dq = jnp.zeros((ROWS, 256), F32)
    dk = jnp.zeros((KEYS, 256), F32)
    dv = jnp.zeros((KEYS, 256), F32)
    zero = jnp.zeros_like(queries)
    for h in range(3):
        own = jnp.where(lanes_of_head(h, 0), queries, zero)
        own_grad = jnp.where(lanes_of_head(h, HD), grad_ctx, zero)
        row_dot = jnp.sum(jnp.where(lanes_of_head(h, HD), products, 0.0), axis=1, keepdims=True)
        scores = dot_nt(own, keys) + bias_ref[...]
        prob = jnp.exp(scores - totals[:, h : h + 1])
        dv = dv + dot_tn(prob.astype(BF), own_grad)
        grad_scores = (prob * (dot_nt(own_grad, values) - row_dot)).astype(BF)
        dq = jnp.where(lanes_of_head(h, 0), dot_nn(grad_scores, keys), dq)
        dk = dk + dot_tn(grad_scores, own)
    dq = dq * 0.125
    gap = jnp.zeros((KEYS, 128), F32)
    dkv = jnp.concatenate([dk, gap], axis=1) + jnp.concatenate([gap, dv], axis=1)
    q_sum = jnp.sum(dq, axis=0, keepdims=True)
    v_sum = jnp.sum(dv, axis=0, keepdims=True)
    dkv = dkv.astype(BF)
    dq = dq.astype(BF)
    packed = xr_ref[...]
    low_kv = dot_tn(packed, dkv)
    from_q = dot_tn(packed[:ROWS], dq)
    from_o = dot_tn(low, ctx_ref[0])
    gap = jnp.zeros((D, 128), F32)
    from_qo = jnp.concatenate([from_q, gap], axis=1) + jnp.concatenate([gap, from_o], axis=1)
    split_out(jnp.concatenate([low_kv, from_qo], axis=1), keep_ref, send_ref)
    extra = small_sums(scal, pieces > 1, first + step, q_sum, v_sum, all_ref, fin_ref, hid_ref)
    keep_ref[:, 0, FB:] = extra[: PARTS // 2]
    send_ref[:, 0, FB:] = extra[PARTS // 2 :]
    total_ref[...] += dot_nt(dkv, weight[:, :384])
    total_ref[:ROWS] += dot_nt(dq, weight[:, 384:640])

    @pl.when(step == count - 1)
    def _():
        if first + count < 4:
            refs[2][...] = total_ref[...]
            return
        x0_ref, x2_ref, x1_ref, x3_ref = refs[2:6]
        grads = total_ref[...].astype(BF)
        frow = feature_row(scal, pieces > 1)
        x0_ref[...] = dot_nt(pick(scal, frow, 0), grads)
        x2_ref[...] = dot_nt(pick(scal, frow, 1), grads)
        for n, ref in ((2, x1_ref), (3, x3_ref)):
            part = dot_nt(pick(scal, frow, n), grads).astype(BF)
            ref[:, :ROWS] = part[:, ROWS:]
            ref[:, ROWS:] = part[:, :ROWS]


def attend_back(scal, kept, packed, kv, queries, context, log_total, one, low, small, weights, first, count, held):
    pieces = len(weights)
    half = PARTS // 2
    at = lambda j: (j + first, 0, 0)
    wide = pl.BlockSpec((half, 1, FB + 16, D), lambda j: (0, j + first, 0, 0))
    n_in = 12 + pieces
    last = first + count == 4
    return call(
        functools.partial(attend_back_body, pieces, first, count),
        (count,),
        [
            SMEM,
            full((8, KEYS)),
            full((KEYS, D)),
            pl.BlockSpec((1, KEYS, 384), at),
            pl.BlockSpec((1, ROWS, 256), at),
            pl.BlockSpec((1, ROWS, 256), at),
            pl.BlockSpec((1, 8, ROWS), at),
            full(one.shape),
            full((ROWS, D)),
            full((8, D)),
            pl.BlockSpec((1, OUT, HL), at),
            pl.BlockSpec((1, 8, D), at),
        ]
        + [pl.BlockSpec((1,) + w.shape[1:], at) for w in weights]
        + [pl.BlockSpec(memory_space=pl.ANY)] * len(held),
        [wide, wide] + ([full((HL, KEYS))] * 4 if last else [full((KEYS, D))]),
        [shape((half, 4, FB + 16, D)), shape((half, 4, FB + 16, D))]
        + ([shape((HL, KEYS), F32)] * 2 + [shape((HL, KEYS))] * 2 if last else [shape((KEYS, D), F32)]),
        [pltpu.VMEM((ROWS, KEYS), F32), pltpu.VMEM((KEYS, D), F32)],
        micros=9 * count,
        limit=22,
        aliases={n_in + n: n for n in range(len(held))},
    )(scal, kept, packed, kv, queries, context, log_total, one, low, *small, *weights, *held)


def pack_vec_body(order_ref, mask_ref, vec_ref, out_ref, total_ref):
    step = pl.program_id(0)
    part = dot_nt(vec_ref[0], spread(order_ref[:1]))

    @pl.when(step == 0)
    def _():
        total_ref[...] = part

    @pl.when(step > 0)
    def _():
        total_ref[...] += part

    @pl.when(step == 3)
    def _():
        out_ref[...] = jnp.transpose(total_ref[...] * mask_ref[...].astype(F32))


def pack_vec(order, mask_row, vecs):
    return call(
        pack_vec_body,
        (4,),
        [
            pl.BlockSpec((8, ROWS), lambda b: (0, b)),
            full((1, TOK)),
            pl.BlockSpec((1, OUT, ROWS), lambda b: (b, 0, 0)),
        ],
        full((TOK, OUT)),
        shape((TOK, OUT), F32),
        [pltpu.VMEM((OUT, TOK), F32)],
        micros=5,
    )(order, mask_row, vecs)


def pack_x_body(order_ref, x0_ref, x1_ref, far_ref, out_ref):
    step = pl.program_id(0)
    near = (x0_ref[...] + x1_ref[...].astype(F32)).astype(BF)
    part = dot_nt(jnp.where(step < 2, near, far_ref[...]), spread(order_ref[:1]))

    @pl.when(step == 0)
    def _():
        out_ref[...] = part

    @pl.when(step > 0)
    def _():
        out_ref[...] += part


def pack_x(order, *parts):
    return call(
        pack_x_body,
        (4,),
        [pl.BlockSpec((8, ROWS), lambda b: (0, b))]
        + [pl.BlockSpec((HL, ROWS), lambda b: (0, b & 1)) for _ in parts],
        full((HL, TOK)),
        shape((HL, TOK), F32),
        micros=5,
    )(order, *parts)


def halves(vector):
    high = vector.astype(BF)
    return high, (vector - high.astype(F32)).astype(BF)


def pack_weights_body(k_ref, v_ref, q_ref, o_ref, in_ref, out_ref, fin_ref, qb, vb, inb, ob, outb, g1, s1, g2, s2, heads_ref, ffn_ref):
    turned = lambda ref: jnp.transpose(ref[...].astype(F32)).astype(BF)
    heads_ref[:FB] = jnp.concatenate([k_ref[...], v_ref[...], q_ref[...], turned(o_ref)], axis=1)
    ffn_ref[:FB] = in_ref[...]
    ffn_ref[FB : 2 * FB] = out_ref[...]
    qb, vb, inb, ob, outb, g1, s1, g2, s2 = (ref[...].reshape(1, ref.shape[0]) for ref in (qb, vb, inb, ob, outb, g1, s1, g2, s2))
    gap = jnp.zeros((1, 64), F32)
    window = []
    for value in (jnp.concatenate([qb, gap], axis=1), jnp.concatenate([gap, vb], axis=1)):
        window += list(halves(value))
    hidden = [halves(inb[:, n * 256 : (n + 1) * 256]) for n in range(3)]
    window += [high for high, _ in hidden] + [low for _, low in hidden]
    window = jnp.concatenate(window + [jnp.zeros((6, 256), BF)], axis=0)
    features = [halves(jnp.concatenate([value, gap], axis=1)) for value in (ob, outb, g1, s1, g2, s2)]
    pad = [jnp.zeros((2, 256), BF)]
    features = jnp.concatenate([high for high, _ in features] + pad + [low for _, low in features] + pad, axis=0)
    final = jnp.concatenate([fin_ref[...], jnp.zeros((16, 64), BF)], axis=1)
    extra = jnp.concatenate([final, window, features], axis=1)
    heads_ref[FB:] = extra


def pack_weights(weights, vectors):
    return call(
        pack_weights_body,
        (1,),
        [full(w.shape) for w in weights] + [full(v.shape) for v in vectors],
        [full((FB + 16, D)), full((2 * FB, D))],
        [shape((FB + 16, D)), shape((2 * FB, D))],
        micros=3,
        limit=56,
    )(*weights, *vectors)


def ffn_out_body(a_ref, b_ref, out_ref, in_ref):
    total = a_ref[...] + b_ref[...].astype(F32)
    out_ref[...] = total[:FB]
    in_ref[...] = total[FB:]


def ffn_out(a, b):
    both = [full((FB, D))] * 2
    return call(ffn_out_body, (1,), [full(a.shape), full(b.shape)], both, [shape((FB, D), F32)] * 2, micros=3)(a, b)


def heads_out_body(a_ref, b_ref, q_ref, k_ref, v_ref, o_ref, fin_ref, inb, qb, vb, ob, outb, g1, s1, g2, s2):
    total = a_ref[...] + b_ref[...].astype(F32)
    k_ref[...] = total[:FB, :HL]
    v_ref[...] = total[:FB, HL:384]
    q_ref[...] = total[:FB, 384:576]
    o_ref[...] = jnp.transpose(total[:FB, 576:])
    tile = total[FB:]
    fin_ref[...] = tile[:, :HL]
    qb[...] = tile[8:9, 256 : 256 + HL].reshape(HL)
    vb[...] = tile[9:10, 320:512].reshape(HL)
    for n, ref in ((5, ob), (2, outb), (3, g1), (4, s1), (0, g2), (1, s2)):
        ref[...] = tile[n : n + 1, 256 : 256 + HL].reshape(HL)
    inb[...] = jnp.concatenate([tile[n : n + 1, 512:] for n in range(3)], axis=1).reshape(D)


def heads_out(a, b):
    dims = [(FB, HL)] * 3 + [(HL, FB), (16, HL), (D,)] + [(HL,)] * 8
    return call(
        heads_out_body, (1,), [full(a.shape), full(b.shape)], [full(d) for d in dims], [shape(d, F32) for d in dims], micros=3
    )(a, b)


def hi_lo(vector):
    high = vector.astype(BF)
    high = lax.optimization_barrier(high)
    return high, (vector - high.astype(F32)).astype(BF)


def extra_rows(final_t, q_bias, v_bias, inner_bias, features):
    q_hi, q_lo = hi_lo(jnp.pad(q_bias, (0, 64)))
    v_hi, v_lo = hi_lo(jnp.pad(v_bias, (64, 0)))
    in_hi, in_lo = hi_lo(inner_bias.reshape(3, 256))
    window = jnp.concatenate([jnp.stack([q_hi, q_lo, v_hi, v_lo]), in_hi, in_lo], axis=0)
    window = jnp.pad(window, ((0, 6), (0, 0)))
    f_hi, f_lo = hi_lo(jnp.pad(jnp.stack(features), ((0, 2), (0, 64))))
    final_t = jnp.pad(final_t, ((0, 16 - final_t.shape[0]), (0, 64)))
    return jnp.concatenate([final_t, window, jnp.concatenate([f_hi, f_lo], axis=0)], axis=1)


def local(
    inputs,
    token_order,
    lengths,
    token_mask,
    cotangent,
    query_weight,
    key_weight,
    value_weight,
    output_weight,
    inner_weight,
    outer_weight,
    final_weight,
    query_bias,
    value_bias,
    output_bias,
    inner_bias,
    outer_bias,
    first_gain,
    first_shift,
    second_gain,
    second_shift,
):
    m, i = lax.axis_index("mp"), lax.axis_index("dp")
    n_dp = lax.axis_size("dp")
    rows = D // n_dp
    by_xor = n_dp == 8
    scal = jnp.concatenate([jnp.stack([i, m]).astype(jnp.int32), lengths[0]])
    features_of = [output_bias, outer_bias, first_gain, first_shift, second_gain, second_shift]

    if by_xor:
        heads_own, ffn_own = pack_weights(
            [key_weight, value_weight, query_weight, output_weight, inner_weight, outer_weight.T, final_weight.T],
            [query_bias, value_bias, inner_bias] + features_of,
        )
    else:
        extra = extra_rows(final_weight.T, query_bias, value_bias, inner_bias, features_of)
        heads_own = jnp.concatenate([key_weight, value_weight, query_weight, output_weight.T], axis=1)
        heads_own = jnp.concatenate([heads_own, extra], axis=0)
        ffn_own = jnp.concatenate([inner_weight, outer_weight.T], axis=0)

    mask_row = token_mask.reshape(1, TOK)
    heads_own, ffn_own, inputs = sync(heads_own, ffn_own, inputs)
    heads_got = [swap(heads_own, "mp", bit) for bit in (2, 1, 3)]
    features, kept, cot, order = pack_in(scal, token_order, inputs, mask_row, cotangent)
    near, away = features[:, :KEYS], features[:, KEYS:]
    ffn_own, near, away = sync(ffn_own, near, away)
    ffn_got = [swap(ffn_own, "mp", bit) for bit in (2, 1, 3)]
    heads_got = sync(*heads_got)
    heads = jnp.stack([h[:rows] for h in (heads_own, *heads_got)])
    extras = jnp.stack([h[rows:] for h in (heads_own, *heads_got)])
    if by_xor:
        heads, near, away = sync(heads, near, away)
        head_x, head_y = over_plane(heads)
        head_x, head_y = sync(head_x, head_y)
        far_a, far_b = sync(*over_corner(head_x, head_y))
        far_a, far_b, ffn_got, near, away, heads, head_x, head_y = sync(far_a, far_b, ffn_got, near, away, heads, head_x, head_y)
        x1, x2 = swap(near, "mp", 1), swap(away, "mp", 2)
        ffn = jnp.stack([ffn_own, *ffn_got])
        ffn = jnp.concatenate([ffn, extras], axis=1)
        ffn_x, ffn_y = over_plane(ffn)
        far = jnp.concatenate([far_a, far_b], axis=0)
        head_pieces = [heads, head_x, head_y, far]
        head_pieces += [swap(p, "dp", 1) for p in head_pieces]
        x1, x2 = sync(x1, x2)
        x3 = swap(x2, "mp", 1)
        part, fvec, bias = prepare(by_xor, scal, kept, near, x2, x1, extras)
        x3, ffn_x, ffn_y, part, *head_pieces = sync(x3, ffn_x, ffn_y, part, *head_pieces)
        far_a, far_b = over_corner(ffn_x, ffn_y)
        ffn_pieces = [swap(p, "dp", 1) for p in (ffn, ffn_x, ffn_y)]
    else:
        ffn = jnp.concatenate([jnp.stack([ffn_own, *ffn_got]), extras], axis=1)
        x1, x2 = swap(near, "mp", 1), swap(away, "mp", 2)
        x3 = swap(x2, "mp", 1)
        part, fvec, bias = prepare(by_xor, scal, kept, near, x2, x1, extras)
        head_pieces, ffn_pieces, final = plain_pieces(heads, ffn)

    packed, kv, queries, context, log_total, wo = attend(scal, part, bias, x3, extras, head_pieces)
    if by_xor:
        context, far_a, far_b, *ffn_pieces = sync(context, far_a, far_b, *ffn_pieces)
        far = jnp.concatenate([far_a, far_b], axis=0)
        ffn_pieces = [ffn, ffn_x, ffn_y, far] + ffn_pieces + [swap(far, "dp", 1)]
        unit, scale, normed_low = first_norm(context, wo, packed, fvec)
        unit, last = sync(unit, ffn_pieces[-1])
        ffn_pieces[-1] = last
        final = jnp.concatenate([p[:, 2 * FB :, :HL] for p in ffn_pieces], axis=1)
    if not by_xor:
        unit, scale, normed_low = first_norm(context, wo, packed, fvec)
    grad_two, vec, fin_grad, sums, ffn_keep, ffn_send, pre, hid_sums = hidden(
        scal, unit, normed_low, fvec, extras, final, cot, ffn_pieces, ffn_pieces
    )
    vec_got = swap(vec, "mp", 1)
    saved = (kept, packed, kv, queries, context, log_total)

    def heads_back(one, low, first, count, held):
        small = (all_sums, fin_grad, hid_sums)
        return attend_back(scal, *saved, one, low, small, head_pieces, first, count, held)

    if by_xor:
        ffn_got = swap(ffn_send, "dp", 1)
        grad_one, one_low, all_sums = inner_back(pre, grad_two, unit, scale, fvec, sums, ffn_pieces)
        ffn_got, vec_got, one_low = sync(ffn_got, vec_got, one_low)
        pair = (ffn_keep, ffn_got)
        x_send, y_send = plane_first(*pair)
        one_low, x_send, y_send = sync(one_low, x_send, y_send)
        x_got, y_got = swap(x_send, "dp", 2), swap(y_send, "dp", 4)
        vec_low = jnp.stack([vec, vec_got])
        vec_high = swap(vec_low, "mp", 2)
        head_keep, head_send, dx0, dx2, dx1, dx3 = heads_back(grad_one, one_low, 0, 4, ())
        dx1, dx3, head_send, x_got, y_got, vec_high = sync(dx1, dx3, head_send, x_got, y_got, vec_high)

        dx3_got = swap(dx3, "mp", 1)
        head_got = swap(head_send, "dp", 1)
        to_y, to_x, upper, lower = plane_second(*pair, x_got, y_got)
        from_y, from_x = swap(to_y, "dp", 4), swap(to_x, "dp", 2)
        vecs = jnp.concatenate([vec_low, vec_high], axis=0)
        dx3_got, head_got, dx1, vecs = sync(dx3_got, head_got, dx1, vecs)
        to_far = (dx2 + dx3_got.astype(F32)).astype(BF)
        far, dx1_got = swap(to_far, "mp", 2), swap(dx1, "mp", 1)
        pair = (head_keep, head_got)
        x_send, y_send = plane_first(*pair)
        x_send, y_send, vecs = sync(x_send, y_send, vecs)
        x_got, y_got = swap(x_send, "dp", 2), swap(y_send, "dp", 4)
        vectors = pack_vec(order, mask_row, vecs)
        from_y, from_x, vectors = sync(from_y, from_x, vectors)
        upper = upper + from_y.astype(F32)
        lower = (lower + from_x.astype(F32)).astype(BF)
        lower_got = swap(lower, "mp", 1)
        x_got, y_got, dx1_got, far = sync(x_got, y_got, dx1_got, far)
        to_y, to_x, h_upper, h_lower = plane_second(*pair, x_got, y_got)
        from_y, from_x = swap(to_y, "dp", 4), swap(to_x, "dp", 2)
        inputs_grad = pack_x(order, dx0, dx1_got, far)
        from_y, from_x, lower_got, inputs_grad = sync(from_y, from_x, lower_got, inputs_grad)
        h_upper = h_upper + from_y.astype(F32)
        h_lower = (h_lower + from_x.astype(F32)).astype(BF)
        h_lower_got = swap(h_lower, "mp", 1)
        upper = upper + lower_got.astype(F32)
        last = swap(upper[1].astype(BF), "mp", 2)
        h_lower_got, last = sync(h_lower_got, last)
        h_upper = h_upper + h_lower_got.astype(F32)
        h_last = swap(h_upper[1].astype(BF), "mp", 2)
        g_out, g_in = ffn_out(upper[0], last)
        g_q, g_k, g_v, g_o, g_fin, g_inb, g_qb, g_vb, g_ob, g_outb, g_g1, g_s1, g_g2, g_s2 = heads_out(h_upper[0], h_last)
        g_out, g_fin = g_out.T, g_fin.T
    else:
        grad_one, one_low, all_sums = inner_back(pre, grad_two, unit, scale, fvec, sums, ffn_pieces)
        head_keep, head_send, dx0, dx2, dx1, dx3 = heads_back(grad_one, one_low, 0, 4, ())
        far = swap((dx2 + swap(dx3, "mp", 1).astype(F32)).astype(BF), "mp", 2)
        inputs_grad = pack_x(order, dx0, swap(dx1, "mp", 1), far)
        vec_low = jnp.stack([vec, vec_got])
        vectors = pack_vec(order, mask_row, jnp.concatenate([vec_low, swap(vec_low, "mp", 2)], axis=0))
        ends = []
        for keep, send in ((ffn_keep, ffn_send), (head_keep, head_send)):
            total = scatter_plain(jnp.concatenate([keep, send], axis=0).transpose(1, 0, 2, 3).astype(F32))
            upper = total[:2] + swap(total[2:].astype(BF), "mp", 1).astype(F32)
            ends.append(upper[0] + swap(upper[1].astype(BF), "mp", 2).astype(F32))
        ffn_sum, head_sum = ends
        tile = head_sum[rows:]
        g_out, g_in, g_fin = ffn_sum[:rows].T, ffn_sum[rows:], tile[: OUT // n_dp, :HL].T
        g_g2, g_s2, g_outb, g_g1, g_s1, g_ob = (tile[n, 256 : 256 + HL] for n in range(6))
        g_inb = tile[:3, 512:].reshape(D)
        g_k, g_v, g_q, g_o = head_sum[:rows, :HL], head_sum[:rows, HL:384], head_sum[:rows, 384:576], head_sum[:rows, 576:].T
        g_qb, g_vb = tile[8, 256 : 256 + HL], tile[9, 320:512]
    return (
        vectors,
        inputs_grad,
        g_q,
        g_k,
        g_v,
        g_o,
        g_in,
        g_out,
        g_fin,
        g_qb,
        g_vb,
        g_ob,
        g_inb,
        g_outb,
        g_g1,
        g_s1,
        g_g2,
        g_s2,
    )


def solution(mesh):
    return jax.shard_map(
        local,
        mesh=mesh,
        in_specs=(
            P("mp", "dp"),
            P("dp", None),
            P("dp", None),
            P("dp"),
            P("dp", None),
            P("dp", "mp"),
            P("dp", "mp"),
            P("dp", "mp"),
            P("mp", "dp"),
            P("dp", "mp"),
            P("mp", "dp"),
            P("mp", "dp"),
            P("mp"),
            P("mp"),
            P("mp"),
            P("mp"),
            P("mp"),
            P("mp"),
            P("mp"),
            P("mp"),
            P("mp"),
        ),
        out_specs=(
            P("dp", None),
            P("mp", "dp"),
            P("dp", "mp"),
            P("dp", "mp"),
            P("dp", "mp"),
            P("mp", "dp"),
            P("dp", "mp"),
            P("mp", "dp"),
            P("mp", "dp"),
            P("mp"),
            P("mp"),
            P("mp"),
            P("mp"),
            P("mp"),
            P("mp"),
            P("mp"),
            P("mp"),
            P("mp"),
        ),
        check_vma=False,
    )
```

```python
import functools
import math

import jax
import jax.numpy as jnp
from jax import lax
from jax.experimental import pallas as pl
from jax.experimental.pallas import tpu as pltpu
from jax.sharding import PartitionSpec as P

D = 768
HD = 64
HL = 192
FB = 96
PARTS = 8
OUT = 128
TOK = 2048
ROWS = 512
KEYS = 1024
LONG = 1024
CHUNK = 64
EPS = 1e-06
F32 = jnp.float32
BF = jnp.bfloat16


def dot_nn(a, b):
    return lax.dot_general(a, b, (((1,), (0,)), ((), ())), preferred_element_type=F32)


def dot_nt(a, b):
    return lax.dot_general(a, b, (((1,), (1,)), ((), ())), preferred_element_type=F32)


def dot_tn(a, b):
    return lax.dot_general(a, b, (((0,), (0,)), ((), ())), preferred_element_type=F32)


def swap(array, axis, bit):
    size = lax.axis_size(axis)
    return lax.ppermute(array, axis, [(a, a ^ bit) for a in range(size)])


def full(shape):
    zeros = (0,) * len(shape)
    return pl.BlockSpec(shape, lambda *_: zeros)


SMEM = pl.BlockSpec(memory_space=pltpu.SMEM)


def call(body, grid, in_specs, out_specs, out_shape, scratch=(), micros=10, aliases=None, limit=12):
    return pl.pallas_call(
        body,
        grid=grid,
        in_specs=in_specs,
        out_specs=out_specs,
        out_shape=out_shape,
        scratch_shapes=list(scratch),
        input_output_aliases=aliases or {},
        compiler_params=pltpu.CompilerParams(
            dimension_semantics=("arbitrary",) * len(grid), vmem_limit_bytes=limit * 1024 * 1024
        ),
        cost_estimate=pl.CostEstimate(flops=micros * 4 * 10**9, transcendentals=0, bytes_accessed=micros * 12 * 10**6),
    )


def shape(dims, dtype=BF):
    return jax.ShapeDtypeStruct(dims, dtype)


def sync(*values):
    return lax.optimization_barrier(values)


def over_plane(held):
    return swap(held, "dp", 2), swap(held, "dp", 4)


def over_corner(x_part, y_part):
    return swap(y_part[:2], "dp", 2), swap(x_part[2:], "dp", 4)


def plain_pieces(heads, ffn):
    n_dp = lax.axis_size("dp")
    rows = D // n_dp
    whole = lax.all_gather(ffn, "dp", axis=1)
    parts = [whole[:, :, n * rows : (n + 1) * rows].reshape(4, D, D) for n in (0, 1)]
    final = whole[:, :, 2 * rows : 2 * rows + OUT // n_dp, :HL].reshape(4, OUT, HL)
    return [lax.all_gather(heads, "dp", axis=1, tiled=True)], [jnp.concatenate(parts, axis=1)], final


def scatter_plain(both):
    n_dp = lax.axis_size("dp")
    rows = both.shape[2]
    total = []
    for first in range(0, rows - FB + 1, FB):
        part = both[:, :, first : first + FB].reshape(4, D, D)
        total.append(lax.psum_scatter(part, "dp", scatter_dimension=1, tiled=True))
    if rows % FB == 0:
        return jnp.concatenate(total, axis=1)
    final = both[:, :, rows - 16 :, :256].reshape(4, OUT, 256)
    final = lax.psum_scatter(final, "dp", scatter_dimension=1, tiled=True)
    final = jnp.pad(final, ((0, 0), (0, 16 - OUT // n_dp), (0, 0)))
    sums = lax.psum(both[:, 0, rows - 16 :, 256:], "dp")
    return jnp.concatenate(total + [jnp.concatenate([final, sums], axis=2)], axis=1)


def added(pair, *index):
    return pair[0][index].astype(F32) + pair[1][index].astype(F32)


def by_plane(pair):
    return tuple(p.reshape((2, 2) + p.shape[1:]) for p in pair)


LOW, HIGH = slice(0, 2), slice(2, 4)


def plane_first(*pair):
    wide = by_plane(pair)
    return added(wide, slice(None), 1, LOW).astype(BF), added(wide, 1, slice(None), HIGH).astype(BF)


def plane_second(keep, got, x_got, y_got):
    wide = by_plane((keep, got))
    x_part = [added(wide, n, 0, LOW) + x_got[n].astype(F32) for n in range(2)]
    y_part = [added(wide, 0, n, HIGH) + y_got[n].astype(F32) for n in range(2)]
    return x_part[1].astype(BF), y_part[1].astype(BF), x_part[0], y_part[0]


def feature_row(scal, by_xor):
    lane = lax.broadcasted_iota(jnp.int32, (1, D), 1)
    if not by_xor:
        return lane
    part = jnp.zeros((1, D), jnp.int32)
    for n in range(1, PARTS):
        part = part + jnp.where(lane >= n * FB, 1, 0)
    return (((part & 3) * 2 + (part >> 2)) ^ scal[0]) * FB + lane - part * FB


def final_row(scal, by_xor):
    lane = lax.broadcasted_iota(jnp.int32, (1, OUT), 1)
    if not by_xor:
        return lane
    part = lane >> 4
    return (((part & 3) * 2 + (part >> 2)) ^ scal[0]) * 16 + (lane & 15)


def pick(scal, frow, n):
    first = (scal[1] ^ ((n & 1) * 2 + (n >> 1))) * HL
    rows = lax.broadcasted_iota(jnp.int32, (HL, D), 0) + first
    return jnp.where(rows == frow, 1.0, 0.0).astype(BF)


def spread(order_row):
    rows = lax.broadcasted_iota(jnp.int32, (TOK, order_row.shape[1]), 0)
    return jnp.where(rows == order_row, 1.0, 0.0).astype(BF)


def pack_in_body(scal, order_ref, x_ref, mask_ref, cot_ref, out_ref, kept_ref, cot_out_ref, order_out_ref, canon_ref):
    block = pl.program_id(0)

    @pl.when(block == 0)
    def _():
        start, seen = jnp.int32(0), jnp.int32(0)
        for c in range(4):
            start = jnp.where(scal[2 + c] == LONG, seen, start)
            seen = seen + scal[2 + c]
        order = jnp.broadcast_to(order_ref[...], (8, TOK))
        canon_ref[:, :LONG] = pltpu.roll(order, (TOK - start) & (TOK - 1), 1)[:, :LONG]
        lane = lax.broadcasted_iota(jnp.int32, (8, LONG), 1)
        canon_ref[:, LONG:] = jnp.where(lane < start, order[:, :LONG], order[:, LONG:])
        for n in range(4):
            first = pl.multiple_of((scal[1] ^ n) * ROWS, ROWS)
            order_out_ref[:, n * ROWS : (n + 1) * ROWS] = canon_ref[:, pl.ds(first, ROWS)]

    one_hot = spread(order_out_ref[0:1, pl.ds(pl.multiple_of(block * ROWS, ROWS), ROWS)])
    out_ref[...] = dot_nn(x_ref[...], one_hot).astype(BF)
    mask = mask_ref[...].astype(F32)

    @pl.when(block < 2)
    def _():
        kept_ref[...] = dot_nn(jnp.broadcast_to(mask, (16, TOK)).astype(BF), one_hot)[:8]

    @pl.when(block == 0)
    def _():
        cot = (jnp.transpose(cot_ref[...].astype(F32)) * mask).astype(BF)
        cot_out_ref[...] = jnp.transpose(dot_nn(cot, one_hot))


def pack_in(scal, order, inputs, mask_row, cotangent):
    return call(
        pack_in_body,
        (4,),
        [SMEM, full((1, TOK)), full((HL, TOK)), full((1, TOK)), full((TOK, OUT))],
        [
            pl.BlockSpec((HL, ROWS), lambda b: (0, b)),
            pl.BlockSpec((8, ROWS), lambda b: (0, jnp.minimum(b, 1))),
            full((ROWS, OUT)),
            full((8, TOK)),
        ],
        [shape((HL, TOK)), shape((8, KEYS), F32), shape((ROWS, OUT), F32), shape((8, TOK), jnp.int32)],
        [pltpu.VMEM((8, TOK), jnp.int32)],
        micros=6,
    )(scal, order, inputs, mask_row, cotangent)


def join(refs, rows, first=0, last=D):
    parts = [ref[0, :rows, first:last] for ref in refs]
    return parts[0] if len(parts) == 1 else jnp.concatenate(parts, axis=0)


def lanes_of_head(h, shift):
    lane = lax.broadcasted_iota(jnp.int32, (1, 256), 1)
    return (lane >= shift + h * HD) & (lane < shift + (h + 1) * HD)


def allowed_bias(scal, kept):
    pair = scal[1] & 1
    end, count = jnp.int32(0), jnp.int32(0)
    cuts = [jnp.int32(LONG), jnp.int32(LONG)]
    for c in range(4):
        short = scal[2 + c] != LONG
        end = end + jnp.where(short, scal[2 + c], 0)
        count = count + jnp.where(short, 1, 0)
        cuts = [jnp.where(short & (count == n + 1) & (scal[1] >= 2), end, cuts[n]) for n in range(2)]
    q_pos = lax.broadcasted_iota(jnp.int32, (ROWS, 1), 0) + pair * ROWS
    k_pos = lax.broadcasted_iota(jnp.int32, (1, KEYS), 1) + pair * ROWS
    k_pos = k_pos & (KEYS - 1)
    q_seg = jnp.where(q_pos >= cuts[0], 1, 0) + jnp.where(q_pos >= cuts[1], 1, 0)
    k_seg = jnp.where(k_pos >= cuts[0], 1, 0) + jnp.where(k_pos >= cuts[1], 1, 0)
    k_seg = jnp.where(kept > 0.5, k_seg, k_seg + 8)
    return jnp.where((q_seg == k_seg) | (q_pos == k_pos), 0.0, -1e30)


def prepare_body(by_xor, scal, kept_ref, x0, x2, x1, extra_ref, part_ref, fvec_ref, bias_ref):
    frow = feature_row(scal, by_xor)
    upper = jnp.zeros((ROWS, D), F32)
    lower = jnp.zeros((ROWS, D), F32)
    fvec = jnp.zeros((16, D), F32)
    for n in range(4):
        chosen = pick(scal, frow, n)
        fvec = fvec + dot_nn(extra_ref[n, :, 512 : 512 + HL], chosen)
        if n < 3:
            ref = (x0, x2, x1)[n]
            near, away = (ref[:, ROWS:], ref[:, :ROWS]) if n == 2 else (ref[:, :ROWS], ref[:, ROWS:])
            upper = upper + dot_tn(near, chosen)
            lower = lower + dot_tn(away, chosen)
    part_ref[:ROWS] = upper.astype(BF)
    part_ref[ROWS:] = lower.astype(BF)
    fvec_ref[...] = fvec[:8] + fvec[8:]
    bias_ref[...] = allowed_bias(scal, kept_ref[:1])


def prepare(by_xor, scal, kept, x0, x2, x1, extra):
    dims = [(KEYS, D), (8, D), (ROWS, KEYS)]
    return call(
        functools.partial(prepare_body, by_xor),
        (1,),
        [SMEM, full((8, KEYS))] + [full((HL, KEYS))] * 3 + [full((4, 16, D))],
        [full(d) for d in dims],
        [shape(dims[0]), shape(dims[1], F32), shape(dims[2], F32)],
        micros=0,
    )(scal, kept, x0, x2, x1, extra)


def attend_body(pieces, scal, part_ref, bias_ref, x3, extra_ref, *refs):
    weights = refs[:pieces]
    xr_ref, kv_ref, q_ref, ctx_ref, lse_ref, wo_ref = refs[pieces:]
    step = pl.program_id(0)
    rows = D // pieces

    @pl.when(step == 0)
    def _():
        chosen = pick(scal, feature_row(scal, pieces > 1), 3)
        xr_ref[:ROWS] = (part_ref[:ROWS].astype(F32) + dot_tn(x3[:, ROWS:], chosen)).astype(BF)
        xr_ref[ROWS:] = (part_ref[ROWS:].astype(F32) + dot_tn(x3[:, :ROWS], chosen)).astype(BF)

    weight = join(weights, rows)
    wo_ref[0] = weight[:, 512:]
    window = extra_ref[pl.ds(step, 1), :, 256:512][0].astype(F32)
    q_bias = window[0:1] + window[1:2]
    v_bias = window[2:3] + window[3:4]
    lane = lax.broadcasted_iota(jnp.int32, (1, 256), 1)
    packed = xr_ref[...]
    kv = dot_nn(packed, weight[:, :384])
    kv_bias = jnp.concatenate([jnp.zeros((1, 128), F32), v_bias], axis=1)
    kv = (kv + kv_bias).astype(BF)
    queries = (dot_nn(packed[:ROWS], weight[:, 384:640]) + q_bias).astype(BF)
    queries = jnp.where(lane < HL, queries, jnp.zeros_like(queries)) * jnp.asarray(0.125, BF)
    kv_ref[0] = kv
    q_ref[0] = queries
    keys, values = kv[:, :256], kv[:, 128:]
    context = jnp.zeros((ROWS, 256), F32)
    totals = jnp.zeros((ROWS, 128), F32)
    for h in range(3):
        own = jnp.where(lanes_of_head(h, 0), queries, jnp.zeros_like(queries))
        scores = dot_nt(own, keys) + bias_ref[...]
        top = jnp.max(scores, axis=1, keepdims=True)
        weight_h = jnp.exp(scores - top)
        total = jnp.sum(weight_h, axis=1, keepdims=True)
        part = dot_nn(weight_h.astype(BF), values) / total
        context = jnp.where(lanes_of_head(h, HD), part, context)
        totals = jnp.where(lane[:, :128] == h, top + jnp.log(total), totals)
    ctx_ref[0] = context.astype(BF)
    lse_ref[0] = jnp.transpose(totals)[:8]


def attend(scal, part, bias, x3, extra, weights):
    pieces = len(weights)
    return call(
        functools.partial(attend_body, pieces),
        (4,),
        [SMEM, full((KEYS, D)), full((ROWS, KEYS)), full((HL, KEYS)), full((4, 16, D))]
        + [pl.BlockSpec((1,) + w.shape[1:], lambda j: (j, 0, 0)) for w in weights],
        [
            full((KEYS, D)),
            pl.BlockSpec((1, KEYS, 384), lambda j: (j, 0, 0)),
            pl.BlockSpec((1, ROWS, 256), lambda j: (j, 0, 0)),
            pl.BlockSpec((1, ROWS, 256), lambda j: (j, 0, 0)),
            pl.BlockSpec((1, 8, ROWS), lambda j: (j, 0, 0)),
            pl.BlockSpec((1, D, 256), lambda j: (j, 0, 0)),
        ],
        [
            shape((KEYS, D)),
            shape((4, KEYS, 384)),
            shape((4, ROWS, 256)),
            shape((4, ROWS, 256)),
            shape((4, 8, ROWS), F32),
            shape((4, D, 256)),
        ],
        micros=23,
        limit=14,
    )(scal, part, bias, x3, extra, *weights)


def over_rows(body, carried=(), chunk=CHUNK):
    def step(r, carried):
        return body(pl.ds(pl.multiple_of(r * chunk, chunk), chunk), carried)

    return lax.fori_loop(0, ROWS // chunk, step, carried)


def norm(residual, gain, shift):
    mean = jnp.mean(residual, axis=1, keepdims=True)
    spread_row = jnp.mean(residual * residual, axis=1, keepdims=True) - mean * mean
    scale = lax.rsqrt(spread_row + EPS)
    unit = (residual - mean) * scale
    return unit * gain + shift, unit, scale


def norm_back(grad, gain, unit, scale):
    scaled = grad * gain
    mean = jnp.mean(scaled, axis=1, keepdims=True)
    cross = jnp.mean(scaled * unit, axis=1, keepdims=True)
    return scale * (scaled - mean - unit * cross)


def split_out(total, keep_ref, send_ref, first=0):
    low = total.astype(BF).reshape(PARTS, FB, D)
    half = PARTS // 2
    keep_ref[:, 0, first : first + FB] = low[:half]
    send_ref[:, 0, first : first + FB] = low[half:]


ERFC = (-0.82215223, 1.48851587, -1.13520398, 0.27886807, -0.18628806, 0.09678418, 0.37409196, 1.00002368, -1.26551223)


def gelu_parts(pre):
    square = pre * pre * -0.5
    t = 1.0 / (1.0 + jnp.abs(pre) * (0.5 * math.sqrt(0.5)))
    poly = 0.17087277 * t
    for c in ERFC[:-1]:
        poly = (poly + c) * t
    tail = 0.5 * t * jnp.exp(square + (poly + ERFC[-1]))
    half = jnp.where(pre >= 0, 1.0 - tail, tail)
    return pre * half, half + pre * (jnp.exp(square) * (1.0 / math.sqrt(2.0 * math.pi)))


def first_norm_body(ctx_ref, wo_ref, xr_ref, fvec_ref, unit_ref, scale_ref, low_ref):
    total = xr_ref[...].astype(F32) + fvec_ref[0:1]
    for n in range(4):
        total = total + dot_nt(ctx_ref[n], wo_ref[n])
    unit_ref[...] = total

    def rows_of(rows, carried):
        normed, unit, scale = norm(unit_ref[rows, :], fvec_ref[2:3], fvec_ref[3:4])
        unit_ref[rows, :] = unit
        scale_ref[rows, :] = jnp.broadcast_to(scale, (128, 128))
        low_ref[rows, :] = normed.astype(BF)
        return carried

    over_rows(rows_of, (), 128)


def first_norm(context, wo, packed, fvec):
    dims = [(ROWS, D), (ROWS, 128), (ROWS, D)]
    return call(
        first_norm_body,
        (1,),
        [full((4, ROWS, 256)), full((4, D, 256)), full((ROWS, D)), full((8, D))],
        [full(d) for d in dims],
        [shape(d, F32) for d in dims[:2]] + [shape(dims[2])],
        micros=3,
    )(context, wo, packed, fvec)


def hidden_body(pieces, scal, unit_ref, first_ref, fvec_ref, extra_ref, fin_ref, cot_ref, *refs):
    inner_w, outer_w, refs = refs[:pieces], refs[pieces : 2 * pieces], refs[2 * pieces :]
    grad_ref, vec_ref, fin_grad_ref, sums_ref, keep_ref, send_ref, pre_ref, bias_ref = refs[:8]
    act_ref, slope_ref, low_ref, total_ref, unit_two_ref, scale_two_ref = refs[8:]
    step = pl.program_id(0)
    at = pl.ds(step & 3, 1)

    @pl.when(step < 4)
    def _():
        window = extra_ref[at, :, 256:512][0].astype(F32)
        bias = jnp.concatenate([window[4 + n : 5 + n] + window[7 + n : 8 + n] for n in range(3)], axis=1)
        act, slope = gelu_parts(dot_nn(first_ref[...], join(inner_w, D // pieces)) + bias)
        act_ref[at] = act.astype(BF)[None]
        slope_ref[at] = slope.astype(BF)[None]

    @pl.when((step >= 4) & (step < 8))
    def _():
        part = dot_nt(act_ref[at][0], join(outer_w, D // pieces))

        @pl.when(step == 4)
        def _():
            total_ref[...] = unit_ref[...] * fvec_ref[2:3] + fvec_ref[3:4] + fvec_ref[1:2] + part

        @pl.when(step > 4)
        def _():
            total_ref[...] += part

    @pl.when(step == 7)
    def _():
        gain = fvec_ref[4:5]

        def rows_of(rows, carried):
            normed, unit, scale = norm(total_ref[rows, :], gain, fvec_ref[5:6])
            unit_two_ref[rows, :] = unit
            scale_two_ref[rows, :] = jnp.broadcast_to(scale, (CHUNK, 128))
            low_ref[rows, :] = normed.astype(BF)
            return carried

        over_rows(rows_of)
        low = low_ref[...]
        frow = feature_row(scal, pieces > 1)
        final = jnp.zeros((OUT, D), F32)
        for n in range(4):
            final = final + dot_nn(fin_ref[n], pick(scal, frow, n))
        columns = lax.broadcasted_iota(jnp.int32, (OUT, OUT), 0)
        place = jnp.where(columns == final_row(scal, pieces > 1), 1.0, 0.0).astype(BF)
        final = dot_nn(place, final.astype(BF)).astype(BF)
        projected = dot_nt(low, final)
        length = lax.rsqrt(jnp.sum(projected * projected, axis=1, keepdims=True) + EPS)
        units = projected * length
        vec_ref[...] = jnp.transpose(units).astype(BF)
        grads = cot_ref[...]
        grads = length * (grads - units * jnp.sum(grads * units, axis=1, keepdims=True))
        grads = grads.astype(BF)
        fin_grad = dot_tn(place, dot_tn(grads, low).astype(BF)).astype(BF)
        for n in range(4):
            fin_grad_ref[n] = dot_nt(fin_grad, pick(scal, frow, n)).astype(BF)
        total_ref[...] = dot_nn(grads, final)

        def rows_back(rows, carried):
            grad, unit = total_ref[rows, :], unit_two_ref[rows, :]
            back = norm_back(grad, gain, unit, scale_two_ref[rows, :1])
            grad_ref[rows, :] = back
            low_ref[rows, :] = back.astype(BF)
            sums = (grad * unit, grad, back)
            return tuple(c + jnp.sum(t, axis=0, keepdims=True) for c, t in zip(carried, sums))

        sums = over_rows(rows_back, (jnp.zeros((1, D), F32),) * 3)
        for n in range(3):
            sums_ref[n : n + 1] = sums[n]
        sums_ref[3:] = jnp.zeros((5, D), F32)

    @pl.when(step >= 8)
    def _():
        low = low_ref[...]
        grad = dot_nn(low, join(outer_w, D // pieces)) * slope_ref[at][0].astype(F32)
        split_out(dot_tn(low, act_ref[at][0]), keep_ref, send_ref)
        grad_low = grad.astype(BF)
        pre_ref[0] = grad_low
        bias_ref[0] = jnp.broadcast_to(jnp.sum(grad, axis=0, keepdims=True), (8, D))
        split_out(dot_tn(first_ref[...], grad_low), keep_ref, send_ref, FB)


def hidden(scal, unit, low, fvec, extra, final, cot, inner_w, outer_w):
    pieces = len(inner_w)
    half = PARTS // 2
    late = lambda j: (jnp.maximum(j - 8, 0), 0, 0)
    wide = pl.BlockSpec((half, 1, 2 * FB, D), lambda j: (0, jnp.maximum(j - 8, 0), 0, 0))
    return call(
        functools.partial(hidden_body, pieces),
        (12,),
        [SMEM, full((ROWS, D)), full((ROWS, D)), full((8, D)), full((4, 16, D))]
        + [full((4, OUT, HL)), full((ROWS, OUT))]
        + [pl.BlockSpec((1, D // pieces, D), lambda j: (jnp.minimum(j, 3), 0, 0)) for _ in inner_w]
        + [pl.BlockSpec((1, D // pieces, D), lambda j: (jnp.where(j < 4, 0, j & 3), 1, 0)) for _ in outer_w],
        [full((ROWS, D)), full((OUT, ROWS)), full((4, OUT, HL)), full((8, D))]
        + [wide, wide, pl.BlockSpec((1, ROWS, D), late), pl.BlockSpec((1, 8, D), late)],
        [
            shape((ROWS, D), F32),
            shape((OUT, ROWS)),
            shape((4, OUT, HL)),
            shape((8, D), F32),
            shape((half, 4, 2 * FB, D)),
            shape((half, 4, 2 * FB, D)),
            shape((4, ROWS, D)),
            shape((4, 8, D), F32),
        ],
        [
            pltpu.VMEM((4, ROWS, D), BF),
            pltpu.VMEM((4, ROWS, D), BF),
            pltpu.VMEM((ROWS, D), BF),
            pltpu.VMEM((ROWS, D), F32),
            pltpu.VMEM((ROWS, D), F32),
            pltpu.VMEM((ROWS, 128), F32),
        ],
        micros=30,
        limit=18,
    )(scal, unit, low, fvec, extra, final, cot, *inner_w, *outer_w)


def inner_back_body(pieces, pre_ref, grad_ref, unit_ref, scale_ref, fvec_ref, sums_ref, *refs):
    weights = refs[:pieces]
    one_ref, one_low_ref, all_ref, total_ref = refs[pieces:]
    step = pl.program_id(0)
    part = dot_nt(pre_ref[0], join(weights, D // pieces))

    @pl.when(step == 0)
    def _():
        total_ref[...] = grad_ref[...] + part

    @pl.when(step > 0)
    def _():
        total_ref[...] += part

    @pl.when(step == 3)
    def _():
        def rows_back(rows, carried):
            grad, unit = total_ref[rows, :], unit_ref[rows, :]
            back = norm_back(grad, fvec_ref[2:3], unit, scale_ref[rows, :1])
            one_ref[rows, :] = back
            one_low_ref[rows, :] = back.astype(BF)
            sums = (grad * unit, grad, back)
            return tuple(c + jnp.sum(t, axis=0, keepdims=True) for c, t in zip(carried, sums))

        all_ref[0:3] = sums_ref[0:3]
        sums = over_rows(rows_back, (jnp.zeros((1, D), F32),) * 3, 128)
        for n in range(3):
            all_ref[3 + n : 4 + n] = sums[n]
        all_ref[6:] = jnp.zeros((2, D), F32)


def inner_back(pre, grad, unit, scale, fvec, sums, weights):
    pieces = len(weights)
    at = lambda j: (j, 0, 0)
    return call(
        functools.partial(inner_back_body, pieces),
        (4,),
        [
            pl.BlockSpec((1, ROWS, D), at),
            full((ROWS, D)),
            full((ROWS, D)),
            full((ROWS, 128)),
            full((8, D)),
            full((8, D)),
        ]
        + [pl.BlockSpec((1, D // pieces, D), at) for w in weights],
        [full((ROWS, D)), full((ROWS, D)), full((8, D))],
        [shape((ROWS, D), F32), shape((ROWS, D)), shape((8, D), F32)],
        [pltpu.VMEM((ROWS, D), F32)],
        micros=9,
        limit=10,
    )(pre, grad, unit, scale, fvec, sums, *weights)


def small_sums(scal, by_xor, n, q_sum, v_sum, all_ref, fin_ref, hid_ref):
    sums = dot_nt(all_ref[...].astype(BF), pick(scal, feature_row(scal, by_xor), n))
    sums = jnp.concatenate([sums, jnp.zeros((8, 64), F32)], axis=1)
    heads = jnp.concatenate([q_sum, v_sum, jnp.zeros((6, 256), F32)], axis=0)
    hidden = hid_ref[0, 0:1]
    hidden = [hidden[:, 256 * k : 256 * (k + 1)] for k in range(3)]
    hidden = jnp.concatenate(hidden + [jnp.zeros((13, 256), F32)], axis=0)
    wide = jnp.concatenate([jnp.concatenate([sums, heads], axis=0), hidden], axis=1).astype(BF)
    final = fin_ref[0].reshape(PARTS, OUT // PARTS, HL)
    final = jnp.concatenate([final, jnp.zeros((PARTS, OUT // PARTS, 64), BF)], axis=2)
    return jnp.concatenate([final, jnp.broadcast_to(wide[None], (PARTS, 16, 512))], axis=2)


def attend_back_body(pieces, first, count, scal, kept_ref, xr_ref, kv_ref, q_ref, ctx_ref, lse_ref, one_ref, low_ref, all_ref, fin_ref, hid_ref, *refs):
    weights = refs[:pieces]
    refs = refs[pieces + (2 if first else 0) :]
    keep_ref, send_ref = refs[:2]
    bias_ref, total_ref = refs[-2:]
    step = pl.program_id(0)

    @pl.when(step == 0)
    def _():
        bias_ref[...] = allowed_bias(scal, kept_ref[:1])
        total_ref[:ROWS] = one_ref[:ROWS]
        total_ref[ROWS:] = one_ref[ROWS:] if first else jnp.zeros((ROWS, D), F32)

    weight = join(weights, D // pieces)
    low = low_ref[...]
    lane = lax.broadcasted_iota(jnp.int32, (1, 256), 1)
    grad_ctx = dot_nn(low, weight[:, 512:])
    grad_ctx = jnp.where(lane >= HD, grad_ctx, 0.0).astype(BF)
    keys, values = kv_ref[0, :, :256], kv_ref[0, :, 128:]
    queries = q_ref[0]
    products = grad_ctx.astype(F32) * ctx_ref[0].astype(F32)
    totals = jnp.transpose(lse_ref[0])
    dq = jnp.zeros((ROWS, 256), F32)
    dk = jnp.zeros((KEYS, 256), F32)
    dv = jnp.zeros((KEYS, 256), F32)
    zero = jnp.zeros_like(queries)
    for h in range(3):
        own = jnp.where(lanes_of_head(h, 0), queries, zero)
        own_grad = jnp.where(lanes_of_head(h, HD), grad_ctx, zero)
        row_dot = jnp.sum(jnp.where(lanes_of_head(h, HD), products, 0.0), axis=1, keepdims=True)
        scores = dot_nt(own, keys) + bias_ref[...]
        prob = jnp.exp(scores - totals[:, h : h + 1])
        dv = dv + dot_tn(prob.astype(BF), own_grad)
        grad_scores = (prob * (dot_nt(own_grad, values) - row_dot)).astype(BF)
        dq = jnp.where(lanes_of_head(h, 0), dot_nn(grad_scores, keys), dq)
        dk = dk + dot_tn(grad_scores, own)
    dq = dq * 0.125
    gap = jnp.zeros((KEYS, 128), F32)
    dkv = jnp.concatenate([dk, gap], axis=1) + jnp.concatenate([gap, dv], axis=1)
    q_sum = jnp.sum(dq, axis=0, keepdims=True)
    v_sum = jnp.sum(dv, axis=0, keepdims=True)
    dkv = dkv.astype(BF)
    dq = dq.astype(BF)
    packed = xr_ref[...]
    low_kv = dot_tn(packed, dkv)
    from_q = dot_tn(packed[:ROWS], dq)
    from_o = dot_tn(low, ctx_ref[0])
    gap = jnp.zeros((D, 128), F32)
    from_qo = jnp.concatenate([from_q, gap], axis=1) + jnp.concatenate([gap, from_o], axis=1)
    split_out(jnp.concatenate([low_kv, from_qo], axis=1), keep_ref, send_ref)
    extra = small_sums(scal, pieces > 1, first + step, q_sum, v_sum, all_ref, fin_ref, hid_ref)
    keep_ref[:, 0, FB:] = extra[: PARTS // 2]
    send_ref[:, 0, FB:] = extra[PARTS // 2 :]
    total_ref[...] += dot_nt(dkv, weight[:, :384])
    total_ref[:ROWS] += dot_nt(dq, weight[:, 384:640])

    @pl.when(step == count - 1)
    def _():
        if first + count < 4:
            refs[2][...] = total_ref[...]
            return
        x0_ref, x2_ref, x1_ref, x3_ref = refs[2:6]
        grads = total_ref[...].astype(BF)
        frow = feature_row(scal, pieces > 1)
        x0_ref[...] = dot_nt(pick(scal, frow, 0), grads)
        x2_ref[...] = dot_nt(pick(scal, frow, 1), grads)
        for n, ref in ((2, x1_ref), (3, x3_ref)):
            part = dot_nt(pick(scal, frow, n), grads).astype(BF)
            ref[:, :ROWS] = part[:, ROWS:]
            ref[:, ROWS:] = part[:, :ROWS]


def attend_back(scal, kept, packed, kv, queries, context, log_total, one, low, small, weights, first, count, held):
    pieces = len(weights)
    half = PARTS // 2
    at = lambda j: (j + first, 0, 0)
    wide = pl.BlockSpec((half, 1, FB + 16, D), lambda j: (0, j + first, 0, 0))
    n_in = 12 + pieces
    last = first + count == 4
    return call(
        functools.partial(attend_back_body, pieces, first, count),
        (count,),
        [
            SMEM,
            full((8, KEYS)),
            full((KEYS, D)),
            pl.BlockSpec((1, KEYS, 384), at),
            pl.BlockSpec((1, ROWS, 256), at),
            pl.BlockSpec((1, ROWS, 256), at),
            pl.BlockSpec((1, 8, ROWS), at),
            full(one.shape),
            full((ROWS, D)),
            full((8, D)),
            pl.BlockSpec((1, OUT, HL), at),
            pl.BlockSpec((1, 8, D), at),
        ]
        + [pl.BlockSpec((1,) + w.shape[1:], at) for w in weights]
        + [pl.BlockSpec(memory_space=pl.ANY)] * len(held),
        [wide, wide] + ([full((HL, KEYS))] * 4 if last else [full((KEYS, D))]),
        [shape((half, 4, FB + 16, D)), shape((half, 4, FB + 16, D))]
        + ([shape((HL, KEYS), F32)] * 2 + [shape((HL, KEYS))] * 2 if last else [shape((KEYS, D), F32)]),
        [pltpu.VMEM((ROWS, KEYS), F32), pltpu.VMEM((KEYS, D), F32)],
        micros=9 * count,
        limit=22,
        aliases={n_in + n: n for n in range(len(held))},
    )(scal, kept, packed, kv, queries, context, log_total, one, low, *small, *weights, *held)


def pack_vec_body(order_ref, mask_ref, vec_ref, out_ref, total_ref):
    step = pl.program_id(0)
    part = dot_nt(vec_ref[0], spread(order_ref[:1]))

    @pl.when(step == 0)
    def _():
        total_ref[...] = part

    @pl.when(step > 0)
    def _():
        total_ref[...] += part

    @pl.when(step == 3)
    def _():
        out_ref[...] = jnp.transpose(total_ref[...] * mask_ref[...].astype(F32))


def pack_vec(order, mask_row, vecs):
    return call(
        pack_vec_body,
        (4,),
        [
            pl.BlockSpec((8, ROWS), lambda b: (0, b)),
            full((1, TOK)),
            pl.BlockSpec((1, OUT, ROWS), lambda b: (b, 0, 0)),
        ],
        full((TOK, OUT)),
        shape((TOK, OUT), F32),
        [pltpu.VMEM((OUT, TOK), F32)],
        micros=5,
    )(order, mask_row, vecs)


def pack_x_body(order_ref, x0_ref, x1_ref, far_ref, out_ref):
    step = pl.program_id(0)
    near = (x0_ref[...] + x1_ref[...].astype(F32)).astype(BF)
    part = dot_nt(jnp.where(step < 2, near, far_ref[...]), spread(order_ref[:1]))

    @pl.when(step == 0)
    def _():
        out_ref[...] = part

    @pl.when(step > 0)
    def _():
        out_ref[...] += part


def pack_x(order, *parts):
    return call(
        pack_x_body,
        (4,),
        [pl.BlockSpec((8, ROWS), lambda b: (0, b))]
        + [pl.BlockSpec((HL, ROWS), lambda b: (0, b & 1)) for _ in parts],
        full((HL, TOK)),
        shape((HL, TOK), F32),
        micros=5,
    )(order, *parts)


def halves(vector):
    high = vector.astype(BF)
    return high, (vector - high.astype(F32)).astype(BF)


def pack_weights_body(k_ref, v_ref, q_ref, o_ref, in_ref, out_ref, fin_ref, qb, vb, inb, ob, outb, g1, s1, g2, s2, heads_ref, ffn_ref):
    turned = lambda ref: jnp.transpose(ref[...].astype(F32)).astype(BF)
    heads_ref[:FB] = jnp.concatenate([k_ref[...], v_ref[...], q_ref[...], turned(o_ref)], axis=1)
    ffn_ref[:FB] = in_ref[...]
    ffn_ref[FB : 2 * FB] = out_ref[...]
    qb, vb, inb, ob, outb, g1, s1, g2, s2 = (ref[...].reshape(1, ref.shape[0]) for ref in (qb, vb, inb, ob, outb, g1, s1, g2, s2))
    gap = jnp.zeros((1, 64), F32)
    window = []
    for value in (jnp.concatenate([qb, gap], axis=1), jnp.concatenate([gap, vb], axis=1)):
        window += list(halves(value))
    hidden = [halves(inb[:, n * 256 : (n + 1) * 256]) for n in range(3)]
    window += [high for high, _ in hidden] + [low for _, low in hidden]
    window = jnp.concatenate(window + [jnp.zeros((6, 256), BF)], axis=0)
    features = [halves(jnp.concatenate([value, gap], axis=1)) for value in (ob, outb, g1, s1, g2, s2)]
    pad = [jnp.zeros((2, 256), BF)]
    features = jnp.concatenate([high for high, _ in features] + pad + [low for _, low in features] + pad, axis=0)
    final = jnp.concatenate([fin_ref[...], jnp.zeros((16, 64), BF)], axis=1)
    extra = jnp.concatenate([final, window, features], axis=1)
    heads_ref[FB:] = extra


def pack_weights(weights, vectors):
    return call(
        pack_weights_body,
        (1,),
        [full(w.shape) for w in weights] + [full(v.shape) for v in vectors],
        [full((FB + 16, D)), full((2 * FB, D))],
        [shape((FB + 16, D)), shape((2 * FB, D))],
        micros=3,
        limit=56,
    )(*weights, *vectors)


def ffn_out_body(a_ref, b_ref, out_ref, in_ref):
    total = a_ref[...] + b_ref[...].astype(F32)
    out_ref[...] = total[:FB]
    in_ref[...] = total[FB:]


def ffn_out(a, b):
    both = [full((FB, D))] * 2
    return call(ffn_out_body, (1,), [full(a.shape), full(b.shape)], both, [shape((FB, D), F32)] * 2, micros=3)(a, b)


def heads_out_body(a_ref, b_ref, q_ref, k_ref, v_ref, o_ref, fin_ref, inb, qb, vb, ob, outb, g1, s1, g2, s2):
    total = a_ref[...] + b_ref[...].astype(F32)
    k_ref[...] = total[:FB, :HL]
    v_ref[...] = total[:FB, HL:384]
    q_ref[...] = total[:FB, 384:576]
    o_ref[...] = jnp.transpose(total[:FB, 576:])
    tile = total[FB:]
    fin_ref[...] = tile[:, :HL]
    qb[...] = tile[8:9, 256 : 256 + HL].reshape(HL)
    vb[...] = tile[9:10, 320:512].reshape(HL)
    for n, ref in ((5, ob), (2, outb), (3, g1), (4, s1), (0, g2), (1, s2)):
        ref[...] = tile[n : n + 1, 256 : 256 + HL].reshape(HL)
    inb[...] = jnp.concatenate([tile[n : n + 1, 512:] for n in range(3)], axis=1).reshape(D)


def heads_out(a, b):
    dims = [(FB, HL)] * 3 + [(HL, FB), (16, HL), (D,)] + [(HL,)] * 8
    return call(
        heads_out_body, (1,), [full(a.shape), full(b.shape)], [full(d) for d in dims], [shape(d, F32) for d in dims], micros=3
    )(a, b)


def hi_lo(vector):
    high = vector.astype(BF)
    high = lax.optimization_barrier(high)
    return high, (vector - high.astype(F32)).astype(BF)


def extra_rows(final_t, q_bias, v_bias, inner_bias, features):
    q_hi, q_lo = hi_lo(jnp.pad(q_bias, (0, 64)))
    v_hi, v_lo = hi_lo(jnp.pad(v_bias, (64, 0)))
    in_hi, in_lo = hi_lo(inner_bias.reshape(3, 256))
    window = jnp.concatenate([jnp.stack([q_hi, q_lo, v_hi, v_lo]), in_hi, in_lo], axis=0)
    window = jnp.pad(window, ((0, 6), (0, 0)))
    f_hi, f_lo = hi_lo(jnp.pad(jnp.stack(features), ((0, 2), (0, 64))))
    final_t = jnp.pad(final_t, ((0, 16 - final_t.shape[0]), (0, 64)))
    return jnp.concatenate([final_t, window, jnp.concatenate([f_hi, f_lo], axis=0)], axis=1)


def local(
    inputs,
    token_order,
    lengths,
    token_mask,
    cotangent,
    query_weight,
    key_weight,
    value_weight,
    output_weight,
    inner_weight,
    outer_weight,
    final_weight,
    query_bias,
    value_bias,
    output_bias,
    inner_bias,
    outer_bias,
    first_gain,
    first_shift,
    second_gain,
    second_shift,
):
    m, i = lax.axis_index("mp"), lax.axis_index("dp")
    n_dp = lax.axis_size("dp")
    rows = D // n_dp
    by_xor = n_dp == 8
    scal = jnp.concatenate([jnp.stack([i, m]).astype(jnp.int32), lengths[0]])
    features_of = [output_bias, outer_bias, first_gain, first_shift, second_gain, second_shift]

    if by_xor:
        heads_own, ffn_own = pack_weights(
            [key_weight, value_weight, query_weight, output_weight, inner_weight, outer_weight.T, final_weight.T],
            [query_bias, value_bias, inner_bias] + features_of,
        )
    else:
        extra = extra_rows(final_weight.T, query_bias, value_bias, inner_bias, features_of)
        heads_own = jnp.concatenate([key_weight, value_weight, query_weight, output_weight.T], axis=1)
        heads_own = jnp.concatenate([heads_own, extra], axis=0)
        ffn_own = jnp.concatenate([inner_weight, outer_weight.T], axis=0)

    mask_row = token_mask.reshape(1, TOK)
    heads_own, ffn_own, inputs = sync(heads_own, ffn_own, inputs)
    heads_got = [swap(heads_own, "mp", bit) for bit in (2, 1, 3)]
    features, kept, cot, order = pack_in(scal, token_order, inputs, mask_row, cotangent)
    near, away = features[:, :KEYS], features[:, KEYS:]
    ffn_own, near, away = sync(ffn_own, near, away)
    ffn_got = [swap(ffn_own, "mp", bit) for bit in (2, 1, 3)]
    heads_got = sync(*heads_got)
    heads = jnp.stack([h[:rows] for h in (heads_own, *heads_got)])
    extras = jnp.stack([h[rows:] for h in (heads_own, *heads_got)])
    if by_xor:
        heads, near, away = sync(heads, near, away)
        head_x, head_y = over_plane(heads)
        head_x, head_y = sync(head_x, head_y)
        far_a, far_b, near, away = sync(*over_corner(head_x, head_y), near, away)
        far_a, far_b, ffn_got, heads, head_x, head_y = sync(far_a, far_b, ffn_got, heads, head_x, head_y)
        x1, x2 = swap(near, "mp", 1), swap(away, "mp", 2)
        ffn = jnp.stack([ffn_own, *ffn_got])
        ffn = jnp.concatenate([ffn, extras], axis=1)
        ffn_x, ffn_y = over_plane(ffn)
        far = jnp.concatenate([far_a, far_b], axis=0)
        head_pieces = [heads, head_x, head_y, far]
        head_pieces += [swap(p, "dp", 1) for p in head_pieces]
        x1, x2 = sync(x1, x2)
        x3 = swap(x2, "mp", 1)
        part, fvec, bias = prepare(by_xor, scal, kept, near, x2, x1, extras)
        x3, ffn_x, ffn_y, part, *head_pieces = sync(x3, ffn_x, ffn_y, part, *head_pieces)
        far_a, far_b = over_corner(ffn_x, ffn_y)
        ffn_pieces = [swap(p, "dp", 1) for p in (ffn, ffn_x, ffn_y)]
    else:
        ffn = jnp.concatenate([jnp.stack([ffn_own, *ffn_got]), extras], axis=1)
        x1, x2 = swap(near, "mp", 1), swap(away, "mp", 2)
        x3 = swap(x2, "mp", 1)
        part, fvec, bias = prepare(by_xor, scal, kept, near, x2, x1, extras)
        head_pieces, ffn_pieces, final = plain_pieces(heads, ffn)

    packed, kv, queries, context, log_total, wo = attend(scal, part, bias, x3, extras, head_pieces)
    if by_xor:
        context, far_a, far_b, *ffn_pieces = sync(context, far_a, far_b, *ffn_pieces)
        far = jnp.concatenate([far_a, far_b], axis=0)
        ffn_pieces = [ffn, ffn_x, ffn_y, far] + ffn_pieces + [swap(far, "dp", 1)]
        unit, scale, normed_low = first_norm(context, wo, packed, fvec)
        unit, last = sync(unit, ffn_pieces[-1])
        ffn_pieces[-1] = last
        final = jnp.concatenate([p[:, 2 * FB :, :HL] for p in ffn_pieces], axis=1)
    if not by_xor:
        unit, scale, normed_low = first_norm(context, wo, packed, fvec)
    grad_two, vec, fin_grad, sums, ffn_keep, ffn_send, pre, hid_sums = hidden(
        scal, unit, normed_low, fvec, extras, final, cot, ffn_pieces, ffn_pieces
    )
    vec_got = swap(vec, "mp", 1)
    saved = (kept, packed, kv, queries, context, log_total)

    def heads_back(one, low, first, count, held):
        small = (all_sums, fin_grad, hid_sums)
        return attend_back(scal, *saved, one, low, small, head_pieces, first, count, held)

    if by_xor:
        ffn_got = swap(ffn_send, "dp", 1)
        grad_one, one_low, all_sums = inner_back(pre, grad_two, unit, scale, fvec, sums, ffn_pieces)
        ffn_got, vec_got, one_low = sync(ffn_got, vec_got, one_low)
        pair = (ffn_keep, ffn_got)
        x_send, y_send = plane_first(*pair)
        one_low, x_send, y_send = sync(one_low, x_send, y_send)
        x_got, y_got = swap(x_send, "dp", 2), swap(y_send, "dp", 4)
        vec_low = jnp.stack([vec, vec_got])
        vec_high = swap(vec_low, "mp", 2)
        head_keep, head_send, dx0, dx2, dx1, dx3 = heads_back(grad_one, one_low, 0, 4, ())
        dx1, dx3, head_send, x_got, y_got, vec_high = sync(dx1, dx3, head_send, x_got, y_got, vec_high)

        dx3_got = swap(dx3, "mp", 1)
        head_got = swap(head_send, "dp", 1)
        to_y, to_x, upper, lower = plane_second(*pair, x_got, y_got)
        from_y, from_x = swap(to_y, "dp", 4), swap(to_x, "dp", 2)
        vecs = jnp.concatenate([vec_low, vec_high], axis=0)
        dx3_got, head_got, dx1, vecs = sync(dx3_got, head_got, dx1, vecs)
        to_far = (dx2 + dx3_got.astype(F32)).astype(BF)
        far, dx1_got = swap(to_far, "mp", 2), swap(dx1, "mp", 1)
        pair = (head_keep, head_got)
        x_send, y_send = plane_first(*pair)
        x_send, y_send, vecs = sync(x_send, y_send, vecs)
        x_got, y_got = swap(x_send, "dp", 2), swap(y_send, "dp", 4)
        vectors = pack_vec(order, mask_row, vecs)
        from_y, from_x, vectors = sync(from_y, from_x, vectors)
        upper = upper + from_y.astype(F32)
        lower = (lower + from_x.astype(F32)).astype(BF)
        lower_got = swap(lower, "mp", 1)
        x_got, y_got, dx1_got, far = sync(x_got, y_got, dx1_got, far)
        to_y, to_x, h_upper, h_lower = plane_second(*pair, x_got, y_got)
        from_y, from_x = swap(to_y, "dp", 4), swap(to_x, "dp", 2)
        inputs_grad = pack_x(order, dx0, dx1_got, far)
        from_y, from_x, lower_got, inputs_grad = sync(from_y, from_x, lower_got, inputs_grad)
        h_upper = h_upper + from_y.astype(F32)
        h_lower = (h_lower + from_x.astype(F32)).astype(BF)
        h_lower_got = swap(h_lower, "mp", 1)
        upper = upper + lower_got.astype(F32)
        last = swap(upper[1].astype(BF), "mp", 2)
        h_lower_got, last = sync(h_lower_got, last)
        h_upper = h_upper + h_lower_got.astype(F32)
        h_last = swap(h_upper[1].astype(BF), "mp", 2)
        g_out, g_in = ffn_out(upper[0], last)
        g_q, g_k, g_v, g_o, g_fin, g_inb, g_qb, g_vb, g_ob, g_outb, g_g1, g_s1, g_g2, g_s2 = heads_out(h_upper[0], h_last)
        g_out, g_fin = g_out.T, g_fin.T
    else:
        grad_one, one_low, all_sums = inner_back(pre, grad_two, unit, scale, fvec, sums, ffn_pieces)
        head_keep, head_send, dx0, dx2, dx1, dx3 = heads_back(grad_one, one_low, 0, 4, ())
        far = swap((dx2 + swap(dx3, "mp", 1).astype(F32)).astype(BF), "mp", 2)
        inputs_grad = pack_x(order, dx0, swap(dx1, "mp", 1), far)
        vec_low = jnp.stack([vec, vec_got])
        vectors = pack_vec(order, mask_row, jnp.concatenate([vec_low, swap(vec_low, "mp", 2)], axis=0))
        ends = []
        for keep, send in ((ffn_keep, ffn_send), (head_keep, head_send)):
            total = scatter_plain(jnp.concatenate([keep, send], axis=0).transpose(1, 0, 2, 3).astype(F32))
            upper = total[:2] + swap(total[2:].astype(BF), "mp", 1).astype(F32)
            ends.append(upper[0] + swap(upper[1].astype(BF), "mp", 2).astype(F32))
        ffn_sum, head_sum = ends
        tile = head_sum[rows:]
        g_out, g_in, g_fin = ffn_sum[:rows].T, ffn_sum[rows:], tile[: OUT // n_dp, :HL].T
        g_g2, g_s2, g_outb, g_g1, g_s1, g_ob = (tile[n, 256 : 256 + HL] for n in range(6))
        g_inb = tile[:3, 512:].reshape(D)
        g_k, g_v, g_q, g_o = head_sum[:rows, :HL], head_sum[:rows, HL:384], head_sum[:rows, 384:576], head_sum[:rows, 576:].T
        g_qb, g_vb = tile[8, 256 : 256 + HL], tile[9, 320:512]
    return (
        vectors,
        inputs_grad,
        g_q,
        g_k,
        g_v,
        g_o,
        g_in,
        g_out,
        g_fin,
        g_qb,
        g_vb,
        g_ob,
        g_inb,
        g_outb,
        g_g1,
        g_s1,
        g_g2,
        g_s2,
    )


def solution(mesh):
    return jax.shard_map(
        local,
        mesh=mesh,
        in_specs=(
            P("mp", "dp"),
            P("dp", None),
            P("dp", None),
            P("dp"),
            P("dp", None),
            P("dp", "mp"),
            P("dp", "mp"),
            P("dp", "mp"),
            P("mp", "dp"),
            P("dp", "mp"),
            P("mp", "dp"),
            P("mp", "dp"),
            P("mp"),
            P("mp"),
            P("mp"),
            P("mp"),
            P("mp"),
            P("mp"),
            P("mp"),
            P("mp"),
            P("mp"),
        ),
        out_specs=(
            P("dp", None),
            P("mp", "dp"),
            P("dp", "mp"),
            P("dp", "mp"),
            P("dp", "mp"),
            P("mp", "dp"),
            P("dp", "mp"),
            P("mp", "dp"),
            P("mp", "dp"),
            P("mp"),
            P("mp"),
            P("mp"),
            P("mp"),
            P("mp"),
            P("mp"),
            P("mp"),
            P("mp"),
            P("mp"),
        ),
        check_vma=False,
    )
```
